128 devices in a mesh: dp: 8 (over y_lo, x), mp: 16 (over y_hi, z, core).
Axes of the slice: x: 4, y: 4 (y_hi: 2, y_lo: 2; y = y_hi * 2 + y_lo), z: 4, core: 2. Of those that a mesh axis runs over, the one named last changes fastest.
Arguments:
- tokens: bfloat16 [16384, 2304], P(('dp', 'mp')), may hold values from -6 to 6
- ada_ffn: float32 [16, 2, 2304], P('dp'), may hold values from -4 to 4
- ffn_gate: float32 [16, 2304], P('dp'), may hold values from 0.5 to 1.5
- up_weight: bfloat16 [2304, 9216], P(None, 'mp'), may hold values from -0.125 to 0.125
- up_bias: float32 [9216], P('mp'), may hold values from -6 to 6
- down_weight: bfloat16 [9216, 2304], P('mp'), may hold values from -0.125 to 0.125
- down_bias: float32 [2304], replicated, may hold values from -6 to 6
- ada_head: float32 [16, 2, 2304], P('dp'), may hold values from -4 to 4
- head_weight: bfloat16 [2304, 4096], P(None, 'mp'), may hold values from -0.125 to 0.125
- head_bias: float32 [4096], P('mp'), may hold values from -6 to 6
- gumbel_noise: float32 [8, 1024, 4096], P('dp', None, 'mp'), as said below
- codebook: bfloat16 [4096, 32], P('mp'), may hold values from -16 to 16
- phi_weight: float32 [32, 32, 3, 3], replicated, may hold values from -0.375 to 0.375
- phi_bias: float32 [32], replicated, may hold values from -6 to 6
- f_hat: float32 [8, 32, 1024], P('dp', None, 'mp'), may hold values from -6 to 6
Outputs:
- block_out: bfloat16 [16384, 2304], P(('dp', 'mp'))
- f_hat_out: float32 [8, 32, 1024], P('dp', None, 'mp')
The draws below stay inside these ranges and needn't reach their ends.
Inputs may be any that keep to these rules, and one draw needn't show every extreme that they name: `gumbel_noise`: noise added to the guided logits.
All inputs are finite; a program needn't handle non-finite values.
Results may differ from the reference program's by a relative error of at most 0.024.
Values may be sent and summed in bfloat16 or wider, within the bound.
A program may use at most 256 MiB of HBM per device.

```python
import jax
import jax.numpy as jnp
from jax import lax

D = 2304
FF = 9216
VOCAB = 4096
CVAE = 32
SIDE = 32
NEW = 1024
IMGS = 16
TOKENS = 16384
HALF = 1
PAIRS = 8
CONDS = 4
VB = 256
N_MP = 16


def draw_gumbel_noise(key, part):
    key_list = jax.random.split(key, 1)
    full_shape = (PAIRS, NEW, VOCAB)
    uniform_draw = jax.random.uniform(key_list[0], full_shape, jnp.float32, 1e-06, 1.0 - 1e-06)
    return -jnp.log(-jnp.log(uniform_draw))


def steps_of(key, shape, shards, least, largest):
    factor_of, own = 1.0, jax.random.fold_in(key, 6)
    for dim, shards_of in shards:
        draws = jnp.exp(jax.random.uniform(jax.random.fold_in(own, dim), (shards_of,), jnp.float32, least / len(shards), largest / len(shards)))
        factor_of = factor_of * jnp.repeat(draws, shape[dim] // shards_of).reshape([-1 if axis == dim else 1 for axis in range(len(shape))])
    return factor_of


def noise(own_key, shape, scale, limit, pieces=(), kind=jnp.bfloat16):
    loudness = steps_of(own_key, shape, pieces, -0.22, 0.18) if pieces else 1.0
    entries = jax.random.normal(own_key, shape, jnp.float32) * scale * loudness
    return jnp.minimum(jnp.maximum(entries, -limit), limit).astype(kind)


def setup_inputs(seed: int = 0) -> dict:
    splits = jax.random.split(jax.random.key(seed), 16)
    tokens = noise(splits[0], (TOKENS, D), 1.0, 6.0, ((0, 128),))
    ada_ffn = noise(splits[1], (IMGS, 2, D), 0.3, 4.0, ((0, 8),), jnp.float32)
    ffn_gate = jnp.clip(0.5 + 1.0 * jax.random.uniform(splits[2], (IMGS, D), jnp.float32) ** steps_of(splits[2], (IMGS, D), ((0, 8),), -0.2, 0.2), 0.5, 1.5)
    up_weight = noise(splits[3], (D, FF), D ** -0.5, 0.125, ((1, 16),))
    up_bias = noise(splits[4], (FF,), 0.5, 6.0, ((0, 16),), jnp.float32)
    down_weight = noise(splits[5], (FF, D), (FF // 4) ** -0.5, 0.125, ((0, 16),))
    down_bias = noise(splits[6], (D,), 0.5, 6.0, (), jnp.float32)
    ada_head = noise(splits[7], (IMGS, 2, D), 0.3, 4.0, ((0, 8),), jnp.float32)
    head_weight = noise(splits[8], (D, VOCAB), D ** -0.5, 0.125, ((1, 16),))
    head_bias = noise(splits[9], (VOCAB,), 1.0, 6.0, ((0, 16),), jnp.float32)
    gumbel_noise = draw_gumbel_noise(jax.random.fold_in(splits[15], 71), 0)
    codebook = noise(splits[11], (VOCAB, CVAE), 3.0, 16.0, ((0, 16),))
    phi_weight = noise(splits[12], (CVAE, CVAE, 3, 3), (9 * CVAE) ** -0.5, 0.375, (), jnp.float32)
    phi_bias = noise(splits[13], (CVAE,), 0.5, 6.0, (), jnp.float32)
    f_hat = noise(splits[14], (PAIRS, CVAE, NEW), 1.0, 6.0, ((0, 8), (2, 16)), jnp.float32)
    return dict(tokens=tokens, ada_ffn=ada_ffn, ffn_gate=ffn_gate, up_weight=up_weight, up_bias=up_bias, down_weight=down_weight, down_bias=down_bias, ada_head=ada_head, head_weight=head_weight, head_bias=head_bias, gumbel_noise=gumbel_noise, codebook=codebook, phi_weight=phi_weight, phi_bias=phi_bias, f_hat=f_hat)


GUIDE = 1.5

def norm_rows(values):
    row_mean = lax.optimization_barrier(jnp.mean(values, axis=-1, keepdims=True))
    centred = values - row_mean
    spread = lax.optimization_barrier(jnp.mean(centred * centred, axis=-1, keepdims=True))
    return centred * lax.rsqrt(spread + 1e-06)

def modulate(values, ada_one):
    return norm_rows(values) * (1.0 + ada_one[1]) + ada_one[0]

def reference(tokens, ada_ffn, ffn_gate, up_weight, up_bias, down_weight, down_bias, ada_head, head_weight, head_bias, gumbel_noise, codebook, phi_weight, phi_bias, f_hat):

    def one_image(inputs):
        image_rows, ffn_ada, gate_row, head_ada = inputs
        normed = modulate(image_rows.astype(jnp.float32), ffn_ada).astype(jnp.bfloat16)
        hidden = jax.nn.gelu(jnp.dot(normed, up_weight, preferred_element_type=jnp.float32) + up_bias, approximate=True).astype(jnp.bfloat16)
        ffn_sum = jnp.dot(hidden, down_weight, preferred_element_type=jnp.float32)
        image_out = (image_rows.astype(jnp.float32) + gate_row * (ffn_sum + down_bias)).astype(jnp.bfloat16)
        head_in = modulate(image_out.astype(jnp.float32), head_ada).astype(jnp.bfloat16)
        logits = jnp.dot(head_in, head_weight, preferred_element_type=jnp.float32) + head_bias
        return (image_out, logits)
    stream_out, logits = lax.map(one_image, (tokens.reshape(IMGS, NEW, D), ada_ffn, ffn_gate, ada_head))
    logits = logits.reshape(2, CONDS, 2, HALF, NEW, VOCAB)
    guided = (1.0 + GUIDE) * logits[0] - GUIDE * logits[1]
    guided = jnp.transpose(guided, (1, 0, 2, 3, 4)).reshape(PAIRS, NEW, VOCAB)
    scores = guided + gumbel_noise
    code_blocks = codebook.reshape(N_MP, VB, CVAE).astype(jnp.float32)

    def sample(score_rows):
        blocks = score_rows.reshape(NEW, N_MP, VB)
        peak_part = lax.optimization_barrier(jnp.max(blocks, axis=2))
        weights = jnp.exp(blocks - peak_part[:, :, None]).astype(jnp.bfloat16)
        total_part = lax.optimization_barrier(jnp.sum(weights.astype(jnp.float32), axis=2))
        code_part = jnp.einsum('tbv,bvc->tbc', weights.astype(jnp.float32), code_blocks, precision=lax.Precision.HIGHEST)
        peak = lax.optimization_barrier(jnp.max(peak_part, axis=1))
        factor = jnp.exp(peak_part - peak[:, None])
        return lax.optimization_barrier(jnp.sum(code_part * factor[:, :, None], axis=1)) / lax.optimization_barrier(jnp.sum(total_part * factor, axis=1))[:, None]
    soft_code = lax.map(sample, scores)
    code_maps = soft_code.reshape(PAIRS, SIDE, SIDE, CVAE)
    padded = jnp.pad(code_maps, ((0, 0), (1, 1), (1, 1), (0, 0)))
    conv_out = jnp.zeros((PAIRS, CVAE, SIDE, SIDE), jnp.float32) + phi_bias[None, :, None, None]
    for row_step in range(3):
        for col_step in range(3):
            conv_out = conv_out + jnp.einsum('pyxc,oc->poyx', padded[:, row_step:row_step + SIDE, col_step:col_step + SIDE, :], phi_weight[:, :, row_step, col_step], precision=lax.Precision.HIGHEST)
    own_cells = jnp.transpose(code_maps, (0, 3, 1, 2))
    f_hat_out = f_hat + (0.5 * own_cells + 0.5 * conv_out).reshape(PAIRS, CVAE, NEW)
    return (stream_out.reshape(TOKENS, D), f_hat_out)
```

```python
import functools

import jax
import jax.numpy as jnp
from jax import lax
from jax.experimental import pallas as pl
from jax.experimental.pallas import tpu as pltpu
from jax.sharding import PartitionSpec as P

MESH = pl.DeviceIdType.MESH
BF = jnp.bfloat16
F32 = jnp.float32

D = 2304
ROWS = 128
HID = 576
UNITS = 3
UK = D // UNITS
UQ = UK // 4
CW = D // UNITS
DQ = HID // 4
SIDE = 32
VB = 256
MSG = 40
GUIDE = 1.5


def position():
    dp, mp = lax.axis_index("dp"), lax.axis_index("mp")
    return dp // 4, dp % 4, mp // 8, (mp // 2) % 4, mp % 2


def device(ylo, x, yhi, z, core):
    return (ylo * 4 + x, yhi * 8 + z * 2 + core)


def remote(src, dst, send, recv, target):
    return pltpu.make_async_remote_copy(
        src_ref=src, dst_ref=dst, send_sem=send, recv_sem=recv, device_id=target, device_id_type=MESH
    )


def norm_rows(values):
    centred = values - jnp.mean(values, axis=-1, keepdims=True)
    spread = jnp.mean(centred * centred, axis=-1, keepdims=True)
    return centred * lax.rsqrt(spread + 1e-06)


def gelu(v):
    return 0.5 * v * (1.0 + jnp.tanh(0.7978845608028654 * (v + 0.044715 * v * v * v)))


def greet(targets):
    barrier = pltpu.get_barrier_semaphore()
    for target in targets:
        pl.semaphore_signal(barrier, inc=1, device_id=target, device_id_type=MESH)
    return lambda: pl.semaphore_wait(barrier, len(targets))


def ffn_kernel(
    tok, ada, gate, up_w, up_b, down_w, down_b, out,
    xn, up, dn, ub, hid, part, opp, nxt, got1, got2,
    loc_s, y_s, y_r, a_s, a_r, b_s, b_r, c_s, c_r, o_s, o_r, z_s, z_r, bias_s, bias_r, p_s, p_r, q_s, q_r,
):
    ylo, x, yhi, z, core = position()
    sib = device(ylo, x, yhi, z, 1 - core)
    partner = device(1 - ylo, x, 1 - yhi, z, core)
    partner_sib = device(1 - ylo, x, 1 - yhi, z, 1 - core)
    xr, xl = device(ylo, (x + 1) % 4, yhi, z, core), device(ylo, (x + 3) % 4, yhi, z, core)
    zr_i, zl_i, zo_i = (z + 1) % 4, (z + 3) % 4, (z + 2) % 4
    zr, zl = device(ylo, x, yhi, zr_i, core), device(ylo, x, yhi, zl_i, core)
    arrived = greet([sib, partner, partner_sib, xr, xl, zr, zl])

    local = [pltpu.make_async_copy(up_w, up.at[0], loc_s.at[0])]
    for j in range(UNITS):
        local.append(pltpu.make_async_copy(down_w.at[:, pl.ds(j * CW, CW)], dn.at[j, 0], loc_s.at[1 + j]))
    local[0].start()

    @pl.loop(0, ROWS // 16)
    def _(i):
        rows = pl.ds(pl.multiple_of(i * 16, 16), 16)
        pair = ada[yhi]
        v = norm_rows(tok[rows, :].astype(F32)) * (1.0 + pair[1:2, :]) + pair[0:1, :]
        xn[z, rows, :] = v.astype(BF)

    arrived()

    def y_copy(k):
        if k < UNITS:
            rows = pl.ds(pl.multiple_of(k * UK + x * UQ, 16), UQ)
            return remote(up_w.at[rows, :], up.at[2, rows, :], y_s.at[k], y_r.at[k], partner)
        j = k - UNITS
        rows = pl.ds(pl.multiple_of(x * DQ, 16), DQ)
        return remote(
            down_w.at[rows, pl.ds(j * CW, CW)], dn.at[j, 2, rows, :], y_s.at[k], y_r.at[k], partner
        )

    def piece(k, q, half=None):
        if k < UNITS:
            if half is None:
                return up.at[2, pl.ds(pl.multiple_of(k * UK + q * UQ, 16), UQ), :]
            return up.at[2, pl.ds(pl.multiple_of(k * UK + q * UQ + half * (UQ // 2), 16), UQ // 2), :]
        rows = pl.ds(pl.multiple_of(q * DQ, 16), DQ)
        if half is None:
            return dn.at[k - UNITS, 2, rows, :]
        return dn.at[k - UNITS, 2, rows, pl.ds(half * (CW // 2), CW // 2)]

    x_l, x_r = (x + 3) % 4, (x + 1) % 4

    def a_copies(k):
        ref = piece(k, x)
        return [
            remote(ref, ref, a_s.at[k, 0], a_r.at[k, 0], xr),
            remote(ref, ref, a_s.at[k, 1], a_r.at[k, 1], xl),
        ]

    def b_copies(k):
        from_left, from_right = piece(k, x_l, 0), piece(k, x_r, 1)
        return [
            remote(from_left, from_left, b_s.at[k, 0], b_r.at[k, 0], xr),
            remote(from_right, from_right, b_s.at[k, 1], b_r.at[k, 1], xl),
        ]

    def c_copy(k):
        if k < UNITS:
            rows = pl.ds(k * UK, UK)
            return remote(up.at[2, rows, :], up.at[3, rows, :], c_s.at[k], c_r.at[k], sib)
        return remote(dn.at[k - UNITS, 2], dn.at[k - UNITS, 3], c_s.at[k], c_r.at[k], sib)

    y = [y_copy(k) for k in range(2 * UNITS)]
    a = [a_copies(k) for k in range(2 * UNITS)]
    b = [b_copies(k) for k in range(2 * UNITS)]
    c = [c_copy(k) for k in range(2 * UNITS)]
    y[0].start()
    z1 = [
        remote(xn.at[z], xn.at[z], z_s.at[0], z_r.at[0], zr),
        remote(xn.at[z], xn.at[z], z_s.at[1], z_r.at[1], zl),
    ]
    z2 = [
        remote(xn.at[zl_i, pl.ds(0, 64)], xn.at[zl_i, pl.ds(0, 64)], z_s.at[2], z_r.at[2], zr),
        remote(xn.at[zr_i, pl.ds(64, 64)], xn.at[zr_i, pl.ds(64, 64)], z_s.at[3], z_r.at[3], zl),
    ]
    for cp in z1:
        cp.start()
    y[1].start()
    own_up = remote(up_w, up.at[1], o_s.at[0], o_r.at[0], sib)
    own_up.start()
    own_dn = [
        remote(down_w.at[:, pl.ds(j * CW, CW)], dn.at[j, 1], o_s.at[1 + j], o_r.at[1 + j], sib)
        for j in range(UNITS)
    ]
    pltpu.make_async_copy(up_b, ub.at[0], loc_s.at[4]).start()
    biases = [
        remote(up_b, ub.at[1], bias_s.at[0], bias_r.at[0], sib),
        remote(up_b, ub.at[2], bias_s.at[1], bias_r.at[1], partner),
        remote(up_b, ub.at[3], bias_s.at[2], bias_r.at[2], partner_sib),
    ]
    for cp in biases:
        cp.start()

    def hidden(first):
        @pl.loop(0, 4)
        def _(i):
            p, m = first + i // 2, i % 2
            lhs = xn[pl.ds(2 * m, 2)].reshape(256, D)
            acc = jnp.dot(lhs, up[p], preferred_element_type=F32)
            hid[p, pl.ds(pl.multiple_of(m * 256, 256), 256), :] = gelu(acc + ub[p]).astype(BF)

    def partial(j):
        @pl.loop(0, 2)
        def _(m):
            rows = pl.ds(pl.multiple_of(m * 256, 256), 256)
            acc = jnp.dot(hid[0, rows, :], dn[j, 0], preferred_element_type=F32)
            for p in range(1, 4):
                acc = acc + jnp.dot(hid[p, rows, :], dn[j, p], preferred_element_type=F32)
            part[j, pl.ds(2 * m, 2)] = acc.reshape(2, ROWS, CW)

        opp[j] = part[j, zo_i].astype(BF)
        for cp in p1(j):
            cp.start()

    def p1(j):
        return [
            remote(opp.at[j, pl.ds(0, 64)], got1.at[j, 0], p_s.at[j, 0], p_r.at[j, 0], zr),
            remote(opp.at[j, pl.ds(64, 64)], got1.at[j, 1], p_s.at[j, 1], p_r.at[j, 1], zl),
        ]

    def p2(j):
        return [
            remote(nxt.at[j, 0], got2.at[j, 0], q_s.at[j, 0], q_r.at[j, 0], zr),
            remote(nxt.at[j, 1], got2.at[j, 1], q_s.at[j, 1], q_r.at[j, 1], zl),
        ]

    def second(j):
        for cp in p1(j):
            cp.wait_recv()
        nxt[j, 0, 0:64] = (part[j, zr_i, 0:64] + got1[j, 0].astype(F32)).astype(BF)
        nxt[j, 0, 64:128] = part[j, zr_i, 64:128].astype(BF)
        nxt[j, 1, 0:64] = part[j, zl_i, 0:64].astype(BF)
        nxt[j, 1, 64:128] = (part[j, zl_i, 64:128] + got1[j, 1].astype(F32)).astype(BF)
        for cp in p2(j):
            cp.start()

    def finish(j):
        for cp in p2(j):
            cp.wait_recv()
        cols = pl.ds(j * CW, CW)
        total = part[j, z] + got2[j, 0].astype(F32) + got2[j, 1].astype(F32)
        total = total + down_b[:, cols]
        out[:, cols] = (tok[:, cols].astype(F32) + gate[pl.ds(yhi, 1), cols] * total).astype(BF)

    last = 2 * UNITS - 1

    def tick(k):
        if k <= last:
            y[k].wait_recv()
            for cp in a[k]:
                cp.start()
            if k + 2 <= last:
                y[k + 2].start()
        if 0 <= k - 1 <= last:
            for cp in a[k - 1]:
                cp.wait_recv()
            for cp in b[k - 1]:
                cp.start()
        if 0 <= k - 2 <= last:
            for cp in b[k - 2]:
                cp.wait_recv()
            c[k - 2].start()

    tick(0)
    tick(1)
    for cp in local[1:]:
        cp.start()
    for cp in own_dn:
        cp.start()
    for cp in z1:
        cp.wait_recv()
    for cp in z2:
        cp.start()
    tick(2)
    for cp in z2:
        cp.wait_recv()
    local[0].wait()
    own_up.wait_recv()
    pltpu.make_async_copy(up_b, ub.at[0], loc_s.at[4]).wait()
    for cp in biases:
        cp.wait_recv()
    hidden(0)
    tick(3)
    tick(4)
    for k in range(UNITS):
        c[k].wait_recv()
    hidden(2)
    tick(5)
    for cp in local[1:]:
        cp.wait()
    for cp in own_dn:
        cp.wait_recv()
    c[3].wait_recv()
    partial(0)
    tick(6)
    c[4].wait_recv()
    partial(1)
    second(0)
    tick(7)
    c[5].wait_recv()
    partial(2)
    second(1)
    second(2)
    for j in range(UNITS):
        finish(j)

    for cp in y + c + z1 + z2 + [own_up] + own_dn + biases:
        cp.wait_send()
    for group in a + b + [p1(j) for j in range(UNITS)] + [p2(j) for j in range(UNITS)]:
        for cp in group:
            cp.wait_send()


def ffn_block(tokens, ada, gate, up_w, up_b, down_w, down_b):
    dma = pltpu.SemaphoreType.DMA
    units = 2 * UNITS
    vmem, anywhere = pl.BlockSpec(memory_space=pltpu.VMEM), pl.BlockSpec(memory_space=pl.ANY)
    return pl.pallas_call(
        ffn_kernel,
        out_shape=jax.ShapeDtypeStruct((ROWS, D), BF),
        in_specs=[vmem, vmem, vmem, anywhere, vmem, anywhere, vmem],
        out_specs=vmem,
        scratch_shapes=[
            pltpu.VMEM((4, ROWS, D), BF),
            pltpu.VMEM((4, D, HID), BF),
            pltpu.VMEM((UNITS, 4, HID, CW), BF),
            pltpu.VMEM((4, 1, HID), F32),
            pltpu.VMEM((4, 512, HID), BF),
            pltpu.VMEM((UNITS, 4, ROWS, CW), F32),
            pltpu.VMEM((UNITS, ROWS, CW), BF),
            pltpu.VMEM((UNITS, 2, ROWS, CW), BF),
            pltpu.VMEM((UNITS, 2, ROWS // 2, CW), BF),
            pltpu.VMEM((UNITS, 2, ROWS, CW), BF),
            dma((5,)),
            dma((units,)), dma((units,)),
            dma((units, 2)), dma((units, 2)),
            dma((units, 2)), dma((units, 2)),
            dma((units,)), dma((units,)),
            dma((1 + UNITS,)), dma((1 + UNITS,)),
            dma((4,)), dma((4,)),
            dma((3,)), dma((3,)),
            dma((UNITS, 2)), dma((UNITS, 2)),
            dma((UNITS, 2)), dma((UNITS, 2)),
        ],
        name="ffn_block",
        compiler_params=pltpu.CompilerParams(
            collective_id=1, has_side_effects=True, vmem_limit_bytes=60 * 1024 * 1024
        ),
    )(tokens, ada, gate, up_w, up_b.reshape(1, -1), down_w, down_b.reshape(1, -1))


def head_kernel(
    blk, ada, head_w, head_b, noise, book, phi, phi_b, f_hat, out,
    h, mine, theirs, g, book_x, stage, turned, got,
    t_s, t_r, y_s, y_r, l_s, z_s, z_r, w_s, w_r, c_s, c_r, m_s, m_r,
):
    ylo, x, yhi, z, core = position()
    dp, mp = lax.axis_index("dp"), lax.axis_index("mp")
    sib = device(ylo, x, yhi, z, 1 - core)
    twin = device(1 - ylo, x, yhi, z, core)
    partner = device(1 - ylo, x, 1 - yhi, z, core)
    zr_i, zl_i, zo_i = (z + 1) % 4, (z + 3) % 4, (z + 2) % 4
    zr, zl = device(ylo, x, yhi, zr_i, core), device(ylo, x, yhi, zl_i, core)
    arrived = greet([twin, partner] + [(dp, (mp + o) % 16) for o in range(1, 16)])

    @pl.loop(0, ROWS // 16)
    def _(i):
        rows = pl.ds(pl.multiple_of(i * 16, 16), 16)
        pair = ada[yhi]
        v = norm_rows(blk[rows, :].astype(F32)) * (1.0 + pair[1:2, :]) + pair[0:1, :]
        h[rows, :] = v.astype(BF)

    book_x[...] = jnp.where(lax.broadcasted_iota(jnp.int32, (VB, 128), 1) == SIDE, 1.0, 0.0).astype(BF)
    book_x[:, 0:32] = book[...]
    arrived()

    lo = pl.multiple_of(ylo * 64, 64)
    other = pl.multiple_of((1 - ylo) * 64, 64)
    t = [
        remote(
            h.at[pl.ds(pl.multiple_of(other + k * CR, CR), CR)], theirs.at[pl.ds(k * CR, CR)],
            t_s.at[k], t_r.at[k], twin,
        )
        for k in range(NCH)
    ]
    for cp in t:
        cp.start()
    same = ylo == yhi
    home = device(yhi, x, yhi, z, core)
    away = device(yhi, x, 1 - yhi, z, core)
    own_weight = jnp.where(ylo == 0, 1.0 + GUIDE, -GUIDE)
    twin_weight = jnp.where(ylo == 0, -GUIDE, 1.0 + GUIDE)

    def slot(k, zi, half):
        return g.at[zi, core, half, pl.ds(k * CR, CR)]

    def away_copy(k):
        return remote(mine.at[pl.ds(k * CR, CR)], slot(k, z, ylo), y_s.at[k, 0], y_r.at[k, ylo], away)

    def home_copy(k):
        return remote(mine.at[pl.ds(k * CR, CR)], slot(k, z, ylo), y_s.at[k, 1], y_r.at[k, ylo], home)

    def stay_copy(k):
        return pltpu.make_async_copy(mine.at[pl.ds(k * CR, CR)], slot(k, z, ylo), l_s.at[k])

    def z1(k):
        return [
            remote(slot(k, z, i), slot(k, z, i), z_s.at[k, d, i], z_r.at[k, d, i], target)
            for d, target in ((0, zr), (1, zl)) for i in range(2)
        ]

    def z2(k):
        return [
            remote(slot(k, zl_i, 0), slot(k, zl_i, 0), w_s.at[k, 0], w_r.at[k, 0], zr),
            remote(slot(k, zr_i, 1), slot(k, zr_i, 1), w_s.at[k, 1], w_r.at[k, 1], zl),
        ]

    def cross(k, step, zi):
        return [
            remote(slot(k, zi, i), slot(k, zi, i), c_s.at[k, step, i], c_r.at[k, step, i], sib)
            for i in range(2)
        ]

    def mix(k):
        t[k].wait_recv()
        rows = pl.ds(k * CR, CR)
        own = h[pl.ds(pl.multiple_of(lo + k * CR, CR), CR), :].astype(F32)
        mine[rows, :] = (own_weight * own + twin_weight * theirs[rows, :].astype(F32)).astype(BF)
        away_copy(k).start()

        @pl.when(same)
        def _():
            stay_copy(k).start()

        @pl.when(jnp.logical_not(same))
        def _():
            home_copy(k).start()

    def gathered(k):
        @pl.when(same)
        def _():
            stay_copy(k).wait()
            remote(mine.at[pl.ds(k * CR, CR)], slot(k, z, 1 - ylo), y_s.at[k, 0], y_r.at[k, 1 - ylo], away).wait_recv()

        @pl.when(jnp.logical_not(same))
        def _():
            for i in range(2):
                remote(mine.at[pl.ds(k * CR, CR)], slot(k, z, i), y_s.at[k, 0], y_r.at[k, i], away).wait_recv()

        for cp in z1(k) + cross(k, 0, z):
            cp.start()

    def second(k):
        for cp in z1(k):
            cp.wait_recv()
        for cp in z2(k) + cross(k, 1, zr_i) + cross(k, 2, zl_i):
            cp.start()

    def third(k):
        for cp in z2(k):
            cp.wait_recv()
        for cp in cross(k, 3, zo_i):
            cp.start()

    for k in range(NCH + 3):
        if k < NCH:
            mix(k)
        if 0 <= k - 1 < NCH:
            gathered(k - 1)
        if 0 <= k - 2 < NCH:
            second(k - 2)
        if 0 <= k - 3 < NCH:
            third(k - 3)
    for k in range(NCH):
        for cp in cross(k, 0, z) + cross(k, 1, zr_i) + cross(k, 2, zl_i) + cross(k, 3, zo_i):
            cp.wait_recv()

    @pl.loop(0, 4)
    def _(i):
        rows = pl.ds(pl.multiple_of(i * 256, 256), 256)
        lhs = g[pl.ds(i, 1)].reshape(256, D)
        scores = jnp.dot(lhs, head_w[...], preferred_element_type=F32) + head_b[...] + noise[0, rows, :]
        peak = jnp.max(scores, axis=1, keepdims=True)
        weights = jnp.exp(scores - peak).astype(BF)
        code = jnp.dot(weights, book_x[...], preferred_element_type=F32)
        code = jnp.where(lax.broadcasted_iota(jnp.int32, code.shape, 1) == SIDE + 1, peak, code)
        flipped = jnp.transpose(code)
        turned[:, pl.ds(pl.multiple_of(128 + i * 256, 128), 256)] = flipped[0:MSG, :]

    zeros = jnp.zeros((MSG, 128), F32)
    turned[:, 0:128] = zeros
    turned[:, 1152:1280] = zeros
    cells = turned[...]
    for parity, shift in ((0, 96), (1, 32)):
        rolled = pltpu.roll(cells, 1280 - shift, 1)
        for i in range(8):
            to = 2 * i + parity
            start = (128 + 64 * to - 32 - shift)
            stage[to] = rolled[:, start:start + 128]

    posts = []
    for o in range(1, 16):
        to = (mp + o) % 16
        cp = remote(stage.at[to], got.at[o], m_s.at[o], m_r.at[o], (dp, to))
        cp.start()
        posts.append(cp)
    got[0] = stage[mp]
    for cp in posts:
        cp.wait_recv()
    peaks = got[:, SIDE + 1:SIDE + 2, :]
    factor = jnp.exp(peaks - jnp.max(peaks, axis=0, keepdims=True))
    sums = jnp.sum(got[:, 0:MSG, :] * factor, axis=0)
    lane = lax.broadcasted_iota(jnp.int32, (1, 128), 1)
    outside = jnp.logical_or(jnp.logical_and(mp == 0, lane < 32), jnp.logical_and(mp == 15, lane >= 96))
    soft = jnp.where(outside, 0.0, sums[0:32] / jnp.where(outside, 1.0, sums[32:33]))
    taps = []
    for i in range(3):
        for j in range(3):
            offset = 32 * (i - 1) + (j - 1)
            tap = soft if offset == 0 else pltpu.roll(soft, (-offset) % 128, 1)
            if j == 0:
                tap = jnp.where(lane % 32 == 0, 0.0, tap)
            if j == 2:
                tap = jnp.where(lane % 32 == 31, 0.0, tap)
            taps.append(tap)
    conv = jnp.dot(
        phi[...], jnp.concatenate(taps, axis=0), preferred_element_type=F32, precision=lax.Precision.HIGHEST
    )
    total = 0.5 * soft + 0.5 * (conv + phi_b[...])
    out[0] = f_hat[0] + pltpu.roll(total, 96, 1)[:, 0:64]

    for cp in t + posts:
        cp.wait_send()
    for k in range(NCH):
        away_copy(k).wait_send()

        @pl.when(jnp.logical_not(same))
        def _():
            home_copy(k).wait_send()

        for cp in z1(k) + z2(k) + cross(k, 0, z) + cross(k, 1, zr_i) + cross(k, 2, zl_i) + cross(k, 3, zo_i):
            cp.wait_send()


NCH = 2
CR = 64 // NCH


def head_block(block_out, ada, head_w, head_b, noise, book, phi, phi_b, f_hat):
    dma = pltpu.SemaphoreType.DMA
    vmem = pl.BlockSpec(memory_space=pltpu.VMEM)
    return pl.pallas_call(
        head_kernel,
        out_shape=jax.ShapeDtypeStruct((1, 32, 64), F32),
        in_specs=[vmem] * 9,
        out_specs=vmem,
        scratch_shapes=[
            pltpu.VMEM((ROWS, D), BF),
            pltpu.VMEM((64, D), BF),
            pltpu.VMEM((64, D), BF),
            pltpu.VMEM((4, 2, 2, 64, D), BF),
            pltpu.VMEM((VB, 128), BF),
            pltpu.VMEM((16, MSG, 128), F32),
            pltpu.VMEM((MSG, 1280), F32),
            pltpu.VMEM((16, MSG, 128), F32),
            dma((NCH,)), dma((NCH,)),
            dma((NCH, 2)), dma((NCH, 2)),
            dma((NCH,)),
            dma((NCH, 2, 2)), dma((NCH, 2, 2)),
            dma((NCH, 2)), dma((NCH, 2)),
            dma((NCH, 4, 2)), dma((NCH, 4, 2)),
            dma((16,)), dma((16,)),
        ],
        name="head_block",
        compiler_params=pltpu.CompilerParams(
            collective_id=2, has_side_effects=True, vmem_limit_bytes=60 * 1024 * 1024
        ),
    )(
        block_out, ada, head_w, head_b.reshape(1, -1), noise, book,
        jnp.transpose(phi, (0, 2, 3, 1)).reshape(32, 288), phi_b.reshape(32, 1), f_hat,
    )


def body(
    tokens, ada_ffn, ffn_gate, up_weight, up_bias, down_weight, down_bias, ada_head,
    head_weight, head_bias, gumbel_noise, codebook, phi_weight, phi_bias, f_hat,
):
    block_out = ffn_block(tokens, ada_ffn, ffn_gate, up_weight, up_bias, down_weight, down_bias)
    f_hat_out = head_block(
        block_out, ada_head, head_weight, head_bias, gumbel_noise, codebook, phi_weight, phi_bias, f_hat
    )
    return (block_out, f_hat_out)


def solution(mesh):
    in_specs = (
        P(("dp", "mp"), None),
        P("dp", None, None),
        P("dp", None),
        P(None, "mp"),
        P("mp"),
        P("mp", None),
        P(),
        P("dp", None, None),
        P(None, "mp"),
        P("mp"),
        P("dp", None, "mp"),
        P("mp", None),
        P(),
        P(),
        P("dp", None, "mp"),
    )
    out_specs = (P(("dp", "mp"), None), P("dp", None, "mp"))
    return jax.shard_map(body, mesh=mesh, in_specs=in_specs, out_specs=out_specs, check_vma=False)
```

```python
import functools

import jax
import jax.numpy as jnp
from jax import lax
from jax.experimental import pallas as pl
from jax.experimental.pallas import tpu as pltpu
from jax.sharding import PartitionSpec as P

MESH = pl.DeviceIdType.MESH
BF = jnp.bfloat16
F32 = jnp.float32

D = 2304
ROWS = 128
HID = 576
FOREIGN = 2 * HID
DQ = HID // 4
UNITS = (
    ("ring", "up", 0, 128),
    ("ring", "up", 128, 192),
    ("ring", "up", 320, 256),
    ("twin", "down", 0, 512),
    ("ring", "down", 512, 768),
    ("ring", "down", 1280, 512),
    ("twin", "down", 1792, 512),
)
PUSHED = (0, 1, 2, 3, 4, 5, 6)
NU = len(UNITS)
CHUNKS = tuple(k for k in range(NU) if UNITS[k][1] == "down")
NC = len(CHUNKS)
STEPS = (
    ("y", 0), ("a", 0), ("y", 1), ("b", 0), ("z", 1),
    ("y", 2), ("a", 1), ("z", 2), ("tile", 0), ("y", 3),
    ("tile", 1), ("tile", 2), ("a", 2), ("tile", 3), ("early", 0),
    ("early", 1), ("b", 1), ("early", 2), ("y", 4), ("early", 3),
    ("b", 2), ("a", 3), ("y", 5), ("late", 0), ("tile", 4),
    ("tile", 5), ("tile", 6), ("tile", 7), ("tile", 8), ("a", 4),
    ("first", 0), ("y", 6), ("a", 5), ("second", 0), ("b", 4),
    ("first", 1), ("b", 5), ("finish", 0), ("first", 2), ("a", 6),
    ("second", 1), ("first", 3), ("second", 2), ("finish", 1), ("second", 3),
    ("finish", 2), ("finish", 3),
)
NARROW = 256
FIRST = 1024
SIDE = 32
VB = 256
MSG = 40
GUIDE = 1.5


def position():
    dp, mp = lax.axis_index("dp"), lax.axis_index("mp")
    return dp // 4, dp % 4, mp // 8, (mp // 2) % 4, mp % 2


def device(ylo, x, yhi, z, core):
    return (ylo * 4 + x, yhi * 8 + z * 2 + core)


def remote(src, dst, send, recv, target):
    return pltpu.make_async_remote_copy(
        src_ref=src, dst_ref=dst, send_sem=send, recv_sem=recv, device_id=target, device_id_type=MESH
    )


def norm_rows(values):
    centred = values - jnp.mean(values, axis=-1, keepdims=True)
    spread = jnp.mean(centred * centred, axis=-1, keepdims=True)
    return centred * lax.rsqrt(spread + 1e-06)


def gelu(v):
    return 0.5 * v * (1.0 + jnp.tanh(0.7978845608028654 * (v + 0.044715 * v * v * v)))


def greet(targets):
    barrier = pltpu.get_barrier_semaphore()
    for target in targets:
        pl.semaphore_signal(barrier, inc=1, device_id=target, device_id_type=MESH)
    return lambda: pl.semaphore_wait(barrier, len(targets))


def ffn_part(
    arrived, tok, ada, gate, up_w, up_b, down_w, down_b, out,
    xn, up, dns, ub, bias_row, hid, parts, opps, nbrs, gots,
    loc_s, y_s, y_r, a_s, a_r, b_s, b_r, c_s, c_r, o_s, o_r, z_s, z_r, bias_s, bias_r,
    p_s, p_r, q_s, q_r,
):
    ylo, x, yhi, z, core = position()
    sib = device(ylo, x, yhi, z, 1 - core)
    partner = device(1 - ylo, x, 1 - yhi, z, core)
    partner_sib = device(1 - ylo, x, 1 - yhi, z, 1 - core)
    twin = device(1 - ylo, x, yhi, z, core)
    x_l, x_r = (x + 3) % 4, (x + 1) % 4
    xr, xl = device(ylo, x_r, yhi, z, core), device(ylo, x_l, yhi, z, core)
    zr_i, zl_i, zo_i = (z + 1) % 4, (z + 3) % 4, (z + 2) % 4
    zr, zl = device(ylo, x, yhi, zr_i, core), device(ylo, x, yhi, zl_i, core)

    own_rows, sib_rows = pl.ds(0, HID), pl.ds(HID, HID)

    def cols(j):
        return pl.ds(UNITS[CHUNKS[j]][2], UNITS[CHUNKS[j]][3])

    loc_up = pltpu.make_async_copy(up_w, up.at[own_rows], loc_s.at[0])
    loc_up.start()
    loc_dn = [
        pltpu.make_async_copy(down_w.at[:, cols(j)], dns[j].at[own_rows], loc_s.at[3 + j]) for j in range(NC)
    ]
    loc_bias = pltpu.make_async_copy(up_b, ub.at[0], loc_s.at[2])
    loc_bias.start()

    @pl.loop(0, ROWS // 16)
    def _(i):
        rows = pl.ds(pl.multiple_of(i * 16, 16), 16)
        pair = ada[yhi]
        v = norm_rows(tok[rows, :].astype(F32)) * (1.0 + pair[1:2, :]) + pair[0:1, :]
        xn[z, rows, :] = v.astype(BF)

    arrived()

    def part_of(k, count, index, foreign=True):
        way, panel, first, size = UNITS[k]
        base = FOREIGN if foreign else 0
        if panel == "up":
            rows = pl.ds(pl.multiple_of(base + first + index * (size // count), 16), size // count)
            return (up if foreign else up_w).at[rows]
        rows = pl.ds(pl.multiple_of(base + index * (HID // count), 16), HID // count)
        return dns[CHUNKS.index(k)].at[rows] if foreign else down_w.at[rows, pl.ds(first, size)]

    def half_of(k, index, half):
        way, panel, first, size = UNITS[k]
        if panel == "up":
            rows = pl.ds(pl.multiple_of(FOREIGN + first + index * (size // 4), 16), size // 4)
            return up.at[rows, pl.ds(half * (D // 2), D // 2)]
        rows = pl.ds(pl.multiple_of(FOREIGN + index * DQ, 16), DQ)
        return dns[CHUNKS.index(k)].at[rows, pl.ds(half * (size // 2), size // 2)]

    def whole(k, base):
        way, panel, first, size = UNITS[k]
        if panel == "up":
            return up.at[pl.ds(base + first, size)]
        return dns[CHUNKS.index(k)].at[pl.ds(base, HID)]

    y, a, b, c = [], [], [], []
    for k in range(NU):
        c.append(remote(whole(k, FOREIGN), whole(k, FOREIGN + HID), c_s.at[k], c_r.at[k], sib))
        if UNITS[k][0] == "ring":
            own = part_of(k, 4, x)
            y.append(remote(part_of(k, 4, x, False), own, y_s.at[k], y_r.at[k], partner))
            a.append([
                remote(own, own, a_s.at[k, 0], a_r.at[k, 0], xr), remote(own, own, a_s.at[k, 1], a_r.at[k, 1], xl)
            ])
            from_l, from_r = half_of(k, x_l, 0), half_of(k, x_r, 1)
            b.append([
                remote(from_l, from_l, b_s.at[k, 0], b_r.at[k, 0], xr),
                remote(from_r, from_r, b_s.at[k, 1], b_r.at[k, 1], xl),
            ])
        else:
            y.append(remote(
                part_of(k, 2, 1 - ylo, False), part_of(k, 2, 1 - ylo), y_s.at[k], y_r.at[k], partner
            ))
            own = part_of(k, 2, ylo)
            a.append([remote(own, own, a_s.at[k, 0], a_r.at[k, 0], twin)])
            b.append([])

    z1 = [
        remote(xn.at[z], xn.at[z], z_s.at[0], z_r.at[0], zr),
        remote(xn.at[z], xn.at[z], z_s.at[1], z_r.at[1], zl),
    ]
    z2 = [
        remote(xn.at[zl_i, pl.ds(0, 64)], xn.at[zl_i, pl.ds(0, 64)], z_s.at[2], z_r.at[2], zr),
        remote(xn.at[zr_i, pl.ds(64, 64)], xn.at[zr_i, pl.ds(64, 64)], z_s.at[3], z_r.at[3], zl),
    ]
    own_up = remote(up_w, up.at[sib_rows], o_s.at[0], o_r.at[0], sib)
    own_dn = [
        remote(down_w.at[:, cols(j)], dns[j].at[sib_rows], o_s.at[1 + j], o_r.at[1 + j], sib) for j in range(NC)
    ]
    biases = [
        remote(up_b, ub.at[1], bias_s.at[0], bias_r.at[0], sib),
        remote(up_b, ub.at[2], bias_s.at[1], bias_r.at[1], partner),
        remote(up_b, ub.at[3], bias_s.at[2], bias_r.at[2], partner_sib),
    ]

    def start(*copies):
        for cp in copies:
            cp.start()

    def recv(*copies):
        for cp in copies:
            cp.wait_recv()

    def hidden(n):
        units = pl.ds(n * NARROW, NARROW)

        @pl.loop(0, 2)
        def _(m):
            rows = pl.ds(pl.multiple_of(m * 256, 256), 256)
            acc = lax.dot_general(
                xn[pl.ds(2 * m, 2)].reshape(256, D), up[units, :], (((1,), (1,)), ((), ())),
                preferred_element_type=F32,
            )
            hid[rows, units] = gelu(acc + bias_row[:, units]).astype(BF)

    def partial(j, late):
        units = pl.ds(FIRST, D - FIRST) if late else pl.ds(0, FIRST)
        width = UNITS[CHUNKS[j]][3]

        @pl.loop(0, 2)
        def _(m):
            rows = pl.ds(pl.multiple_of(m * 256, 256), 256)
            acc = jnp.dot(hid[rows, units], dns[j][units], preferred_element_type=F32).reshape(2, ROWS, width)
            if late:
                acc = acc + parts[j][pl.ds(2 * m, 2)]
            parts[j][pl.ds(2 * m, 2)] = acc

    low, high = pl.ds(0, 64), pl.ds(64, 64)

    p1 = [
        [
            remote(opps[j].at[low], gots[j].at[0, 0], p_s.at[j, 0, 0], p_r.at[j, 0, 0], zr),
            remote(opps[j].at[high], gots[j].at[1, 0], p_s.at[j, 1, 0], p_r.at[j, 1, 0], zl),
        ]
        for j in range(NC)
    ]
    ind = [
        [
            remote(nbrs[j].at[0, 0], gots[j].at[0, 1], p_s.at[j, 0, 1], p_r.at[j, 0, 1], zr),
            remote(nbrs[j].at[1, 0], gots[j].at[1, 1], p_s.at[j, 1, 1], p_r.at[j, 1, 1], zl),
        ]
        for j in range(NC)
    ]
    p2 = [
        [
            remote(nbrs[j].at[0, 1], gots[j].at[0, 2], q_s.at[j, 0], q_r.at[j, 0], zr),
            remote(nbrs[j].at[1, 1], gots[j].at[1, 2], q_s.at[j, 1], q_r.at[j, 1], zl),
        ]
        for j in range(NC)
    ]

    def reduce_first(j):
        recv(c[CHUNKS[j]])
        partial(j, True)
        opps[j][...] = parts[j][zo_i].astype(BF)
        start(*p1[j])
        nbrs[j][0, 0] = parts[j][zr_i, high].astype(BF)
        nbrs[j][1, 0] = parts[j][zl_i, low].astype(BF)
        start(*ind[j])

    def reduce_second(j):
        recv(*p1[j])
        nbrs[j][0, 1] = (parts[j][zr_i, low] + gots[j][0, 0].astype(F32)).astype(BF)
        nbrs[j][1, 1] = (parts[j][zl_i, high] + gots[j][1, 0].astype(F32)).astype(BF)
        start(*p2[j])

    def finish(j):
        recv(*ind[j], *p2[j])
        for rows, left, right in ((low, 2, 1), (high, 1, 2)):
            total = parts[j][z, rows] + gots[j][0, left].astype(F32) + gots[j][1, right].astype(F32)
            total = total + down_b[:, cols(j)]
            out[rows, cols(j)] = (
                tok[rows, cols(j)].astype(F32) + gate[pl.ds(yhi, 1), cols(j)] * total
            ).astype(BF)

    start(y[PUSHED[0]], *z1, *biases, own_up)
    for cp in loc_dn:
        cp.start()
    y[PUSHED[0]].wait_send()
    start(y[PUSHED[1]], y[PUSHED[2]])
    for op, k in STEPS:
        if op == "y":
            recv(y[k])
            start(*a[k])
            at = PUSHED.index(k)
            if 0 < at < NU - 2:
                start(y[PUSHED[at + 2]])
        elif op == "a":
            recv(*a[k])
            start(*(b[k] if UNITS[k][0] == "ring" else [c[k]]))
        elif op == "b":
            recv(*b[k])
            start(c[k])
        elif op == "z" and k == 1:
            recv(*z1)
            start(*z2, *own_dn)
        elif op == "z":
            loc_bias.wait()
            recv(*biases)
            bias_row[...] = jnp.concatenate([ub[i] for i in range(4)], axis=1)
            loc_up.wait()
            recv(own_up, *z2)
        elif op == "early":
            loc_dn[k].wait()
            recv(own_dn[k])
            partial(k, False)
        elif op == "tile":
            hidden(k)
        elif op == "late":
            recv(*[c[i] for i in range(NU) if UNITS[i][1] == "up"])
        elif op == "first":
            reduce_first(k)
        elif op == "second":
            reduce_second(k)
        else:
            finish(k)

    y[PUSHED[0]] = None
    for cp in [v for v in y if v is not None] + c + z1 + z2 + [own_up] + own_dn + biases:
        cp.wait_send()
    for group in a + b + p1 + ind + p2:
        for cp in group:
            cp.wait_send()


def head_part(
    blk, ada, head_w, head_b, noise, phi, phi_b, f_hat, out,
    h, mine, theirs, g, book_x, stage, turned, got,
    t_s, t_r, y_s, y_r, l_s, z_s, z_r, w_s, w_r, c_s, c_r, m_s, m_r,
):
    ylo, x, yhi, z, core = position()
    dp, mp = lax.axis_index("dp"), lax.axis_index("mp")
    sib = device(ylo, x, yhi, z, 1 - core)
    twin = device(1 - ylo, x, yhi, z, core)
    partner = device(1 - ylo, x, 1 - yhi, z, core)
    zr_i, zl_i, zo_i = (z + 1) % 4, (z + 3) % 4, (z + 2) % 4
    zr, zl = device(ylo, x, yhi, zr_i, core), device(ylo, x, yhi, zl_i, core)
    lo = pl.multiple_of(ylo * 64, 64)
    other = pl.multiple_of((1 - ylo) * 64, 64)
    t = [
        remote(
            h.at[pl.ds(pl.multiple_of(other + k * CR, CR), CR)], theirs.at[pl.ds(k * CR, CR)],
            t_s.at[k], t_r.at[k], twin,
        )
        for k in range(NCH)
    ]
    pair = ada[yhi]

    def normalise(rows):
        v = norm_rows(blk[rows, :].astype(F32)) * (1.0 + pair[1:2, :]) + pair[0:1, :]
        h[rows, :] = v.astype(BF)

    for k in range(NCH):
        normalise(pl.ds(pl.multiple_of(other + k * CR, CR), CR))
        t[k].start()
    for k in range(NCH):
        normalise(pl.ds(pl.multiple_of(lo + k * CR, CR), CR))
    same = ylo == yhi
    home = device(yhi, x, yhi, z, core)
    away = device(yhi, x, 1 - yhi, z, core)
    own_weight = jnp.where(ylo == 0, 1.0 + GUIDE, -GUIDE)
    twin_weight = jnp.where(ylo == 0, -GUIDE, 1.0 + GUIDE)

    def slot(k, zi, half):
        return g.at[zi, core, half, pl.ds(k * CR, CR)]

    def away_copy(k):
        return remote(mine.at[pl.ds(k * CR, CR)], slot(k, z, ylo), y_s.at[k, 0], y_r.at[k, ylo], away)

    def home_copy(k):
        return remote(mine.at[pl.ds(k * CR, CR)], slot(k, z, ylo), y_s.at[k, 1], y_r.at[k, ylo], home)

    def stay_copy(k):
        return pltpu.make_async_copy(mine.at[pl.ds(k * CR, CR)], slot(k, z, ylo), l_s.at[k])

    def z1(k):
        return [
            remote(slot(k, z, i), slot(k, z, i), z_s.at[k, d, i], z_r.at[k, d, i], target)
            for d, target in ((0, zr), (1, zl)) for i in range(2)
        ]

    def z2(k):
        return [
            remote(slot(k, zl_i, 0), slot(k, zl_i, 0), w_s.at[k, 0], w_r.at[k, 0], zr),
            remote(slot(k, zr_i, 1), slot(k, zr_i, 1), w_s.at[k, 1], w_r.at[k, 1], zl),
        ]

    def cross(k, step, zi):
        return [
            remote(slot(k, zi, i), slot(k, zi, i), c_s.at[k, step, i], c_r.at[k, step, i], sib)
            for i in range(2)
        ]

    def mix(k):
        t[k].wait_recv()
        rows = pl.ds(k * CR, CR)
        own = h[pl.ds(pl.multiple_of(lo + k * CR, CR), CR), :].astype(F32)
        mine[rows, :] = (own_weight * own + twin_weight * theirs[rows, :].astype(F32)).astype(BF)
        away_copy(k).start()

        @pl.when(same)
        def _():
            stay_copy(k).start()

        @pl.when(jnp.logical_not(same))
        def _():
            home_copy(k).start()

    def gathered(k):
        @pl.when(same)
        def _():
            stay_copy(k).wait()
            remote(mine.at[pl.ds(k * CR, CR)], slot(k, z, 1 - ylo), y_s.at[k, 0], y_r.at[k, 1 - ylo], away).wait_recv()

        @pl.when(jnp.logical_not(same))
        def _():
            for i in range(2):
                remote(mine.at[pl.ds(k * CR, CR)], slot(k, z, i), y_s.at[k, 0], y_r.at[k, i], away).wait_recv()

        for cp in z1(k) + cross(k, 0, z):
            cp.start()

    def second(k):
        for cp in z1(k):
            cp.wait_recv()
        for cp in z2(k) + cross(k, 1, zr_i) + cross(k, 2, zl_i):
            cp.start()

    def third(k):
        for cp in z2(k):
            cp.wait_recv()
        for cp in cross(k, 3, zo_i):
            cp.start()

    for k in range(NCH + 3):
        if k < NCH:
            mix(k)
        if 0 <= k - 1 < NCH:
            gathered(k - 1)
        if 0 <= k - 2 < NCH:
            second(k - 2)
        if 0 <= k - 3 < NCH:
            third(k - 3)
    for k in range(NCH):
        for cp in cross(k, 0, z) + cross(k, 1, zr_i) + cross(k, 2, zl_i) + cross(k, 3, zo_i):
            cp.wait_recv()

    @pl.loop(0, 4)
    def _(i):
        rows = pl.ds(pl.multiple_of(i * 256, 256), 256)
        lhs = g[pl.ds(i, 1)].reshape(256, D)
        scores = jnp.dot(lhs, head_w[...], preferred_element_type=F32) + head_b[...] + noise[0, rows, :]
        peak = jnp.max(scores, axis=1, keepdims=True)
        weights = jnp.exp(scores - peak).astype(BF)
        code = jnp.dot(weights, book_x[...], preferred_element_type=F32)
        code = jnp.where(lax.broadcasted_iota(jnp.int32, code.shape, 1) == SIDE + 1, peak, code)
        flipped = jnp.transpose(code)
        turned[:, pl.ds(pl.multiple_of(128 + i * 256, 128), 256)] = flipped[0:MSG, :]

    zeros = jnp.zeros((MSG, 128), F32)
    turned[:, 0:128] = zeros
    turned[:, 1152:1280] = zeros
    cells = turned[...]
    for parity, shift in ((0, 96), (1, 32)):
        rolled = pltpu.roll(cells, 1280 - shift, 1)
        for i in range(8):
            to = 2 * i + parity
            start = (128 + 64 * to - 32 - shift)
            stage[to] = rolled[:, start:start + 128]

    posts = []
    for o in range(1, 16):
        to = (mp + o) % 16
        cp = remote(stage.at[to], got.at[o], m_s.at[o], m_r.at[o], (dp, to))
        cp.start()
        posts.append(cp)
    got[0] = stage[mp]
    for cp in posts:
        cp.wait_recv()
    peaks = got[:, SIDE + 1:SIDE + 2, :]
    factor = jnp.exp(peaks - jnp.max(peaks, axis=0, keepdims=True))
    sums = jnp.sum(got[:, 0:MSG, :] * factor, axis=0)
    lane = lax.broadcasted_iota(jnp.int32, (1, 128), 1)
    outside = jnp.logical_or(jnp.logical_and(mp == 0, lane < 32), jnp.logical_and(mp == 15, lane >= 96))
    soft = jnp.where(outside, 0.0, sums[0:32] / jnp.where(outside, 1.0, sums[32:33]))
    taps = []
    for i in range(3):
        for j in range(3):
            offset = 32 * (i - 1) + (j - 1)
            tap = soft if offset == 0 else pltpu.roll(soft, (-offset) % 128, 1)
            if j == 0:
                tap = jnp.where(lane % 32 == 0, 0.0, tap)
            if j == 2:
                tap = jnp.where(lane % 32 == 31, 0.0, tap)
            taps.append(tap)
    square = lax.broadcasted_iota(jnp.int32, (32, 32), 0) == lax.broadcasted_iota(jnp.int32, (32, 32), 1)
    conv = jnp.sum(jnp.where(square, phi_b[...], 0.0), axis=1, keepdims=True)
    for i in range(3):
        for j in range(3):
            conv = conv + jnp.dot(
                phi[i, j], taps[3 * i + j], preferred_element_type=F32, precision=lax.Precision.HIGHEST
            )
    total = 0.5 * soft + 0.5 * conv
    out[0] = f_hat[0] + pltpu.roll(total, 96, 1)[:, 0:64]

    for cp in t + posts:
        cp.wait_send()
    for k in range(NCH):
        away_copy(k).wait_send()

        @pl.when(jnp.logical_not(same))
        def _():
            home_copy(k).wait_send()

        for cp in z1(k) + z2(k) + cross(k, 0, z) + cross(k, 1, zr_i) + cross(k, 2, zl_i) + cross(k, 3, zo_i):
            cp.wait_send()


NCH = 4
CR = 64 // NCH


def kernel(
    tok, ada, gate, up_w, up_b, down_w, down_b, ada_head, head_w, head_b, noise, book, phi, phi_b, f_hat, out, f_out,
    ffn_scratch, head_scratch, head_w_here, noise_here, load_s,
):
    ylo, x, yhi, z, core = position()
    dp, mp = lax.axis_index("dp"), lax.axis_index("mp")
    arrived = greet(
        [
            device(1 - ylo, x, yhi, z, core), device(1 - ylo, x, 1 - yhi, z, core),
            device(1 - ylo, x, 1 - yhi, z, 1 - core),
            device(ylo, (x + 1) % 4, yhi, z, core), device(ylo, (x + 3) % 4, yhi, z, core),
        ]
        + [(dp, (mp + o) % 16) for o in range(1, 16)]
    )
    loads = [
        pltpu.make_async_copy(head_w, head_w_here, load_s.at[0]),
        pltpu.make_async_copy(noise, noise_here, load_s.at[1]),
    ]
    for cp in loads:
        cp.start()
    book_x = head_scratch[4]
    wide = jnp.concatenate([book[...].astype(F32), jnp.zeros((96, VB), F32)], axis=0)
    wide = jnp.where(lax.broadcasted_iota(jnp.int32, (128, VB), 0) == SIDE, 1.0, wide)
    book_x[...] = jnp.transpose(wide).astype(BF)
    ffn_part(arrived, tok, ada, gate, up_w, up_b, down_w, down_b, out, *ffn_scratch)
    for cp in loads:
        cp.wait()
    head_part(out, ada_head, head_w_here, head_b, noise_here, phi, phi_b, f_hat, f_out, *head_scratch)


def body(
    tokens, ada_ffn, ffn_gate, up_weight, up_bias, down_weight, down_bias, ada_head,
    head_weight, head_bias, gumbel_noise, codebook, phi_weight, phi_bias, f_hat,
):
    dma = pltpu.SemaphoreType.DMA
    widths = [UNITS[k][3] for k in CHUNKS]
    vmem, anywhere = pl.BlockSpec(memory_space=pltpu.VMEM), pl.BlockSpec(memory_space=pl.ANY)
    ffn_scratch = [
        pltpu.VMEM((4, ROWS, D), BF),
        pltpu.VMEM((4 * HID, D), BF),
        [pltpu.VMEM((4 * HID, w), BF) for w in widths],
        pltpu.VMEM((4, 1, HID), F32),
        pltpu.VMEM((1, 4 * HID), F32),
        pltpu.VMEM((512, 4 * HID), BF),
        [pltpu.VMEM((4, ROWS, w), F32) for w in widths],
        [pltpu.VMEM((ROWS, w), BF) for w in widths],
        [pltpu.VMEM((2, 2, 64, w), BF) for w in widths],
        [pltpu.VMEM((2, 3, 64, w), BF) for w in widths],
        dma((3 + NC,)),
        dma((NU,)), dma((NU,)),
        dma((NU, 2)), dma((NU, 2)),
        dma((NU, 2)), dma((NU, 2)),
        dma((NU,)), dma((NU,)),
        dma((1 + NC,)), dma((1 + NC,)),
        dma((4,)), dma((4,)),
        dma((3,)), dma((3,)),
        dma((NC, 2, 2)), dma((NC, 2, 2)),
        dma((NC, 2)), dma((NC, 2)),
    ]
    head_scratch = [
        pltpu.VMEM((ROWS, D), BF),
        pltpu.VMEM((64, D), BF),
        pltpu.VMEM((64, D), BF),
        pltpu.VMEM((4, 2, 2, 64, D), BF),
        pltpu.VMEM((VB, 128), BF),
        pltpu.VMEM((16, MSG, 128), F32),
        pltpu.VMEM((MSG, 1280), F32),
        pltpu.VMEM((16, MSG, 128), F32),
        dma((NCH,)), dma((NCH,)),
        dma((NCH, 2)), dma((NCH, 2)),
        dma((NCH,)),
        dma((NCH, 2, 2)), dma((NCH, 2, 2)),
        dma((NCH, 2)), dma((NCH, 2)),
        dma((NCH, 4, 2)), dma((NCH, 4, 2)),
        dma((16,)), dma((16,)),
    ]
    return pl.pallas_call(
        kernel,
        out_shape=(jax.ShapeDtypeStruct((ROWS, D), BF), jax.ShapeDtypeStruct((1, 32, 64), F32)),
        in_specs=[vmem, vmem, vmem, anywhere, vmem, anywhere, vmem, vmem, anywhere, vmem, anywhere] + [vmem] * 4,
        out_specs=(vmem, vmem),
        scratch_shapes=[
            ffn_scratch,
            head_scratch,
            pltpu.VMEM((D, VB), BF),
            pltpu.VMEM((1, 1024, VB), F32),
            dma((2,)),
        ],
        name="var_step",
        compiler_params=pltpu.CompilerParams(
            collective_id=1, has_side_effects=True, vmem_limit_bytes=60 * 1024 * 1024
        ),
    )(
        tokens, ada_ffn, ffn_gate, up_weight.T, up_bias.reshape(1, -1), down_weight, down_bias.reshape(1, -1),
        ada_head, head_weight, head_bias.reshape(1, -1), gumbel_noise, codebook.T,
        jnp.transpose(phi_weight, (2, 3, 0, 1)), phi_bias.reshape(1, -1), f_hat,
    )


def solution(mesh):
    in_specs = (
        P(("dp", "mp"), None),
        P("dp", None, None),
        P("dp", None),
        P(None, "mp"),
        P("mp"),
        P("mp", None),
        P(),
        P("dp", None, None),
        P(None, "mp"),
        P("mp"),
        P("dp", None, "mp"),
        P("mp", None),
        P(),
        P(),
        P("dp", None, "mp"),
    )
    out_specs = (P(("dp", "mp"), None), P("dp", None, "mp"))
    return jax.shard_map(body, mesh=mesh, in_specs=in_specs, out_specs=out_specs, check_vma=False)
```

```python
import functools

import jax
import jax.numpy as jnp
from jax import lax
from jax.experimental import pallas as pl
from jax.experimental.pallas import tpu as pltpu
from jax.sharding import PartitionSpec as P

MESH = pl.DeviceIdType.MESH
BF = jnp.bfloat16
F32 = jnp.float32

D = 2304
ROWS = 128
HID = 576
FOREIGN = 2 * HID
DQ = HID // 4
TH = HID // 2
UNITS = (
    ("ring", "up", 0, 128),
    ("ring", "up", 128, 192),
    ("ring", "up", 320, 256),
    ("twin", "down", 0, 512),
    ("ring", "down", 512, 768),
    ("ring", "down", 1280, 512),
    ("twin", "down", 1792, 512),
)
PUSHED = (0, 1, 2, 3, 4, 5, 6)
NU = len(UNITS)
CHUNKS = tuple(k for k in range(NU) if UNITS[k][1] == "down")
NC = len(CHUNKS)
STEPS = (
    ("y", 0), ("a", 0), ("y", 1), ("b", 0), ("z", 1),
    ("y", 2), ("a", 1), ("z", 2), ("tile", 0), ("y", 3),
    ("tile", 1), ("tile", 2), ("a", 2), ("tile", 3), ("early", 0),
    ("early", 1), ("b", 1), ("early", 2), ("y", 4), ("early", 3),
    ("b", 2), ("a", 3), ("y", 5), ("late", 0), ("tile", 4),
    ("tile", 5), ("tile", 6), ("tile", 7), ("tile", 8), ("a", 4),
    ("first", 0), ("y", 6), ("a", 5), ("second", 0), ("b", 4),
    ("first", 1), ("b", 5), ("finish", 0), ("first", 2), ("a", 6),
    ("second", 1), ("first", 3), ("panel", 0), ("second", 2), ("finish", 1),
    ("panel", 1), ("second", 3), ("finish", 2), ("finish", 3),
)
NARROW = 256
FIRST = 1024
SIDE = 32
VB = 256
MSG = 40
GUIDE = 1.5


def position():
    dp, mp = lax.axis_index("dp"), lax.axis_index("mp")
    return dp // 4, dp % 4, mp // 8, (mp // 2) % 4, mp % 2


def device(ylo, x, yhi, z, core):
    return (ylo * 4 + x, yhi * 8 + z * 2 + core)


def remote(src, dst, send, recv, target):
    return pltpu.make_async_remote_copy(
        src_ref=src, dst_ref=dst, send_sem=send, recv_sem=recv, device_id=target, device_id_type=MESH
    )


def norm_rows(values):
    centred = values - jnp.mean(values, axis=-1, keepdims=True)
    spread = jnp.mean(centred * centred, axis=-1, keepdims=True)
    return centred * lax.rsqrt(spread + 1e-06)


def gelu(v):
    return 0.5 * v * (1.0 + jnp.tanh(0.7978845608028654 * (v + 0.044715 * v * v * v)))


def greet(targets):
    barrier = pltpu.get_barrier_semaphore()
    for target in targets:
        pl.semaphore_signal(barrier, inc=1, device_id=target, device_id_type=MESH)
    return lambda: pl.semaphore_wait(barrier, len(targets))


def ffn_part(
    arrived, ahead, tok, ada, gate, up_w, up_b, down_w, down_b, out,
    xn, up, dns, ub, bias_row, down_row, hid, parts, opps, nbrs, gots,
    loc_s, y_s, y_r, a_s, a_r, b_s, b_r, c_s, c_r, o_s, o_r, z_s, z_r, bias_s, bias_r,
    p_s, p_r, q_s, q_r,
):
    ylo, x, yhi, z, core = position()
    sib = device(ylo, x, yhi, z, 1 - core)
    partner = device(1 - ylo, x, 1 - yhi, z, core)
    partner_sib = device(1 - ylo, x, 1 - yhi, z, 1 - core)
    twin = device(1 - ylo, x, yhi, z, core)
    x_l, x_r = (x + 3) % 4, (x + 1) % 4
    xr, xl = device(ylo, x_r, yhi, z, core), device(ylo, x_l, yhi, z, core)
    zr_i, zl_i, zo_i = (z + 1) % 4, (z + 3) % 4, (z + 2) % 4
    zr, zl = device(ylo, x, yhi, zr_i, core), device(ylo, x, yhi, zl_i, core)

    own_rows, sib_rows = pl.ds(0, HID), pl.ds(HID, HID)

    def cols(j):
        return pl.ds(UNITS[CHUNKS[j]][2], UNITS[CHUNKS[j]][3])

    loc_up = pltpu.make_async_copy(up_w, up.at[own_rows], loc_s.at[0])
    loc_up.start()
    loc_dn = [
        pltpu.make_async_copy(down_w.at[:, cols(j)], dns[j].at[own_rows], loc_s.at[3 + j]) for j in range(NC)
    ]
    loc_bias = pltpu.make_async_copy(up_b, ub.at[0, 0], loc_s.at[2])
    loc_bias.start()
    loc_down = pltpu.make_async_copy(down_b, down_row.at[0], loc_s.at[3 + NC])
    loc_down.start()

    @pl.loop(0, ROWS // 16)
    def _(i):
        rows = pl.ds(pl.multiple_of(i * 16, 16), 16)
        pair = ada[yhi]
        v = norm_rows(tok[rows, :].astype(F32)) * (1.0 + pair[1:2, :]) + pair[0:1, :]
        xn[z, rows, :] = v.astype(BF)

    arrived()

    def part_of(k, count, index, foreign=True):
        way, panel, first, size = UNITS[k]
        base = FOREIGN if foreign else 0
        if panel == "up":
            rows = pl.ds(pl.multiple_of(base + first + index * (size // count), 16), size // count)
            return (up if foreign else up_w).at[rows]
        rows = pl.ds(pl.multiple_of(base + index * (HID // count), 16), HID // count)
        return dns[CHUNKS.index(k)].at[rows] if foreign else down_w.at[rows, pl.ds(first, size)]

    def half_of(k, index, half):
        way, panel, first, size = UNITS[k]
        if panel == "up":
            rows = pl.ds(pl.multiple_of(FOREIGN + first + index * (size // 4), 16), size // 4)
            return up.at[rows, pl.ds(half * (D // 2), D // 2)]
        rows = pl.ds(pl.multiple_of(FOREIGN + index * DQ, 16), DQ)
        return dns[CHUNKS.index(k)].at[rows, pl.ds(half * (size // 2), size // 2)]

    def whole(k, base):
        way, panel, first, size = UNITS[k]
        if panel == "up":
            return up.at[pl.ds(base + first, size)]
        return dns[CHUNKS.index(k)].at[pl.ds(base, HID)]

    y, a, b, c = [], [], [], []
    for k in range(NU):
        c.append(remote(whole(k, FOREIGN), whole(k, FOREIGN + HID), c_s.at[k], c_r.at[k], sib))
        if UNITS[k][0] == "ring":
            own = part_of(k, 4, x)
            y.append(remote(part_of(k, 4, x, False), own, y_s.at[k], y_r.at[k], partner))
            a.append([
                remote(own, own, a_s.at[k, 0], a_r.at[k, 0], xr), remote(own, own, a_s.at[k, 1], a_r.at[k, 1], xl)
            ])
            from_l, from_r = half_of(k, x_l, 0), half_of(k, x_r, 1)
            b.append([
                remote(from_l, from_l, b_s.at[k, 0], b_r.at[k, 0], xr),
                remote(from_r, from_r, b_s.at[k, 1], b_r.at[k, 1], xl),
            ])
        else:
            y.append(remote(
                part_of(k, 2, 1 - ylo, False), part_of(k, 2, 1 - ylo), y_s.at[k], y_r.at[k], partner
            ))
            own = part_of(k, 2, ylo)
            a.append([remote(own, own, a_s.at[k, 0], a_r.at[k, 0], twin)])
            b.append([])

    z1 = [
        remote(xn.at[z], xn.at[z], z_s.at[0], z_r.at[0], zr),
        remote(xn.at[z], xn.at[z], z_s.at[1], z_r.at[1], zl),
    ]
    z2 = [
        remote(xn.at[zl_i, pl.ds(0, 64)], xn.at[zl_i, pl.ds(0, 64)], z_s.at[2], z_r.at[2], zr),
        remote(xn.at[zr_i, pl.ds(64, 64)], xn.at[zr_i, pl.ds(64, 64)], z_s.at[3], z_r.at[3], zl),
    ]
    own_up = remote(up_w, up.at[sib_rows], o_s.at[0], o_r.at[0], sib)
    own_dn = [
        remote(down_w.at[:, cols(j)], dns[j].at[sib_rows], o_s.at[1 + j], o_r.at[1 + j], sib) for j in range(NC)
    ]
    biases = [
        remote(up_b, ub.at[1, 0], bias_s.at[0], bias_r.at[0], sib),
        remote(up_b, ub.at[2, 0], bias_s.at[1], bias_r.at[1], partner),
        remote(up_b, ub.at[3, 0], bias_s.at[2], bias_r.at[2], partner_sib),
    ]

    def start(*copies):
        for cp in copies:
            cp.start()

    def recv(*copies):
        for cp in copies:
            cp.wait_recv()

    def hidden(n):
        units = pl.ds(n * NARROW, NARROW)

        @pl.loop(0, 2)
        def _(m):
            rows = pl.ds(pl.multiple_of(m * 256, 256), 256)
            acc = lax.dot_general(
                xn[pl.ds(2 * m, 2)].reshape(256, D), up[units, :], (((1,), (1,)), ((), ())),
                preferred_element_type=F32,
            )
            hid[rows, units] = gelu(acc + bias_row[:, units]).astype(BF)

    def partial(j, late):
        units = pl.ds(FIRST, D - FIRST) if late else pl.ds(0, FIRST)
        width = UNITS[CHUNKS[j]][3]

        @pl.loop(0, 2)
        def _(m):
            rows = pl.ds(pl.multiple_of(m * 256, 256), 256)
            acc = jnp.dot(hid[rows, units], dns[j][units], preferred_element_type=F32).reshape(2, ROWS, width)
            if late:
                acc = acc + parts[j][pl.ds(2 * m, 2)]
            parts[j][pl.ds(2 * m, 2)] = acc

    low, high = pl.ds(0, 64), pl.ds(64, 64)

    p1 = [
        [
            remote(opps[j].at[low], gots[j].at[0, 0], p_s.at[j, 0, 0], p_r.at[j, 0, 0], zr),
            remote(opps[j].at[high], gots[j].at[1, 0], p_s.at[j, 1, 0], p_r.at[j, 1, 0], zl),
        ]
        for j in range(NC)
    ]
    ind = [
        [
            remote(nbrs[j].at[0, 0], gots[j].at[0, 1], p_s.at[j, 0, 1], p_r.at[j, 0, 1], zr),
            remote(nbrs[j].at[1, 0], gots[j].at[1, 1], p_s.at[j, 1, 1], p_r.at[j, 1, 1], zl),
        ]
        for j in range(NC)
    ]
    p2 = [
        [
            remote(nbrs[j].at[0, 1], gots[j].at[0, 2], q_s.at[j, 0], q_r.at[j, 0], zr),
            remote(nbrs[j].at[1, 1], gots[j].at[1, 2], q_s.at[j, 1], q_r.at[j, 1], zl),
        ]
        for j in range(NC)
    ]

    def reduce_first(j):
        recv(c[CHUNKS[j]])
        partial(j, True)
        opps[j][...] = parts[j][zo_i].astype(BF)
        start(*p1[j])
        nbrs[j][0, 0] = parts[j][zr_i, high].astype(BF)
        nbrs[j][1, 0] = parts[j][zl_i, low].astype(BF)
        start(*ind[j])

    def reduce_second(j):
        recv(*p1[j])
        nbrs[j][0, 1] = (parts[j][zr_i, low] + gots[j][0, 0].astype(F32)).astype(BF)
        nbrs[j][1, 1] = (parts[j][zl_i, high] + gots[j][1, 0].astype(F32)).astype(BF)
        start(*p2[j])

    def finish(j):
        recv(*ind[j], *p2[j])
        for rows, left, right in ((low, 2, 1), (high, 1, 2)):
            total = parts[j][z, rows] + gots[j][0, left].astype(F32) + gots[j][1, right].astype(F32)
            total = total + down_row[:, cols(j)]
            out[rows, cols(j)] = (
                tok[rows, cols(j)].astype(F32) + gate[pl.ds(yhi, 1), cols(j)] * total
            ).astype(BF)

    start(y[PUSHED[0]], *z1, *biases, own_up)
    for cp in loc_dn:
        cp.start()
    y[PUSHED[0]].wait_send()
    start(y[PUSHED[1]], y[PUSHED[2]])
    for op, k in STEPS:
        if op == "y":
            recv(y[k])
            start(*a[k])
            at = PUSHED.index(k)
            if 0 < at < NU - 2:
                start(y[PUSHED[at + 2]])
            if k == PUSHED[-1]:
                start(ahead[0], *ahead[3])
        elif op == "panel" and k == 0:
            recv(ahead[0])
            start(*ahead[1])
        elif op == "panel":
            recv(*ahead[1])
            start(*ahead[2])
        elif op == "a":
            recv(*a[k])
            start(*(b[k] if UNITS[k][0] == "ring" else [c[k]]))
        elif op == "b":
            recv(*b[k])
            start(c[k])
        elif op == "z" and k == 1:
            recv(*z1)
            start(*z2, *own_dn)
        elif op == "z":
            loc_bias.wait()
            loc_down.wait()
            recv(*biases)
            bias_row[...] = jnp.concatenate([ub[i] for i in range(4)], axis=1)
            loc_up.wait()
            recv(own_up, *z2)
        elif op == "early":
            loc_dn[k].wait()
            recv(own_dn[k])
            partial(k, False)
        elif op == "tile":
            hidden(k)
        elif op == "late":
            recv(*[c[i] for i in range(NU) if UNITS[i][1] == "up"])
        elif op == "first":
            reduce_first(k)
        elif op == "second":
            reduce_second(k)
        else:
            finish(k)

    y[PUSHED[0]] = None
    for cp in [v for v in y if v is not None] + c + z1 + z2 + [own_up] + own_dn + biases:
        cp.wait_send()
    for group in a + b + p1 + ind + p2:
        for cp in group:
            cp.wait_send()


def head_part(
    ahead, blk, ada, head_w, head_b, noise, phi, phi_b, f_hat, out,
    h, mine, theirs, g, book_x, stage, turned, got,
    t_s, t_r, y_s, y_r, l_s, z_s, z_r, w_s, w_r, c_s, c_r, m_s, m_r,
):
    ylo, x, yhi, z, core = position()
    dp, mp = lax.axis_index("dp"), lax.axis_index("mp")
    sib = device(ylo, x, yhi, z, 1 - core)
    twin = device(1 - ylo, x, yhi, z, core)
    partner = device(1 - ylo, x, 1 - yhi, z, core)
    zr_i, zl_i, zo_i = (z + 1) % 4, (z + 3) % 4, (z + 2) % 4
    zr, zl = device(ylo, x, yhi, zr_i, core), device(ylo, x, yhi, zl_i, core)
    lo = pl.multiple_of(ylo * 64, 64)
    other = pl.multiple_of((1 - ylo) * 64, 64)
    t = [
        remote(
            h.at[pl.ds(pl.multiple_of(other + k * CR, CR), CR)], theirs.at[pl.ds(k * CR, CR)],
            t_s.at[k], t_r.at[k], twin,
        )
        for k in range(NCH)
    ]
    pair = ada[yhi]

    def normalise(rows):
        v = norm_rows(blk[rows, :].astype(F32)) * (1.0 + pair[1:2, :]) + pair[0:1, :]
        h[rows, :] = v.astype(BF)

    for k in range(NCH):
        normalise(pl.ds(pl.multiple_of(other + k * CR, CR), CR))
        t[k].start()
    for k in range(NCH):
        normalise(pl.ds(pl.multiple_of(lo + k * CR, CR), CR))
    same = ylo == yhi
    own_weight = jnp.where(ylo == 0, 1.0 + GUIDE, -GUIDE)
    twin_weight = jnp.where(ylo == 0, -GUIDE, 1.0 + GUIDE)

    def slot(k, zi):
        return g.at[zi, core, pl.ds(k * CR, CR)]

    def slot_half(k, zi, half):
        return g.at[zi, core, pl.ds(k * CR, CR), pl.ds(half * (D // 2), D // 2)]

    def mixed(k):
        return mine.at[pl.ds(k * CR, CR)]

    swap = [remote(mixed(k), slot(k, z), y_s.at[k], y_r.at[k], partner) for k in range(NCH)]
    stay = [pltpu.make_async_copy(mixed(k), slot(k, z), l_s.at[k]) for k in range(NCH)]
    z1 = [
        [remote(slot(k, z), slot(k, z), z_s.at[k, d], z_r.at[k, d], to) for d, to in ((0, zr), (1, zl))]
        for k in range(NCH)
    ]
    z2 = [
        [
            remote(slot_half(k, zl_i, 0), slot_half(k, zl_i, 0), w_s.at[k, 0], w_r.at[k, 0], zr),
            remote(slot_half(k, zr_i, 1), slot_half(k, zr_i, 1), w_s.at[k, 1], w_r.at[k, 1], zl),
        ]
        for k in range(NCH)
    ]
    cross = [
        [remote(slot(k, zi), slot(k, zi), c_s.at[k, i], c_r.at[k, i], sib) for i, zi in enumerate((z, zr_i, zl_i, zo_i))]
        for k in range(NCH)
    ]

    def mix(k):
        t[k].wait_recv()
        rows = pl.ds(k * CR, CR)
        own = h[pl.ds(pl.multiple_of(lo + k * CR, CR), CR), :].astype(F32)
        mine[rows, :] = (own_weight * own + twin_weight * theirs[rows, :].astype(F32)).astype(BF)

        @pl.when(same)
        def _():
            stay[k].start()

        @pl.when(jnp.logical_not(same))
        def _():
            swap[k].start()

    def gathered(k):
        @pl.when(same)
        def _():
            stay[k].wait()

        @pl.when(jnp.logical_not(same))
        def _():
            swap[k].wait_recv()

        for cp in z1[k] + cross[k][:1]:
            cp.start()

    def second(k):
        for cp in z1[k]:
            cp.wait_recv()
        for cp in z2[k] + cross[k][1:3]:
            cp.start()

    def third(k):
        for cp in z2[k]:
            cp.wait_recv()
        cross[k][3].start()

    for k in range(NCH + 3):
        if k < NCH:
            mix(k)
        if 0 <= k - 1 < NCH:
            gathered(k - 1)
        if 0 <= k - 2 < NCH:
            second(k - 2)
        if 0 <= k - 3 < NCH:
            third(k - 3)
    for cp in ahead[2] + ahead[3]:
        cp.wait_recv()
    for k in range(NCH):
        for cp in cross[k]:
            cp.wait_recv()

    column = lax.broadcasted_iota(jnp.int32, (4, 64, 128), 2)
    nothing = jnp.where(column == SIDE + 1, -1e30, 0.0)

    @pl.loop(0, 2)
    def _(i):
        lhs = g[pl.ds(2 * i, 2)].reshape(256, D)
        scores = []
        for p in range(2):
            logits = jnp.dot(lhs, head_w[p], preferred_element_type=F32) + head_b[p]
            scores.append(logits + noise[p, pl.ds(4 * i, 4)].reshape(256, VB))
        peak = jnp.maximum(
            jnp.max(scores[0], axis=1, keepdims=True), jnp.max(scores[1], axis=1, keepdims=True)
        )
        code = jnp.zeros((256, 128), F32)
        for p in range(2):
            weights = jnp.exp(scores[p] - peak).astype(BF)
            code = code + jnp.dot(weights, book_x[p], preferred_element_type=F32)
        code = jnp.where(lax.broadcasted_iota(jnp.int32, code.shape, 1) == SIDE + 1, peak, code).reshape(4, 64, 128)
        spread = jnp.concatenate(
            [jnp.where(yhi == 0, code, nothing), jnp.where(yhi == 1, code, nothing)], axis=1
        ).reshape(512, 128)
        flipped = jnp.transpose(spread)
        turned[:, pl.ds(pl.multiple_of(128 + i * 512, 128), 512)] = flipped[0:MSG, :]

    zeros = jnp.zeros((MSG, 128), F32)
    turned[:, 0:128] = zeros
    turned[:, 1152:1280] = zeros
    cells = turned[...]
    for parity, shift in ((0, 96), (1, 32)):
        rolled = pltpu.roll(cells, 1280 - shift, 1)
        for i in range(8):
            to = 2 * i + parity
            start = (128 + 64 * to - 32 - shift)
            stage[to] = rolled[:, start:start + 128]

    posts = []
    for o in range(1, 16):
        to = (mp + o) % 16
        cp = remote(stage.at[to], got.at[o], m_s.at[o], m_r.at[o], (dp, to))
        cp.start()
        posts.append(cp)
    got[0] = stage[mp]
    for cp in posts:
        cp.wait_recv()
    peaks = got[:, SIDE + 1:SIDE + 2, :]
    factor = jnp.exp(peaks - jnp.max(peaks, axis=0, keepdims=True))
    sums = jnp.sum(got[:, 0:MSG, :] * factor, axis=0)
    lane = lax.broadcasted_iota(jnp.int32, (1, 128), 1)
    outside = jnp.logical_or(jnp.logical_and(mp == 0, lane < 32), jnp.logical_and(mp == 15, lane >= 96))
    soft = jnp.where(outside, 0.0, sums[0:32] / jnp.where(outside, 1.0, sums[32:33]))
    taps = []
    for i in range(3):
        for j in range(3):
            offset = 32 * (i - 1) + (j - 1)
            tap = soft if offset == 0 else pltpu.roll(soft, (-offset) % 128, 1)
            if j == 0:
                tap = jnp.where(lane % 32 == 0, 0.0, tap)
            if j == 2:
                tap = jnp.where(lane % 32 == 31, 0.0, tap)
            taps.append(tap)
    square = lax.broadcasted_iota(jnp.int32, (32, 32), 0) == lax.broadcasted_iota(jnp.int32, (32, 32), 1)
    conv = jnp.sum(jnp.where(square, phi_b[...], 0.0), axis=1, keepdims=True)
    for i in range(3):
        for j in range(3):
            conv = conv + jnp.dot(
                phi[i, j], taps[3 * i + j], preferred_element_type=F32, precision=lax.Precision.HIGHEST
            )
    total = 0.5 * soft + 0.5 * conv
    out[0] = f_hat[0] + pltpu.roll(total, 96, 1)[:, 0:64]

    for cp in t + posts:
        cp.wait_send()
    for k in range(NCH):

        @pl.when(jnp.logical_not(same))
        def _():
            swap[k].wait_send()

        for cp in z1[k] + z2[k] + cross[k]:
            cp.wait_send()


NCH = 4
CR = 64 // NCH


def kernel(
    tok, ada, gate, up_w, up_b, down_w, down_b, ada_head, head_w, head_b, noise, book, phi, phi_b, f_hat, out, f_out,
    ffn_scratch, head_scratch, head_w_here, head_b_here, noise_here, load_s, far_s, far_r, panel_s, panel_r,
):
    ylo, x, yhi, z, core = position()
    dp, mp = lax.axis_index("dp"), lax.axis_index("mp")
    arrived = greet(
        [
            device(1 - ylo, x, yhi, z, core), device(1 - ylo, x, 1 - yhi, z, core),
            device(1 - ylo, x, 1 - yhi, z, 1 - core),
            device(ylo, (x + 1) % 4, yhi, z, core), device(ylo, (x + 3) % 4, yhi, z, core),
        ]
        + [(dp, (mp + o) % 16) for o in range(1, 16)]
    )
    far = (dp, (mp + 8) % 16)
    mine_rows = pl.ds(pl.multiple_of(yhi * 64, 64), 64)
    far_rows = pl.ds(pl.multiple_of((1 - yhi) * 64, 64), 64)
    loads = [
        pltpu.make_async_copy(head_w, head_w_here.at[0], load_s.at[0]),
        pltpu.make_async_copy(noise.at[:, mine_rows], noise_here.at[0], load_s.at[1]),
        pltpu.make_async_copy(head_b, head_b_here.at[0], load_s.at[2]),
    ]
    for cp in loads:
        cp.start()
    book_x = head_scratch[4]
    wide = jnp.concatenate([book[...].astype(F32), jnp.zeros((96, VB), F32)], axis=0)
    wide = jnp.where(lax.broadcasted_iota(jnp.int32, (128, VB), 0) == SIDE, 1.0, wide)
    book_x[0] = jnp.transpose(wide).astype(BF)
    def quarter(ref, index, first=0, count=HID):
        return ref.at[pl.ds(pl.multiple_of(index * HID + first, 16), count)]

    there = head_w_here.at[1]
    x_l, x_r = (x + 3) % 4, (x + 1) % 4
    ways = ((0, device(ylo, x_r, yhi, z, core), x_l), (1, device(ylo, x_l, yhi, z, core), x_r))
    ahead = [
        remote(quarter(head_w, x), quarter(there, x), far_s.at[0], far_r.at[0], far),
        [remote(quarter(there, x), quarter(there, x), panel_s.at[0, d], panel_r.at[0, d], to) for d, to, _ in ways],
        [
            remote(
                quarter(there, back, d * TH, TH), quarter(there, back, d * TH, TH),
                panel_s.at[1, d], panel_r.at[1, d], to,
            )
            for d, to, back in ways
        ],
        [
            remote(noise.at[:, far_rows], noise_here.at[1], far_s.at[1], far_r.at[1], far),
            remote(book_x.at[0], book_x.at[1], far_s.at[2], far_r.at[2], far),
            remote(head_b, head_b_here.at[1], far_s.at[3], far_r.at[3], far),
        ],
    ]
    ffn_part(arrived, ahead, tok, ada, gate, up_w, up_b, down_w, down_b, out, *ffn_scratch)
    for cp in loads:
        cp.wait()
    head_part(
        ahead, out, ada_head, head_w_here, head_b_here, noise_here, phi, phi_b, f_hat, f_out, *head_scratch
    )
    for cp in ahead[:1] + ahead[1] + ahead[2] + ahead[3]:
        cp.wait_send()


def deliver_kernel(rows, cells, rows_out, cells_out):
    rows_out[...] = rows[...]
    cells_out[...] = cells[...]


def deliver(rows, cells):
    vmem = pl.BlockSpec(memory_space=pltpu.VMEM)
    return pl.pallas_call(
        deliver_kernel,
        out_shape=tuple(jax.ShapeDtypeStruct(v.shape, v.dtype) for v in (rows, cells)),
        in_specs=[vmem] * 2,
        out_specs=(vmem, vmem),
        name="deliver",
    )(rows, cells)


def body(
    tokens, ada_ffn, ffn_gate, up_weight, up_bias, down_weight, down_bias, ada_head,
    head_weight, head_bias, gumbel_noise, codebook, phi_weight, phi_bias, f_hat,
):
    dma = pltpu.SemaphoreType.DMA
    widths = [UNITS[k][3] for k in CHUNKS]
    vmem, anywhere = pl.BlockSpec(memory_space=pltpu.VMEM), pl.BlockSpec(memory_space=pl.ANY)
    ffn_scratch = [
        pltpu.VMEM((4, ROWS, D), BF),
        pltpu.VMEM((4 * HID, D), BF),
        [pltpu.VMEM((4 * HID, w), BF) for w in widths],
        pltpu.VMEM((4, 1, HID), F32),
        pltpu.VMEM((1, 4 * HID), F32),
        pltpu.VMEM((1, D), F32),
        pltpu.VMEM((512, 4 * HID), BF),
        [pltpu.VMEM((4, ROWS, w), F32) for w in widths],
        [pltpu.VMEM((ROWS, w), BF) for w in widths],
        [pltpu.VMEM((2, 2, 64, w), BF) for w in widths],
        [pltpu.VMEM((2, 3, 64, w), BF) for w in widths],
        dma((4 + NC,)),
        dma((NU,)), dma((NU,)),
        dma((NU, 2)), dma((NU, 2)),
        dma((NU, 2)), dma((NU, 2)),
        dma((NU,)), dma((NU,)),
        dma((1 + NC,)), dma((1 + NC,)),
        dma((4,)), dma((4,)),
        dma((3,)), dma((3,)),
        dma((NC, 2, 2)), dma((NC, 2, 2)),
        dma((NC, 2)), dma((NC, 2)),
    ]
    head_scratch = [
        pltpu.VMEM((ROWS, D), BF),
        pltpu.VMEM((64, D), BF),
        pltpu.VMEM((64, D), BF),
        pltpu.VMEM((4, 2, 64, D), BF),
        pltpu.VMEM((2, VB, 128), BF),
        pltpu.VMEM((16, MSG, 128), F32),
        pltpu.VMEM((MSG, 1280), F32),
        pltpu.VMEM((16, MSG, 128), F32),
        dma((NCH,)), dma((NCH,)),
        dma((NCH,)), dma((NCH,)),
        dma((NCH,)),
        dma((NCH, 2)), dma((NCH, 2)),
        dma((NCH, 2)), dma((NCH, 2)),
        dma((NCH, 4)), dma((NCH, 4)),
        dma((16,)), dma((16,)),
    ]
    rows, cells = pl.pallas_call(
        kernel,
        out_shape=(jax.ShapeDtypeStruct((ROWS, D), BF), jax.ShapeDtypeStruct((1, 32, 64), F32)),
        in_specs=[vmem, vmem, vmem, anywhere, anywhere, anywhere, anywhere, vmem, anywhere, vmem, anywhere] + [vmem] * 4,
        out_specs=(vmem, vmem),
        scratch_shapes=[
            ffn_scratch,
            head_scratch,
            pltpu.VMEM((2, D, VB), BF),
            pltpu.VMEM((2, 1, VB), F32),
            pltpu.VMEM((2, 8, 64, VB), F32),
            dma((3,)),
            dma((4,)), dma((4,)),
            dma((2, 2)), dma((2, 2)),
        ],
        name="var_step",
        compiler_params=pltpu.CompilerParams(
            collective_id=1, has_side_effects=True, vmem_limit_bytes=60 * 1024 * 1024
        ),
    )(
        tokens, ada_ffn, ffn_gate, up_weight.T, up_bias, down_weight, down_bias,
        ada_head, head_weight, head_bias.reshape(1, -1), gumbel_noise.reshape(8, 128, VB), codebook.T,
        jnp.transpose(phi_weight, (2, 3, 0, 1)), phi_bias.reshape(1, -1), f_hat,
    )
    return deliver(rows, cells)


def solution(mesh):
    in_specs = (
        P(("dp", "mp"), None),
        P("dp", None, None),
        P("dp", None),
        P(None, "mp"),
        P("mp"),
        P("mp", None),
        P(),
        P("dp", None, None),
        P(None, "mp"),
        P("mp"),
        P("dp", None, "mp"),
        P("mp", None),
        P(),
        P(),
        P("dp", None, "mp"),
    )
    out_specs = (P(("dp", "mp"), None), P("dp", None, "mp"))
    return jax.shard_map(body, mesh=mesh, in_specs=in_specs, out_specs=out_specs, check_vma=False)
```

```python
import functools

import jax
import jax.numpy as jnp
from jax import lax
from jax.experimental import pallas as pl
from jax.experimental.pallas import tpu as pltpu
from jax.sharding import PartitionSpec as P

MESH = pl.DeviceIdType.MESH
BF = jnp.bfloat16
F32 = jnp.float32

D = 2304
ROWS = 128
HID = 576
FOREIGN = 2 * HID
DQ = HID // 4
TH = HID // 2
UNITS = (
    ("ring", "up", 0, 128),
    ("ring", "up", 128, 192),
    ("ring", "up", 320, 256),
    ("twin", "down", 0, 512),
    ("ring", "down", 512, 768),
    ("ring", "down", 1280, 512),
    ("twin", "down", 1792, 512),
)
PUSHED = (0, 1, 2, 3, 4, 5, 6)
NU = len(UNITS)
CHUNKS = tuple(k for k in range(NU) if UNITS[k][1] == "down")
NC = len(CHUNKS)
STEPS = (
    ("y", 0), ("a", 0), ("y", 1), ("b", 0), ("z", 1),
    ("y", 2), ("a", 1), ("z", 2), ("tile", 0), ("y", 3),
    ("tile", 1), ("tile", 2), ("a", 2), ("tile", 3), ("early", 0),
    ("early", 1), ("b", 1), ("early", 2), ("y", 4), ("early", 3),
    ("b", 2), ("a", 3), ("y", 5), ("late", 0), ("tile", 4),
    ("tile", 5), ("tile", 6), ("tile", 7), ("tile", 8), ("a", 4),
    ("first", 0), ("y", 6), ("a", 5), ("second", 0), ("b", 4),
    ("first", 1), ("b", 5), ("finish", 0), ("first", 2), ("a", 6),
    ("second", 1), ("first", 3), ("second", 2), ("panel", 0), ("finish", 1),
    ("second", 3), ("finish", 2), ("finish", 3), ("panel", 1),
)
NARROW = 256
FIRST = 1024
SIDE = 32
VB = 256
MSG = 40
GUIDE = 1.5


def position():
    dp, mp = lax.axis_index("dp"), lax.axis_index("mp")
    return dp // 4, dp % 4, mp // 8, (mp // 2) % 4, mp % 2


def device(ylo, x, yhi, z, core):
    return (ylo * 4 + x, yhi * 8 + z * 2 + core)


def remote(src, dst, send, recv, target):
    return pltpu.make_async_remote_copy(
        src_ref=src, dst_ref=dst, send_sem=send, recv_sem=recv, device_id=target, device_id_type=MESH
    )


def norm_rows(values):
    centred = values - jnp.mean(values, axis=-1, keepdims=True)
    spread = jnp.mean(centred * centred, axis=-1, keepdims=True)
    return centred * lax.rsqrt(spread + 1e-06)


def gelu(v):
    return 0.5 * v * (1.0 + jnp.tanh(0.7978845608028654 * (v + 0.044715 * v * v * v)))


def greet(targets):
    barrier = pltpu.get_barrier_semaphore()
    for target in targets:
        pl.semaphore_signal(barrier, inc=1, device_id=target, device_id_type=MESH)
    return lambda: pl.semaphore_wait(barrier, len(targets))


def ffn_part(
    arrived, ahead, tok, ada, gate, up_w, up_b, down_w, down_b, out,
    xn, up, dns, ub, bias_row, down_row, hid, parts, opps, nbrs, gots,
    loc_s, y_s, y_r, a_s, a_r, b_s, b_r, c_s, c_r, o_s, o_r, z_s, z_r, bias_s, bias_r,
    p_s, p_r, q_s, q_r,
):
    ylo, x, yhi, z, core = position()
    sib = device(ylo, x, yhi, z, 1 - core)
    partner = device(1 - ylo, x, 1 - yhi, z, core)
    partner_sib = device(1 - ylo, x, 1 - yhi, z, 1 - core)
    twin = device(1 - ylo, x, yhi, z, core)
    x_l, x_r = (x + 3) % 4, (x + 1) % 4
    xr, xl = device(ylo, x_r, yhi, z, core), device(ylo, x_l, yhi, z, core)
    zr_i, zl_i, zo_i = (z + 1) % 4, (z + 3) % 4, (z + 2) % 4
    zr, zl = device(ylo, x, yhi, zr_i, core), device(ylo, x, yhi, zl_i, core)

    own_rows, sib_rows = pl.ds(0, HID), pl.ds(HID, HID)

    def cols(j):
        return pl.ds(UNITS[CHUNKS[j]][2], UNITS[CHUNKS[j]][3])

    loc_up = pltpu.make_async_copy(up_w, up.at[own_rows], loc_s.at[0])
    loc_up.start()
    loc_dn = [
        pltpu.make_async_copy(down_w.at[:, cols(j)], dns[j].at[own_rows], loc_s.at[3 + j]) for j in range(NC)
    ]
    loc_bias = pltpu.make_async_copy(up_b, ub.at[0, 0], loc_s.at[2])
    loc_bias.start()
    loc_down = pltpu.make_async_copy(down_b, down_row.at[0], loc_s.at[3 + NC])
    loc_down.start()

    @pl.loop(0, ROWS // 16)
    def _(i):
        rows = pl.ds(pl.multiple_of(i * 16, 16), 16)
        pair = ada[yhi]
        v = norm_rows(tok[rows, :].astype(F32)) * (1.0 + pair[1:2, :]) + pair[0:1, :]
        xn[z, rows, :] = v.astype(BF)

    arrived()

    def part_of(k, count, index, foreign=True):
        way, panel, first, size = UNITS[k]
        base = FOREIGN if foreign else 0
        if panel == "up":
            rows = pl.ds(pl.multiple_of(base + first + index * (size // count), 16), size // count)
            return (up if foreign else up_w).at[rows]
        rows = pl.ds(pl.multiple_of(base + index * (HID // count), 16), HID // count)
        return dns[CHUNKS.index(k)].at[rows] if foreign else down_w.at[rows, pl.ds(first, size)]

    def half_of(k, index, half):
        way, panel, first, size = UNITS[k]
        if panel == "up":
            rows = pl.ds(pl.multiple_of(FOREIGN + first + index * (size // 4), 16), size // 4)
            return up.at[rows, pl.ds(half * (D // 2), D // 2)]
        rows = pl.ds(pl.multiple_of(FOREIGN + index * DQ, 16), DQ)
        return dns[CHUNKS.index(k)].at[rows, pl.ds(half * (size // 2), size // 2)]

    def whole(k, base):
        way, panel, first, size = UNITS[k]
        if panel == "up":
            return up.at[pl.ds(base + first, size)]
        return dns[CHUNKS.index(k)].at[pl.ds(base, HID)]

    y, a, b, c = [], [], [], []
    for k in range(NU):
        c.append(remote(whole(k, FOREIGN), whole(k, FOREIGN + HID), c_s.at[k], c_r.at[k], sib))
        if UNITS[k][0] == "ring":
            own = part_of(k, 4, x)
            y.append(remote(part_of(k, 4, x, False), own, y_s.at[k], y_r.at[k], partner))
            a.append([
                remote(own, own, a_s.at[k, 0], a_r.at[k, 0], xr), remote(own, own, a_s.at[k, 1], a_r.at[k, 1], xl)
            ])
            from_l, from_r = half_of(k, x_l, 0), half_of(k, x_r, 1)
            b.append([
                remote(from_l, from_l, b_s.at[k, 0], b_r.at[k, 0], xr),
                remote(from_r, from_r, b_s.at[k, 1], b_r.at[k, 1], xl),
            ])
        else:
            y.append(remote(
                part_of(k, 2, 1 - ylo, False), part_of(k, 2, 1 - ylo), y_s.at[k], y_r.at[k], partner
            ))
            own = part_of(k, 2, ylo)
            a.append([remote(own, own, a_s.at[k, 0], a_r.at[k, 0], twin)])
            b.append([])

    z1 = [
        remote(xn.at[z], xn.at[z], z_s.at[0], z_r.at[0], zr),
        remote(xn.at[z], xn.at[z], z_s.at[1], z_r.at[1], zl),
    ]
    z2 = [
        remote(xn.at[zl_i, pl.ds(0, 64)], xn.at[zl_i, pl.ds(0, 64)], z_s.at[2], z_r.at[2], zr),
        remote(xn.at[zr_i, pl.ds(64, 64)], xn.at[zr_i, pl.ds(64, 64)], z_s.at[3], z_r.at[3], zl),
    ]
    own_up = remote(up_w, up.at[sib_rows], o_s.at[0], o_r.at[0], sib)
    own_dn = [
        remote(down_w.at[:, cols(j)], dns[j].at[sib_rows], o_s.at[1 + j], o_r.at[1 + j], sib) for j in range(NC)
    ]
    biases = [
        remote(up_b, ub.at[1, 0], bias_s.at[0], bias_r.at[0], sib),
        remote(up_b, ub.at[2, 0], bias_s.at[1], bias_r.at[1], partner),
        remote(up_b, ub.at[3, 0], bias_s.at[2], bias_r.at[2], partner_sib),
    ]

    def start(*copies):
        for cp in copies:
            cp.start()

    def recv(*copies):
        for cp in copies:
            cp.wait_recv()

    def hidden(n):
        units = pl.ds(n * NARROW, NARROW)

        @pl.loop(0, 2)
        def _(m):
            rows = pl.ds(pl.multiple_of(m * 256, 256), 256)
            acc = lax.dot_general(
                xn[pl.ds(2 * m, 2)].reshape(256, D), up[units, :], (((1,), (1,)), ((), ())),
                preferred_element_type=F32,
            )
            hid[rows, units] = gelu(acc + bias_row[:, units]).astype(BF)

    def partial(j, late):
        units = pl.ds(FIRST, D - FIRST) if late else pl.ds(0, FIRST)
        width = UNITS[CHUNKS[j]][3]

        @pl.loop(0, 2)
        def _(m):
            rows = pl.ds(pl.multiple_of(m * 256, 256), 256)
            acc = jnp.dot(hid[rows, units], dns[j][units], preferred_element_type=F32).reshape(2, ROWS, width)
            if late:
                acc = acc + parts[j][pl.ds(2 * m, 2)]
            parts[j][pl.ds(2 * m, 2)] = acc

    low, high = pl.ds(0, 64), pl.ds(64, 64)

    p1 = [
        [
            remote(opps[j].at[low], gots[j].at[0, 0], p_s.at[j, 0, 0], p_r.at[j, 0, 0], zr),
            remote(opps[j].at[high], gots[j].at[1, 0], p_s.at[j, 1, 0], p_r.at[j, 1, 0], zl),
        ]
        for j in range(NC)
    ]
    ind = [
        [
            remote(nbrs[j].at[0, 0], gots[j].at[0, 1], p_s.at[j, 0, 1], p_r.at[j, 0, 1], zr),
            remote(nbrs[j].at[1, 0], gots[j].at[1, 1], p_s.at[j, 1, 1], p_r.at[j, 1, 1], zl),
        ]
        for j in range(NC)
    ]
    p2 = [
        [
            remote(nbrs[j].at[0, 1], gots[j].at[0, 2], q_s.at[j, 0], q_r.at[j, 0], zr),
            remote(nbrs[j].at[1, 1], gots[j].at[1, 2], q_s.at[j, 1], q_r.at[j, 1], zl),
        ]
        for j in range(NC)
    ]

    def reduce_first(j):
        recv(c[CHUNKS[j]])
        partial(j, True)
        opps[j][...] = parts[j][zo_i].astype(BF)
        start(*p1[j])
        nbrs[j][0, 0] = parts[j][zr_i, high].astype(BF)
        nbrs[j][1, 0] = parts[j][zl_i, low].astype(BF)
        start(*ind[j])

    def reduce_second(j):
        recv(*p1[j])
        nbrs[j][0, 1] = (parts[j][zr_i, low] + gots[j][0, 0].astype(F32)).astype(BF)
        nbrs[j][1, 1] = (parts[j][zl_i, high] + gots[j][1, 0].astype(F32)).astype(BF)
        start(*p2[j])

    def finish(j):
        recv(*ind[j], *p2[j])
        for rows, left, right in ((low, 2, 1), (high, 1, 2)):
            total = parts[j][z, rows] + gots[j][0, left].astype(F32) + gots[j][1, right].astype(F32)
            total = total + down_row[:, cols(j)]
            out[rows, cols(j)] = (
                tok[rows, cols(j)].astype(F32) + gate[pl.ds(yhi, 1), cols(j)] * total
            ).astype(BF)

    start(y[PUSHED[0]], *z1, *biases, own_up)
    for cp in loc_dn:
        cp.start()
    y[PUSHED[0]].wait_send()
    start(y[PUSHED[1]], y[PUSHED[2]])
    for op, k in STEPS:
        if op == "y":
            recv(y[k])
            start(*a[k])
            at = PUSHED.index(k)
            if 0 < at < NU - 2:
                start(y[PUSHED[at + 2]])
            if k == PUSHED[-1]:
                start(ahead[0], *ahead[3])
        elif op == "panel" and k == 0:
            recv(ahead[0])
            start(*ahead[1])
        elif op == "panel":
            recv(*ahead[1])
            start(*ahead[2])
        elif op == "a":
            recv(*a[k])
            start(*(b[k] if UNITS[k][0] == "ring" else [c[k]]))
        elif op == "b":
            recv(*b[k])
            start(c[k])
        elif op == "z" and k == 1:
            recv(*z1)
            start(*z2, *own_dn)
        elif op == "z":
            loc_bias.wait()
            loc_down.wait()
            recv(*biases)
            bias_row[...] = jnp.concatenate([ub[i] for i in range(4)], axis=1)
            loc_up.wait()
            recv(own_up, *z2)
        elif op == "early":
            loc_dn[k].wait()
            recv(own_dn[k])
            partial(k, False)
        elif op == "tile":
            hidden(k)
        elif op == "late":
            recv(*[c[i] for i in range(NU) if UNITS[i][1] == "up"])
        elif op == "first":
            reduce_first(k)
        elif op == "second":
            reduce_second(k)
        else:
            finish(k)

    y[PUSHED[0]] = None
    for cp in [v for v in y if v is not None] + c + z1 + z2 + [own_up] + own_dn + biases:
        cp.wait_send()
    for group in a + b + p1 + ind + p2:
        for cp in group:
            cp.wait_send()


def head_part(
    ahead, blk, ada, head_w, head_b, noise, phi, phi_b, f_hat, out,
    h, mine, theirs, g, book_x, stage, turned, got,
    t_s, t_r, y_s, y_r, l_s, z_s, z_r, w_s, w_r, c_s, c_r, m_s, m_r,
):
    ylo, x, yhi, z, core = position()
    dp, mp = lax.axis_index("dp"), lax.axis_index("mp")
    sib = device(ylo, x, yhi, z, 1 - core)
    twin = device(1 - ylo, x, yhi, z, core)
    partner = device(1 - ylo, x, 1 - yhi, z, core)
    zr_i, zl_i, zo_i = (z + 1) % 4, (z + 3) % 4, (z + 2) % 4
    zr, zl = device(ylo, x, yhi, zr_i, core), device(ylo, x, yhi, zl_i, core)
    lo = pl.multiple_of(ylo * 64, 64)
    other = pl.multiple_of((1 - ylo) * 64, 64)
    t = [
        remote(
            h.at[pl.ds(pl.multiple_of(other + k * CR, CR), CR)], theirs.at[pl.ds(k * CR, CR)],
            t_s.at[k], t_r.at[k], twin,
        )
        for k in range(NCH)
    ]
    pair = ada[yhi]

    def normalise(rows):
        v = norm_rows(blk[rows, :].astype(F32)) * (1.0 + pair[1:2, :]) + pair[0:1, :]
        h[rows, :] = v.astype(BF)

    for k in range(NCH):
        normalise(pl.ds(pl.multiple_of(other + k * CR, CR), CR))
        t[k].start()
    for k in range(NCH):
        normalise(pl.ds(pl.multiple_of(lo + k * CR, CR), CR))
    same = ylo == yhi
    own_weight = jnp.where(ylo == 0, 1.0 + GUIDE, -GUIDE)
    twin_weight = jnp.where(ylo == 0, -GUIDE, 1.0 + GUIDE)

    def slot(k, zi):
        return g.at[zi, core, pl.ds(k * CR, CR)]

    def slot_half(k, zi, half):
        return g.at[zi, core, pl.ds(k * CR, CR), pl.ds(half * (D // 2), D // 2)]

    def mixed(k):
        return mine.at[pl.ds(k * CR, CR)]

    swap = [remote(mixed(k), slot(k, z), y_s.at[k], y_r.at[k], partner) for k in range(NCH)]
    stay = [pltpu.make_async_copy(mixed(k), slot(k, z), l_s.at[k]) for k in range(NCH)]
    z1 = [
        [remote(slot(k, z), slot(k, z), z_s.at[k, d], z_r.at[k, d], to) for d, to in ((0, zr), (1, zl))]
        for k in range(NCH)
    ]
    z2 = [
        [
            remote(slot_half(k, zl_i, 0), slot_half(k, zl_i, 0), w_s.at[k, 0], w_r.at[k, 0], zr),
            remote(slot_half(k, zr_i, 1), slot_half(k, zr_i, 1), w_s.at[k, 1], w_r.at[k, 1], zl),
        ]
        for k in range(NCH)
    ]
    cross = [
        [remote(slot(k, zi), slot(k, zi), c_s.at[k, i], c_r.at[k, i], sib) for i, zi in enumerate((z, zr_i, zl_i, zo_i))]
        for k in range(NCH)
    ]

    def mix(k):
        t[k].wait_recv()
        rows = pl.ds(k * CR, CR)
        own = h[pl.ds(pl.multiple_of(lo + k * CR, CR), CR), :].astype(F32)
        mine[rows, :] = (own_weight * own + twin_weight * theirs[rows, :].astype(F32)).astype(BF)

        @pl.when(same)
        def _():
            stay[k].start()

        @pl.when(jnp.logical_not(same))
        def _():
            swap[k].start()

    def gathered(k):
        @pl.when(same)
        def _():
            stay[k].wait()

        @pl.when(jnp.logical_not(same))
        def _():
            swap[k].wait_recv()

        for cp in z1[k] + cross[k][:1]:
            cp.start()

    def second(k):
        for cp in z1[k]:
            cp.wait_recv()
        for cp in z2[k] + cross[k][1:3]:
            cp.start()

    def third(k):
        for cp in z2[k]:
            cp.wait_recv()
        cross[k][3].start()

    for k in range(NCH + 3):
        if k < NCH:
            mix(k)
        if 0 <= k - 1 < NCH:
            gathered(k - 1)
        if 0 <= k - 2 < NCH:
            second(k - 2)
        if 0 <= k - 3 < NCH:
            third(k - 3)
    for cp in ahead[2] + ahead[3]:
        cp.wait_recv()
    for k in range(NCH):
        for cp in cross[k]:
            cp.wait_recv()

    column = lax.broadcasted_iota(jnp.int32, (4, 64, 128), 2)
    nothing = jnp.where(column == SIDE + 1, -1e30, 0.0)

    @pl.loop(0, 2)
    def _(i):
        lhs = g[pl.ds(2 * i, 2)].reshape(256, D)
        scores = []
        for p in range(2):
            logits = jnp.dot(lhs, head_w[p], preferred_element_type=F32) + head_b[p]
            scores.append(logits + noise[p, pl.ds(4 * i, 4)].reshape(256, VB))
        peak = jnp.maximum(
            jnp.max(scores[0], axis=1, keepdims=True), jnp.max(scores[1], axis=1, keepdims=True)
        )
        code = jnp.zeros((256, 128), F32)
        for p in range(2):
            weights = jnp.exp(scores[p] - peak).astype(BF)
            code = code + jnp.dot(weights, book_x[p], preferred_element_type=F32)
        code = jnp.where(lax.broadcasted_iota(jnp.int32, code.shape, 1) == SIDE + 1, peak, code).reshape(4, 64, 128)
        spread = jnp.concatenate(
            [jnp.where(yhi == 0, code, nothing), jnp.where(yhi == 1, code, nothing)], axis=1
        ).reshape(512, 128)
        flipped = jnp.transpose(spread)
        turned[:, pl.ds(pl.multiple_of(128 + i * 512, 128), 512)] = flipped[0:MSG, :]

    zeros = jnp.zeros((MSG, 128), F32)
    turned[:, 0:128] = zeros
    turned[:, 1152:1280] = zeros
    cells = turned[...]
    for parity, shift in ((0, 96), (1, 32)):
        rolled = pltpu.roll(cells, 1280 - shift, 1)
        for i in range(8):
            to = 2 * i + parity
            start = (128 + 64 * to - 32 - shift)
            stage[to] = rolled[:, start:start + 128]

    posts = []
    for o in range(1, 16):
        to = (mp + o) % 16
        cp = remote(stage.at[to], got.at[o], m_s.at[o], m_r.at[o], (dp, to))
        cp.start()
        posts.append(cp)
    got[0] = stage[mp]
    for cp in posts:
        cp.wait_recv()
    peaks = got[:, SIDE + 1:SIDE + 2, :]
    factor = jnp.exp(peaks - jnp.max(peaks, axis=0, keepdims=True))
    sums = jnp.sum(got[:, 0:MSG, :] * factor, axis=0)
    lane = lax.broadcasted_iota(jnp.int32, (1, 128), 1)
    outside = jnp.logical_or(jnp.logical_and(mp == 0, lane < 32), jnp.logical_and(mp == 15, lane >= 96))
    soft = jnp.where(outside, 0.0, sums[0:32] / jnp.where(outside, 1.0, sums[32:33]))
    taps = []
    for i in range(3):
        for j in range(3):
            offset = 32 * (i - 1) + (j - 1)
            tap = soft if offset == 0 else pltpu.roll(soft, (-offset) % 128, 1)
            if j == 0:
                tap = jnp.where(lane % 32 == 0, 0.0, tap)
            if j == 2:
                tap = jnp.where(lane % 32 == 31, 0.0, tap)
            taps.append(tap)
    square = lax.broadcasted_iota(jnp.int32, (32, 32), 0) == lax.broadcasted_iota(jnp.int32, (32, 32), 1)
    conv = jnp.sum(jnp.where(square, phi_b[...], 0.0), axis=1, keepdims=True)
    for i in range(3):
        for j in range(3):
            conv = conv + jnp.dot(
                phi[i, j], taps[3 * i + j], preferred_element_type=F32, precision=lax.Precision.HIGHEST
            )
    total = 0.5 * soft + 0.5 * conv
    out[0] = f_hat[0] + pltpu.roll(total, 96, 1)[:, 0:64]

    for cp in t + posts:
        cp.wait_send()
    for k in range(NCH):

        @pl.when(jnp.logical_not(same))
        def _():
            swap[k].wait_send()

        for cp in z1[k] + z2[k] + cross[k]:
            cp.wait_send()


NCH = 4
CR = 64 // NCH


def kernel(
    tok, ada, gate, up_w, up_b, down_w, down_b, ada_head, head_w, head_b, noise, book, phi, phi_b, f_hat, out, f_out,
    ffn_scratch, head_scratch, head_w_here, head_b_here, noise_here, load_s, far_s, far_r, panel_s, panel_r,
):
    ylo, x, yhi, z, core = position()
    dp, mp = lax.axis_index("dp"), lax.axis_index("mp")
    arrived = greet(
        [
            device(1 - ylo, x, yhi, z, core), device(1 - ylo, x, 1 - yhi, z, core),
            device(1 - ylo, x, 1 - yhi, z, 1 - core),
            device(ylo, (x + 1) % 4, yhi, z, core), device(ylo, (x + 3) % 4, yhi, z, core),
        ]
        + [(dp, (mp + o) % 16) for o in range(1, 16)]
    )
    far = (dp, (mp + 8) % 16)
    mine_rows = pl.ds(pl.multiple_of(yhi * 64, 64), 64)
    far_rows = pl.ds(pl.multiple_of((1 - yhi) * 64, 64), 64)
    loads = [
        pltpu.make_async_copy(head_w, head_w_here.at[0], load_s.at[0]),
        pltpu.make_async_copy(noise.at[:, mine_rows], noise_here.at[0], load_s.at[1]),
        pltpu.make_async_copy(head_b, head_b_here.at[0], load_s.at[2]),
    ]
    for cp in loads:
        cp.start()
    book_x = head_scratch[4]
    wide = jnp.concatenate([book[...].astype(F32), jnp.zeros((96, VB), F32)], axis=0)
    wide = jnp.where(lax.broadcasted_iota(jnp.int32, (128, VB), 0) == SIDE, 1.0, wide)
    book_x[0] = jnp.transpose(wide).astype(BF)
    def quarter(ref, index, first=0, count=HID):
        return ref.at[pl.ds(pl.multiple_of(index * HID + first, 16), count)]

    there = head_w_here.at[1]
    x_l, x_r = (x + 3) % 4, (x + 1) % 4
    ways = ((0, device(ylo, x_r, yhi, z, core), x_l), (1, device(ylo, x_l, yhi, z, core), x_r))
    ahead = [
        remote(quarter(head_w, x), quarter(there, x), far_s.at[0], far_r.at[0], far),
        [remote(quarter(there, x), quarter(there, x), panel_s.at[0, d], panel_r.at[0, d], to) for d, to, _ in ways],
        [
            remote(
                quarter(there, back, d * TH, TH), quarter(there, back, d * TH, TH),
                panel_s.at[1, d], panel_r.at[1, d], to,
            )
            for d, to, back in ways
        ],
        [
            remote(noise.at[:, far_rows], noise_here.at[1], far_s.at[1], far_r.at[1], far),
            remote(book_x.at[0], book_x.at[1], far_s.at[2], far_r.at[2], far),
            remote(head_b, head_b_here.at[1], far_s.at[3], far_r.at[3], far),
        ],
    ]
    ffn_part(arrived, ahead, tok, ada, gate, up_w, up_b, down_w, down_b, out, *ffn_scratch)
    for cp in loads:
        cp.wait()
    head_part(
        ahead, out, ada_head, head_w_here, head_b_here, noise_here, phi, phi_b, f_hat, f_out, *head_scratch
    )
    for cp in ahead[:1] + ahead[1] + ahead[2] + ahead[3]:
        cp.wait_send()


def deliver_kernel(rows, cells, rows_out, cells_out):
    rows_out[...] = rows[...]
    cells_out[...] = cells[...]


def deliver(rows, cells):
    vmem = pl.BlockSpec(memory_space=pltpu.VMEM)
    return pl.pallas_call(
        deliver_kernel,
        out_shape=tuple(jax.ShapeDtypeStruct(v.shape, v.dtype) for v in (rows, cells)),
        in_specs=[vmem] * 2,
        out_specs=(vmem, vmem),
        name="deliver",
    )(rows, cells)


def body(
    tokens, ada_ffn, ffn_gate, up_weight, up_bias, down_weight, down_bias, ada_head,
    head_weight, head_bias, gumbel_noise, codebook, phi_weight, phi_bias, f_hat,
):
    dma = pltpu.SemaphoreType.DMA
    widths = [UNITS[k][3] for k in CHUNKS]
    vmem, anywhere = pl.BlockSpec(memory_space=pltpu.VMEM), pl.BlockSpec(memory_space=pl.ANY)
    ffn_scratch = [
        pltpu.VMEM((4, ROWS, D), BF),
        pltpu.VMEM((4 * HID, D), BF),
        [pltpu.VMEM((4 * HID, w), BF) for w in widths],
        pltpu.VMEM((4, 1, HID), F32),
        pltpu.VMEM((1, 4 * HID), F32),
        pltpu.VMEM((1, D), F32),
        pltpu.VMEM((512, 4 * HID), BF),
        [pltpu.VMEM((4, ROWS, w), F32) for w in widths],
        [pltpu.VMEM((ROWS, w), BF) for w in widths],
        [pltpu.VMEM((2, 2, 64, w), BF) for w in widths],
        [pltpu.VMEM((2, 3, 64, w), BF) for w in widths],
        dma((4 + NC,)),
        dma((NU,)), dma((NU,)),
        dma((NU, 2)), dma((NU, 2)),
        dma((NU, 2)), dma((NU, 2)),
        dma((NU,)), dma((NU,)),
        dma((1 + NC,)), dma((1 + NC,)),
        dma((4,)), dma((4,)),
        dma((3,)), dma((3,)),
        dma((NC, 2, 2)), dma((NC, 2, 2)),
        dma((NC, 2)), dma((NC, 2)),
    ]
    head_scratch = [
        pltpu.VMEM((ROWS, D), BF),
        pltpu.VMEM((64, D), BF),
        pltpu.VMEM((64, D), BF),
        pltpu.VMEM((4, 2, 64, D), BF),
        pltpu.VMEM((2, VB, 128), BF),
        pltpu.VMEM((16, MSG, 128), F32),
        pltpu.VMEM((MSG, 1280), F32),
        pltpu.VMEM((16, MSG, 128), F32),
        dma((NCH,)), dma((NCH,)),
        dma((NCH,)), dma((NCH,)),
        dma((NCH,)),
        dma((NCH, 2)), dma((NCH, 2)),
        dma((NCH, 2)), dma((NCH, 2)),
        dma((NCH, 4)), dma((NCH, 4)),
        dma((16,)), dma((16,)),
    ]
    rows, cells = pl.pallas_call(
        kernel,
        out_shape=(jax.ShapeDtypeStruct((ROWS, D), BF), jax.ShapeDtypeStruct((1, 32, 64), F32)),
        in_specs=[vmem, vmem, vmem, anywhere, anywhere, anywhere, anywhere, vmem, anywhere, vmem, anywhere] + [vmem] * 4,
        out_specs=(vmem, vmem),
        scratch_shapes=[
            ffn_scratch,
            head_scratch,
            pltpu.VMEM((2, D, VB), BF),
            pltpu.VMEM((2, 1, VB), F32),
            pltpu.VMEM((2, 8, 64, VB), F32),
            dma((3,)),
            dma((4,)), dma((4,)),
            dma((2, 2)), dma((2, 2)),
        ],
        name="var_step",
        compiler_params=pltpu.CompilerParams(
            collective_id=1, has_side_effects=True, vmem_limit_bytes=60 * 1024 * 1024
        ),
    )(
        tokens, ada_ffn, ffn_gate, up_weight.T, up_bias, down_weight, down_bias,
        ada_head, head_weight, head_bias.reshape(1, -1), gumbel_noise.reshape(8, 128, VB), codebook.T,
        jnp.transpose(phi_weight, (2, 3, 0, 1)), phi_bias.reshape(1, -1), f_hat,
    )
    return deliver(rows, cells)


def solution(mesh):
    in_specs = (
        P(("dp", "mp"), None),
        P("dp", None, None),
        P("dp", None),
        P(None, "mp"),
        P("mp"),
        P("mp", None),
        P(),
        P("dp", None, None),
        P(None, "mp"),
        P("mp"),
        P("dp", None, "mp"),
        P("mp", None),
        P(),
        P(),
        P("dp", None, "mp"),
    )
    out_specs = (P(("dp", "mp"), None), P("dp", None, "mp"))
    return jax.shard_map(body, mesh=mesh, in_specs=in_specs, out_specs=out_specs, check_vma=False)
```

```python
import functools

import jax
import jax.numpy as jnp
from jax import lax
from jax.experimental import pallas as pl
from jax.experimental.pallas import tpu as pltpu
from jax.sharding import PartitionSpec as P

MESH = pl.DeviceIdType.MESH
BF = jnp.bfloat16
F32 = jnp.float32

D = 2304
ROWS = 128
HID = 576
FOREIGN = 2 * HID
DQ = HID // 4
TH = HID // 2
UNITS = (
    ("ring", "up", 0, 128),
    ("ring", "up", 128, 192),
    ("ring", "up", 320, 256),
    ("twin", "down", 0, 512),
    ("ring", "down", 512, 768),
    ("ring", "down", 1280, 512),
    ("twin", "down", 1792, 512),
)
PUSHED = (0, 1, 2, 3, 4, 5, 6)
NU = len(UNITS)
CHUNKS = tuple(k for k in range(NU) if UNITS[k][1] == "down")
NC = len(CHUNKS)
STEPS = (
    ("y", 0), ("a", 0), ("y", 1), ("b", 0), ("z", 1),
    ("y", 2), ("a", 1), ("z", 2), ("tile", 0), ("y", 3),
    ("tile", 1), ("tile", 2), ("a", 2), ("tile", 3), ("early", 0),
    ("early", 1), ("b", 1), ("early", 2), ("y", 4), ("early", 3),
    ("b", 2), ("a", 3), ("y", 5), ("late", 0), ("tile", 4),
    ("tile", 5), ("tile", 6), ("tile", 7), ("tile", 8), ("a", 4),
    ("first", 0), ("y", 6), ("a", 5), ("second", 0), ("b", 4),
    ("first", 1), ("b", 5), ("finish", 0), ("first", 2), ("a", 6),
    ("second", 1), ("first", 3), ("second", 2), ("panel", 0), ("finish", 1),
    ("second", 3), ("finish", 2), ("finish", 3), ("panel", 1),
)
NARROW = 256
FIRST = 1024
SIDE = 32
VB = 256
MSG = 40
GUIDE = 1.5


def position():
    dp, mp = lax.axis_index("dp"), lax.axis_index("mp")
    return dp // 4, dp % 4, mp // 8, (mp // 2) % 4, mp % 2


def device(ylo, x, yhi, z, core):
    return (ylo * 4 + x, yhi * 8 + z * 2 + core)


def remote(src, dst, send, recv, target):
    return pltpu.make_async_remote_copy(
        src_ref=src, dst_ref=dst, send_sem=send, recv_sem=recv, device_id=target, device_id_type=MESH
    )


def norm_rows(values):
    centred = values - jnp.mean(values, axis=-1, keepdims=True)
    spread = jnp.mean(centred * centred, axis=-1, keepdims=True)
    return centred * lax.rsqrt(spread + 1e-06)


def gelu(v):
    return 0.5 * v * (1.0 + jnp.tanh(0.7978845608028654 * (v + 0.044715 * v * v * v)))


def greet(targets):
    barrier = pltpu.get_barrier_semaphore()
    for target in targets:
        pl.semaphore_signal(barrier, inc=1, device_id=target, device_id_type=MESH)
    return lambda: pl.semaphore_wait(barrier, len(targets))


def ffn_part(
    arrived, ahead, tok, ada, gate, up_w, up_b, down_w, down_b, out,
    xn, up, dns, ub, bias_row, down_row, hid, parts, opps, nbrs, gots,
    loc_s, y_s, y_r, a_s, a_r, b_s, b_r, c_s, c_r, o_s, o_r, z_s, z_r, bias_s, bias_r,
    p_s, p_r, q_s, q_r,
):
    ylo, x, yhi, z, core = position()
    sib = device(ylo, x, yhi, z, 1 - core)
    partner = device(1 - ylo, x, 1 - yhi, z, core)
    partner_sib = device(1 - ylo, x, 1 - yhi, z, 1 - core)
    twin = device(1 - ylo, x, yhi, z, core)
    x_l, x_r = (x + 3) % 4, (x + 1) % 4
    xr, xl = device(ylo, x_r, yhi, z, core), device(ylo, x_l, yhi, z, core)
    zr_i, zl_i, zo_i = (z + 1) % 4, (z + 3) % 4, (z + 2) % 4
    zr, zl = device(ylo, x, yhi, zr_i, core), device(ylo, x, yhi, zl_i, core)

    own_rows, sib_rows = pl.ds(0, HID), pl.ds(HID, HID)

    def cols(j):
        return pl.ds(UNITS[CHUNKS[j]][2], UNITS[CHUNKS[j]][3])

    loc_up = pltpu.make_async_copy(up_w, up.at[own_rows], loc_s.at[0])
    loc_up.start()
    loc_dn = [
        pltpu.make_async_copy(down_w.at[:, cols(j)], dns[j].at[own_rows], loc_s.at[3 + j]) for j in range(NC)
    ]
    loc_bias = pltpu.make_async_copy(up_b, ub.at[0, 0], loc_s.at[2])
    loc_bias.start()
    loc_down = pltpu.make_async_copy(down_b, down_row.at[0], loc_s.at[3 + NC])
    loc_down.start()

    @pl.loop(0, ROWS // 16)
    def _(i):
        rows = pl.ds(pl.multiple_of(i * 16, 16), 16)
        pair = ada[yhi]
        v = norm_rows(tok[rows, :].astype(F32)) * (1.0 + pair[1:2, :]) + pair[0:1, :]
        xn[z, rows, :] = v.astype(BF)

    arrived()

    def part_of(k, count, index, foreign=True):
        way, panel, first, size = UNITS[k]
        base = FOREIGN if foreign else 0
        if panel == "up":
            rows = pl.ds(pl.multiple_of(base + first + index * (size // count), 16), size // count)
            return (up if foreign else up_w).at[rows]
        rows = pl.ds(pl.multiple_of(base + index * (HID // count), 16), HID // count)
        return dns[CHUNKS.index(k)].at[rows] if foreign else down_w.at[rows, pl.ds(first, size)]

    def half_of(k, index, half):
        way, panel, first, size = UNITS[k]
        if panel == "up":
            rows = pl.ds(pl.multiple_of(FOREIGN + first + index * (size // 4), 16), size // 4)
            return up.at[rows, pl.ds(half * (D // 2), D // 2)]
        rows = pl.ds(pl.multiple_of(FOREIGN + index * DQ, 16), DQ)
        return dns[CHUNKS.index(k)].at[rows, pl.ds(half * (size // 2), size // 2)]

    def whole(k, base):
        way, panel, first, size = UNITS[k]
        if panel == "up":
            return up.at[pl.ds(base + first, size)]
        return dns[CHUNKS.index(k)].at[pl.ds(base, HID)]

    y, a, b, c = [], [], [], []
    for k in range(NU):
        c.append(remote(whole(k, FOREIGN), whole(k, FOREIGN + HID), c_s.at[k], c_r.at[k], sib))
        if UNITS[k][0] == "ring":
            own = part_of(k, 4, x)
            y.append(remote(part_of(k, 4, x, False), own, y_s.at[k], y_r.at[k], partner))
            a.append([
                remote(own, own, a_s.at[k, 0], a_r.at[k, 0], xr), remote(own, own, a_s.at[k, 1], a_r.at[k, 1], xl)
            ])
            from_l, from_r = half_of(k, x_l, 0), half_of(k, x_r, 1)
            b.append([
                remote(from_l, from_l, b_s.at[k, 0], b_r.at[k, 0], xr),
                remote(from_r, from_r, b_s.at[k, 1], b_r.at[k, 1], xl),
            ])
        else:
            y.append(remote(
                part_of(k, 2, 1 - ylo, False), part_of(k, 2, 1 - ylo), y_s.at[k], y_r.at[k], partner
            ))
            own = part_of(k, 2, ylo)
            a.append([remote(own, own, a_s.at[k, 0], a_r.at[k, 0], twin)])
            b.append([])

    z1 = [
        remote(xn.at[z], xn.at[z], z_s.at[0], z_r.at[0], zr),
        remote(xn.at[z], xn.at[z], z_s.at[1], z_r.at[1], zl),
    ]
    z2 = [
        remote(xn.at[zl_i, pl.ds(0, 64)], xn.at[zl_i, pl.ds(0, 64)], z_s.at[2], z_r.at[2], zr),
        remote(xn.at[zr_i, pl.ds(64, 64)], xn.at[zr_i, pl.ds(64, 64)], z_s.at[3], z_r.at[3], zl),
    ]
    own_up = remote(up_w, up.at[sib_rows], o_s.at[0], o_r.at[0], sib)
    own_dn = [
        remote(down_w.at[:, cols(j)], dns[j].at[sib_rows], o_s.at[1 + j], o_r.at[1 + j], sib) for j in range(NC)
    ]
    biases = [
        remote(up_b, ub.at[1, 0], bias_s.at[0], bias_r.at[0], sib),
        remote(up_b, ub.at[2, 0], bias_s.at[1], bias_r.at[1], partner),
        remote(up_b, ub.at[3, 0], bias_s.at[2], bias_r.at[2], partner_sib),
    ]

    def start(*copies):
        for cp in copies:
            cp.start()

    def recv(*copies):
        for cp in copies:
            cp.wait_recv()

    def hidden(n):
        units = pl.ds(n * NARROW, NARROW)

        @pl.loop(0, 2)
        def _(m):
            rows = pl.ds(pl.multiple_of(m * 256, 256), 256)
            acc = lax.dot_general(
                xn[pl.ds(2 * m, 2)].reshape(256, D), up[units, :], (((1,), (1,)), ((), ())),
                preferred_element_type=F32,
            )
            hid[rows, units] = gelu(acc + bias_row[:, units]).astype(BF)

    def partial(j, late):
        units = pl.ds(FIRST, D - FIRST) if late else pl.ds(0, FIRST)
        width = UNITS[CHUNKS[j]][3]

        @pl.loop(0, 2)
        def _(m):
            rows = pl.ds(pl.multiple_of(m * 256, 256), 256)
            acc = jnp.dot(hid[rows, units], dns[j][units], preferred_element_type=F32).reshape(2, ROWS, width)
            if late:
                acc = acc + parts[j][pl.ds(2 * m, 2)]
            parts[j][pl.ds(2 * m, 2)] = acc

    low, high = pl.ds(0, 64), pl.ds(64, 64)

    p1 = [
        [
            remote(opps[j].at[low], gots[j].at[0, 0], p_s.at[j, 0, 0], p_r.at[j, 0, 0], zr),
            remote(opps[j].at[high], gots[j].at[1, 0], p_s.at[j, 1, 0], p_r.at[j, 1, 0], zl),
        ]
        for j in range(NC)
    ]
    ind = [
        [
            remote(nbrs[j].at[0, 0], gots[j].at[0, 1], p_s.at[j, 0, 1], p_r.at[j, 0, 1], zr),
            remote(nbrs[j].at[1, 0], gots[j].at[1, 1], p_s.at[j, 1, 1], p_r.at[j, 1, 1], zl),
        ]
        for j in range(NC)
    ]
    p2 = [
        [
            remote(nbrs[j].at[0, 1], gots[j].at[0, 2], q_s.at[j, 0], q_r.at[j, 0], zr),
            remote(nbrs[j].at[1, 1], gots[j].at[1, 2], q_s.at[j, 1], q_r.at[j, 1], zl),
        ]
        for j in range(NC)
    ]

    def reduce_first(j):
        recv(c[CHUNKS[j]])
        partial(j, True)
        opps[j][...] = parts[j][zo_i].astype(BF)
        start(*p1[j])
        nbrs[j][0, 0] = parts[j][zr_i, high].astype(BF)
        nbrs[j][1, 0] = parts[j][zl_i, low].astype(BF)
        start(*ind[j])

    def reduce_second(j):
        recv(*p1[j])
        nbrs[j][0, 1] = (parts[j][zr_i, low] + gots[j][0, 0].astype(F32)).astype(BF)
        nbrs[j][1, 1] = (parts[j][zl_i, high] + gots[j][1, 0].astype(F32)).astype(BF)
        start(*p2[j])

    def finish(j):
        recv(*ind[j], *p2[j])
        for rows, left, right in ((low, 2, 1), (high, 1, 2)):
            total = parts[j][z, rows] + gots[j][0, left].astype(F32) + gots[j][1, right].astype(F32)
            total = total + down_row[:, cols(j)]
            out[rows, cols(j)] = (
                tok[rows, cols(j)].astype(F32) + gate[pl.ds(yhi, 1), cols(j)] * total
            ).astype(BF)

    start(y[PUSHED[0]], *z1, *biases, own_up)
    for cp in loc_dn:
        cp.start()
    y[PUSHED[0]].wait_send()
    start(y[PUSHED[1]], y[PUSHED[2]])
    for op, k in STEPS:
        if op == "y":
            recv(y[k])
            start(*a[k])
            at = PUSHED.index(k)
            if 0 < at < NU - 2:
                start(y[PUSHED[at + 2]])
            if k == PUSHED[-1]:
                start(ahead[0], *ahead[3])
        elif op == "panel" and k == 0:
            recv(ahead[0])
            start(*ahead[1])
        elif op == "panel":
            recv(*ahead[1])
            start(*ahead[2])
        elif op == "a":
            recv(*a[k])
            start(*(b[k] if UNITS[k][0] == "ring" else [c[k]]))
        elif op == "b":
            recv(*b[k])
            start(c[k])
        elif op == "z" and k == 1:
            recv(*z1)
            start(*z2, *own_dn)
        elif op == "z":
            loc_bias.wait()
            loc_down.wait()
            recv(*biases)
            bias_row[...] = jnp.concatenate([ub[i] for i in range(4)], axis=1)
            loc_up.wait()
            recv(own_up, *z2)
        elif op == "early":
            loc_dn[k].wait()
            recv(own_dn[k])
            partial(k, False)
        elif op == "tile":
            hidden(k)
        elif op == "late":
            recv(*[c[i] for i in range(NU) if UNITS[i][1] == "up"])
        elif op == "first":
            reduce_first(k)
        elif op == "second":
            reduce_second(k)
        else:
            finish(k)

    y[PUSHED[0]] = None
    for cp in [v for v in y if v is not None] + c + z1 + z2 + [own_up] + own_dn + biases:
        cp.wait_send()
    for group in a + b + p1 + ind + p2:
        for cp in group:
            cp.wait_send()


def head_part(
    ahead, blk, ada, head_w, head_b, noise, phi, phi_b, f_hat, out,
    h, mine, theirs, g, book_x, stage, turned, got,
    t_s, t_r, y_s, y_r, l_s, z_s, z_r, w_s, w_r, c_s, c_r, m_s, m_r,
):
    ylo, x, yhi, z, core = position()
    dp, mp = lax.axis_index("dp"), lax.axis_index("mp")
    sib = device(ylo, x, yhi, z, 1 - core)
    twin = device(1 - ylo, x, yhi, z, core)
    partner = device(1 - ylo, x, 1 - yhi, z, core)
    zr_i, zl_i, zo_i = (z + 1) % 4, (z + 3) % 4, (z + 2) % 4
    zr, zl = device(ylo, x, yhi, zr_i, core), device(ylo, x, yhi, zl_i, core)
    lo = pl.multiple_of(ylo * 64, 64)
    other = pl.multiple_of((1 - ylo) * 64, 64)
    t = [
        remote(
            h.at[pl.ds(pl.multiple_of(other + k * CR, CR), CR)], theirs.at[pl.ds(k * CR, CR)],
            t_s.at[k], t_r.at[k], twin,
        )
        for k in range(NCH)
    ]
    pair = ada[yhi]

    for first in (other, lo):
        rows = pl.ds(first, 64)
        v = norm_rows(blk[rows, :].astype(F32)) * (1.0 + pair[1:2, :]) + pair[0:1, :]
        h[rows, :] = v.astype(BF)
        if first is other:
            for cp in t:
                cp.start()
    same = ylo == yhi
    own_weight = jnp.where(ylo == 0, 1.0 + GUIDE, -GUIDE)
    twin_weight = jnp.where(ylo == 0, -GUIDE, 1.0 + GUIDE)

    def slot(k, zi):
        return g.at[zi, core, pl.ds(k * CR, CR)]

    def slot_half(k, zi, half):
        return g.at[zi, core, pl.ds(k * CR, CR), pl.ds(half * (D // 2), D // 2)]

    def mixed(k):
        return mine.at[pl.ds(k * CR, CR)]

    swap = [remote(mixed(k), slot(k, z), y_s.at[k], y_r.at[k], partner) for k in range(NCH)]
    stay = [pltpu.make_async_copy(mixed(k), slot(k, z), l_s.at[k]) for k in range(NCH)]
    z1 = [
        [remote(slot(k, z), slot(k, z), z_s.at[k, d], z_r.at[k, d], to) for d, to in ((0, zr), (1, zl))]
        for k in range(NCH)
    ]
    z2 = [
        [
            remote(slot_half(k, zl_i, 0), slot_half(k, zl_i, 0), w_s.at[k, 0], w_r.at[k, 0], zr),
            remote(slot_half(k, zr_i, 1), slot_half(k, zr_i, 1), w_s.at[k, 1], w_r.at[k, 1], zl),
        ]
        for k in range(NCH)
    ]
    cross = [
        [remote(slot(k, zi), slot(k, zi), c_s.at[k, i], c_r.at[k, i], sib) for i, zi in enumerate((z, zr_i, zl_i, zo_i))]
        for k in range(NCH)
    ]

    def mix(k):
        t[k].wait_recv()
        rows = pl.ds(k * CR, CR)
        own = h[pl.ds(pl.multiple_of(lo + k * CR, CR), CR), :].astype(F32)
        mine[rows, :] = (own_weight * own + twin_weight * theirs[rows, :].astype(F32)).astype(BF)

        @pl.when(same)
        def _():
            stay[k].start()

        @pl.when(jnp.logical_not(same))
        def _():
            swap[k].start()

    def gathered(k):
        @pl.when(same)
        def _():
            stay[k].wait()

        @pl.when(jnp.logical_not(same))
        def _():
            swap[k].wait_recv()

        for cp in z1[k] + cross[k][:1]:
            cp.start()

    def second(k):
        for cp in z1[k]:
            cp.wait_recv()
        for cp in z2[k] + cross[k][1:3]:
            cp.start()

    def third(k):
        for cp in z2[k]:
            cp.wait_recv()
        cross[k][3].start()

    for k in range(NCH + 3):
        if k < NCH:
            mix(k)
        if 0 <= k - 1 < NCH:
            gathered(k - 1)
        if 0 <= k - 2 < NCH:
            second(k - 2)
        if 0 <= k - 3 < NCH - 1:
            third(k - 3)
    for cp in ahead[2] + ahead[3]:
        cp.wait_recv()
    for k in range(NCH):
        for cp in cross[k][:3]:
            cp.wait_recv()

    column = lax.broadcasted_iota(jnp.int32, (4, 64, 128), 2)
    nothing = jnp.where(column == SIDE + 1, -1e30, 0.0)

    def sample(i):
        lhs = g[pl.ds(2 * i, 2)].reshape(256, D)
        scores = []
        for p in range(2):
            logits = jnp.dot(lhs, head_w[p], preferred_element_type=F32) + head_b[p]
            scores.append(logits + noise[p, pl.ds(4 * i, 4)].reshape(256, VB))
        peak = jnp.maximum(
            jnp.max(scores[0], axis=1, keepdims=True), jnp.max(scores[1], axis=1, keepdims=True)
        )
        code = jnp.zeros((256, 128), F32)
        for p in range(2):
            weights = jnp.exp(scores[p] - peak).astype(BF)
            code = code + jnp.dot(weights, book_x[p], preferred_element_type=F32)
        code = jnp.where(lax.broadcasted_iota(jnp.int32, code.shape, 1) == SIDE + 1, peak, code).reshape(4, 64, 128)
        spread = jnp.concatenate(
            [jnp.where(yhi == 0, code, nothing), jnp.where(yhi == 1, code, nothing)], axis=1
        ).reshape(512, 128)
        flipped = jnp.transpose(spread)
        turned[:, pl.ds(pl.multiple_of(128 + i * 512, 128), 512)] = flipped[0:MSG, :]

    sample(z // 2)
    third(NCH - 1)
    for k in range(NCH):
        cross[k][3].wait_recv()
    sample(1 - z // 2)

    zeros = jnp.zeros((MSG, 128), F32)
    turned[:, 0:128] = zeros
    turned[:, 1152:1280] = zeros
    cells = turned[...]
    for parity, shift in ((0, 96), (1, 32)):
        rolled = pltpu.roll(cells, 1280 - shift, 1)
        for i in range(8):
            to = 2 * i + parity
            start = (128 + 64 * to - 32 - shift)
            stage[to] = rolled[:, start:start + 128]

    posts = []
    for o in range(1, 16):
        to = (mp + o) % 16
        cp = remote(stage.at[to], got.at[o], m_s.at[o], m_r.at[o], (dp, to))
        cp.start()
        posts.append(cp)
    got[0] = stage[mp]
    for cp in posts:
        cp.wait_recv()
    peaks = got[:, SIDE + 1:SIDE + 2, :]
    factor = jnp.exp(peaks - jnp.max(peaks, axis=0, keepdims=True))
    sums = jnp.sum(got[:, 0:MSG, :] * factor, axis=0)
    lane = lax.broadcasted_iota(jnp.int32, (1, 128), 1)
    outside = jnp.logical_or(jnp.logical_and(mp == 0, lane < 32), jnp.logical_and(mp == 15, lane >= 96))
    soft = jnp.where(outside, 0.0, sums[0:32] / jnp.where(outside, 1.0, sums[32:33]))
    taps = []
    for i in range(3):
        for j in range(3):
            offset = 32 * (i - 1) + (j - 1)
            tap = soft if offset == 0 else pltpu.roll(soft, (-offset) % 128, 1)
            if j == 0:
                tap = jnp.where(lane % 32 == 0, 0.0, tap)
            if j == 2:
                tap = jnp.where(lane % 32 == 31, 0.0, tap)
            taps.append(tap)
    square = lax.broadcasted_iota(jnp.int32, (32, 32), 0) == lax.broadcasted_iota(jnp.int32, (32, 32), 1)
    conv = jnp.sum(jnp.where(square, phi_b[...], 0.0), axis=1, keepdims=True) + jnp.dot(
        phi[...], jnp.concatenate(taps, axis=0), preferred_element_type=F32, precision=lax.Precision.HIGHEST
    )
    total = 0.5 * soft + 0.5 * conv
    out[0] = f_hat[0] + pltpu.roll(total, 96, 1)[:, 0:64]

    for cp in t + posts:
        cp.wait_send()
    for k in range(NCH):

        @pl.when(jnp.logical_not(same))
        def _():
            swap[k].wait_send()

        for cp in z1[k] + z2[k] + cross[k]:
            cp.wait_send()


NCH = 4
CR = 64 // NCH


def kernel(
    tok, ada, gate, up_w, up_b, down_w, down_b, ada_head, head_w, head_b, noise, book, phi, phi_b, f_hat, out, f_out,
    ffn_scratch, head_scratch, head_w_here, head_b_here, noise_here, load_s, far_s, far_r, panel_s, panel_r, phi_flat,
):
    ylo, x, yhi, z, core = position()
    dp, mp = lax.axis_index("dp"), lax.axis_index("mp")
    arrived = greet(
        [
            device(1 - ylo, x, yhi, z, core), device(1 - ylo, x, 1 - yhi, z, core),
            device(1 - ylo, x, 1 - yhi, z, 1 - core),
            device(ylo, (x + 1) % 4, yhi, z, core), device(ylo, (x + 3) % 4, yhi, z, core),
        ]
        + [(dp, (mp + o) % 16) for o in range(1, 16)]
    )
    far = (dp, (mp + 8) % 16)
    mine_rows = pl.ds(pl.multiple_of(yhi * 64, 64), 64)
    far_rows = pl.ds(pl.multiple_of((1 - yhi) * 64, 64), 64)
    loads = [
        pltpu.make_async_copy(head_w, head_w_here.at[0], load_s.at[0]),
        pltpu.make_async_copy(noise.at[:, mine_rows], noise_here.at[0], load_s.at[1]),
        pltpu.make_async_copy(head_b, head_b_here.at[0], load_s.at[2]),
    ]
    for cp in loads:
        cp.start()
    phi_flat[...] = jnp.concatenate([phi[i, j] for i in range(3) for j in range(3)], axis=1)
    book_x = head_scratch[4]
    wide = jnp.concatenate([book[...].astype(F32), jnp.zeros((96, VB), F32)], axis=0)
    wide = jnp.where(lax.broadcasted_iota(jnp.int32, (128, VB), 0) == SIDE, 1.0, wide)
    book_x[0] = jnp.transpose(wide).astype(BF)
    def quarter(ref, index, first=0, count=HID):
        return ref.at[pl.ds(pl.multiple_of(index * HID + first, 16), count)]

    there = head_w_here.at[1]
    x_l, x_r = (x + 3) % 4, (x + 1) % 4
    ways = ((0, device(ylo, x_r, yhi, z, core), x_l), (1, device(ylo, x_l, yhi, z, core), x_r))
    ahead = [
        remote(quarter(head_w, x), quarter(there, x), far_s.at[0], far_r.at[0], far),
        [remote(quarter(there, x), quarter(there, x), panel_s.at[0, d], panel_r.at[0, d], to) for d, to, _ in ways],
        [
            remote(
                quarter(there, back, d * TH, TH), quarter(there, back, d * TH, TH),
                panel_s.at[1, d], panel_r.at[1, d], to,
            )
            for d, to, back in ways
        ],
        [
            remote(noise.at[:, far_rows], noise_here.at[1], far_s.at[1], far_r.at[1], far),
            remote(book_x.at[0], book_x.at[1], far_s.at[2], far_r.at[2], far),
            remote(head_b, head_b_here.at[1], far_s.at[3], far_r.at[3], far),
        ],
    ]
    ffn_part(arrived, ahead, tok, ada, gate, up_w, up_b, down_w, down_b, out, *ffn_scratch)
    for cp in loads:
        cp.wait()
    head_part(
        ahead, out, ada_head, head_w_here, head_b_here, noise_here, phi_flat, phi_b, f_hat, f_out, *head_scratch
    )
    for cp in ahead[:1] + ahead[1] + ahead[2] + ahead[3]:
        cp.wait_send()


def deliver_kernel(rows, cells, rows_out, cells_out):
    rows_out[...] = rows[...]
    cells_out[...] = cells[...]


def deliver(rows, cells):
    vmem = pl.BlockSpec(memory_space=pltpu.VMEM)
    return pl.pallas_call(
        deliver_kernel,
        out_shape=tuple(jax.ShapeDtypeStruct(v.shape, v.dtype) for v in (rows, cells)),
        in_specs=[vmem] * 2,
        out_specs=(vmem, vmem),
        name="deliver",
    )(rows, cells)


def body(
    tokens, ada_ffn, ffn_gate, up_weight, up_bias, down_weight, down_bias, ada_head,
    head_weight, head_bias, gumbel_noise, codebook, phi_weight, phi_bias, f_hat,
):
    dma = pltpu.SemaphoreType.DMA
    widths = [UNITS[k][3] for k in CHUNKS]
    vmem, anywhere = pl.BlockSpec(memory_space=pltpu.VMEM), pl.BlockSpec(memory_space=pl.ANY)
    ffn_scratch = [
        pltpu.VMEM((4, ROWS, D), BF),
        pltpu.VMEM((4 * HID, D), BF),
        [pltpu.VMEM((4 * HID, w), BF) for w in widths],
        pltpu.VMEM((4, 1, HID), F32),
        pltpu.VMEM((1, 4 * HID), F32),
        pltpu.VMEM((1, D), F32),
        pltpu.VMEM((512, 4 * HID), BF),
        [pltpu.VMEM((4, ROWS, w), F32) for w in widths],
        [pltpu.VMEM((ROWS, w), BF) for w in widths],
        [pltpu.VMEM((2, 2, 64, w), BF) for w in widths],
        [pltpu.VMEM((2, 3, 64, w), BF) for w in widths],
        dma((4 + NC,)),
        dma((NU,)), dma((NU,)),
        dma((NU, 2)), dma((NU, 2)),
        dma((NU, 2)), dma((NU, 2)),
        dma((NU,)), dma((NU,)),
        dma((1 + NC,)), dma((1 + NC,)),
        dma((4,)), dma((4,)),
        dma((3,)), dma((3,)),
        dma((NC, 2, 2)), dma((NC, 2, 2)),
        dma((NC, 2)), dma((NC, 2)),
    ]
    head_scratch = [
        pltpu.VMEM((ROWS, D), BF),
        pltpu.VMEM((64, D), BF),
        pltpu.VMEM((64, D), BF),
        pltpu.VMEM((4, 2, 64, D), BF),
        pltpu.VMEM((2, VB, 128), BF),
        pltpu.VMEM((16, MSG, 128), F32),
        pltpu.VMEM((MSG, 1280), F32),
        pltpu.VMEM((16, MSG, 128), F32),
        dma((NCH,)), dma((NCH,)),
        dma((NCH,)), dma((NCH,)),
        dma((NCH,)),
        dma((NCH, 2)), dma((NCH, 2)),
        dma((NCH, 2)), dma((NCH, 2)),
        dma((NCH, 4)), dma((NCH, 4)),
        dma((16,)), dma((16,)),
    ]
    rows, cells = pl.pallas_call(
        kernel,
        out_shape=(jax.ShapeDtypeStruct((ROWS, D), BF), jax.ShapeDtypeStruct((1, 32, 64), F32)),
        in_specs=[vmem, vmem, vmem, anywhere, anywhere, anywhere, anywhere, vmem, anywhere, vmem, anywhere] + [vmem] * 4,
        out_specs=(vmem, vmem),
        scratch_shapes=[
            ffn_scratch,
            head_scratch,
            pltpu.VMEM((2, D, VB), BF),
            pltpu.VMEM((2, 1, VB), F32),
            pltpu.VMEM((2, 8, 64, VB), F32),
            dma((3,)),
            dma((4,)), dma((4,)),
            dma((2, 2)), dma((2, 2)),
            pltpu.VMEM((32, 288), F32),
        ],
        name="var_step",
        compiler_params=pltpu.CompilerParams(
            collective_id=1, has_side_effects=True, vmem_limit_bytes=60 * 1024 * 1024
        ),
    )(
        tokens, ada_ffn, ffn_gate, up_weight.T, up_bias, down_weight, down_bias,
        ada_head, head_weight, head_bias.reshape(1, -1), gumbel_noise.reshape(8, 128, VB), codebook.T,
        jnp.transpose(phi_weight, (2, 3, 0, 1)), phi_bias.reshape(1, -1), f_hat,
    )
    return deliver(rows, cells)


def solution(mesh):
    in_specs = (
        P(("dp", "mp"), None),
        P("dp", None, None),
        P("dp", None),
        P(None, "mp"),
        P("mp"),
        P("mp", None),
        P(),
        P("dp", None, None),
        P(None, "mp"),
        P("mp"),
        P("dp", None, "mp"),
        P("mp", None),
        P(),
        P(),
        P("dp", None, "mp"),
    )
    out_specs = (P(("dp", "mp"), None), P("dp", None, "mp"))
    return jax.shard_map(body, mesh=mesh, in_specs=in_specs, out_specs=out_specs, check_vma=False)
```

```python
import functools

import jax
import jax.numpy as jnp
from jax import lax
from jax.experimental import pallas as pl
from jax.experimental.pallas import tpu as pltpu
from jax.sharding import PartitionSpec as P

MESH = pl.DeviceIdType.MESH
BF = jnp.bfloat16
F32 = jnp.float32

D = 2304
ROWS = 128
HID = 576
FOREIGN = 2 * HID
DQ = HID // 4
TH = HID // 2
UNITS = (
    ("ring", "up", 0, 128),
    ("ring", "up", 128, 192),
    ("ring", "up", 320, 256),
    ("twin", "down", 0, 512),
    ("ring", "down", 512, 768),
    ("ring", "down", 1280, 512),
    ("twin", "down", 1792, 512),
)
PUSHED = (0, 1, 2, 3, 4, 5, 6)
NU = len(UNITS)
CHUNKS = tuple(k for k in range(NU) if UNITS[k][1] == "down")
NC = len(CHUNKS)
STEPS = (
    ("y", 0), ("a", 0), ("y", 1), ("b", 0), ("z", 1),
    ("y", 2), ("a", 1), ("z", 2), ("tile", 0), ("y", 3),
    ("tile", 1), ("tile", 2), ("a", 2), ("tile", 3), ("early", 0),
    ("early", 1), ("b", 1), ("early", 2), ("y", 4), ("early", 3),
    ("b", 2), ("a", 3), ("y", 5), ("late", 0), ("tile", 4),
    ("tile", 5), ("tile", 6), ("tile", 7), ("tile", 8), ("a", 4),
    ("first", 0), ("y", 6), ("a", 5), ("second", 0), ("b", 4),
    ("first", 1), ("b", 5), ("finish", 0), ("first", 2), ("a", 6),
    ("second", 1), ("first", 3), ("second", 2), ("panel", 0), ("finish", 1),
    ("second", 3), ("finish", 2), ("finish", 3), ("panel", 1),
)
NARROW = 256
FIRST = 1024
SIDE = 32
VB = 256
MSG = 40
GUIDE = 1.5


def position():
    dp, mp = lax.axis_index("dp"), lax.axis_index("mp")
    return dp // 4, dp % 4, mp // 8, (mp // 2) % 4, mp % 2


def device(ylo, x, yhi, z, core):
    return (ylo * 4 + x, yhi * 8 + z * 2 + core)


def remote(src, dst, send, recv, target):
    return pltpu.make_async_remote_copy(
        src_ref=src, dst_ref=dst, send_sem=send, recv_sem=recv, device_id=target, device_id_type=MESH
    )


def norm_rows(values):
    centred = values - jnp.mean(values, axis=-1, keepdims=True)
    spread = jnp.mean(centred * centred, axis=-1, keepdims=True)
    return centred * lax.rsqrt(spread + 1e-06)


def gelu(v):
    return 0.5 * v * (1.0 + jnp.tanh(0.7978845608028654 * (v + 0.044715 * v * v * v)))


def greet(targets):
    barrier = pltpu.get_barrier_semaphore()
    for target in targets:
        pl.semaphore_signal(barrier, inc=1, device_id=target, device_id_type=MESH)
    return lambda: pl.semaphore_wait(barrier, len(targets))


def ffn_part(
    arrived, prepare, ahead, tok, ada, gate, up_w, up_b, down_w, down_b, out,
    xn, up, dns, ub, bias_row, down_row, hid, parts, opps, nbrs, gots,
    loc_s, y_s, y_r, a_s, a_r, b_s, b_r, c_s, c_r, o_s, o_r, z_s, z_r, bias_s, bias_r,
    p_s, p_r, q_s, q_r,
):
    ylo, x, yhi, z, core = position()
    sib = device(ylo, x, yhi, z, 1 - core)
    partner = device(1 - ylo, x, 1 - yhi, z, core)
    partner_sib = device(1 - ylo, x, 1 - yhi, z, 1 - core)
    twin = device(1 - ylo, x, yhi, z, core)
    x_l, x_r = (x + 3) % 4, (x + 1) % 4
    xr, xl = device(ylo, x_r, yhi, z, core), device(ylo, x_l, yhi, z, core)
    zr_i, zl_i, zo_i = (z + 1) % 4, (z + 3) % 4, (z + 2) % 4
    zr, zl = device(ylo, x, yhi, zr_i, core), device(ylo, x, yhi, zl_i, core)

    own_rows, sib_rows = pl.ds(0, HID), pl.ds(HID, HID)

    def cols(j):
        return pl.ds(UNITS[CHUNKS[j]][2], UNITS[CHUNKS[j]][3])

    loc_up = pltpu.make_async_copy(up_w, up.at[own_rows], loc_s.at[0])
    loc_up.start()
    loc_dn = [
        pltpu.make_async_copy(down_w.at[:, cols(j)], dns[j].at[own_rows], loc_s.at[3 + j]) for j in range(NC)
    ]
    loc_bias = pltpu.make_async_copy(up_b, ub.at[0, 0], loc_s.at[2])
    loc_bias.start()
    loc_down = pltpu.make_async_copy(down_b, down_row.at[0], loc_s.at[3 + NC])
    loc_down.start()

    arrived()

    def part_of(k, count, index, foreign=True):
        way, panel, first, size = UNITS[k]
        base = FOREIGN if foreign else 0
        if panel == "up":
            rows = pl.ds(pl.multiple_of(base + first + index * (size // count), 16), size // count)
            return (up if foreign else up_w).at[rows]
        rows = pl.ds(pl.multiple_of(base + index * (HID // count), 16), HID // count)
        return dns[CHUNKS.index(k)].at[rows] if foreign else down_w.at[rows, pl.ds(first, size)]

    def half_of(k, index, half):
        way, panel, first, size = UNITS[k]
        if panel == "up":
            rows = pl.ds(pl.multiple_of(FOREIGN + first + index * (size // 4), 16), size // 4)
            return up.at[rows, pl.ds(half * (D // 2), D // 2)]
        rows = pl.ds(pl.multiple_of(FOREIGN + index * DQ, 16), DQ)
        return dns[CHUNKS.index(k)].at[rows, pl.ds(half * (size // 2), size // 2)]

    def whole(k, base):
        way, panel, first, size = UNITS[k]
        if panel == "up":
            return up.at[pl.ds(base + first, size)]
        return dns[CHUNKS.index(k)].at[pl.ds(base, HID)]

    y, a, b, c = [], [], [], []
    for k in range(NU):
        c.append(remote(whole(k, FOREIGN), whole(k, FOREIGN + HID), c_s.at[k], c_r.at[k], sib))
        if UNITS[k][0] == "ring":
            own = part_of(k, 4, x)
            y.append(remote(part_of(k, 4, x, False), own, y_s.at[k], y_r.at[k], partner))
            a.append([
                remote(own, own, a_s.at[k, 0], a_r.at[k, 0], xr), remote(own, own, a_s.at[k, 1], a_r.at[k, 1], xl)
            ])
            from_l, from_r = half_of(k, x_l, 0), half_of(k, x_r, 1)
            b.append([
                remote(from_l, from_l, b_s.at[k, 0], b_r.at[k, 0], xr),
                remote(from_r, from_r, b_s.at[k, 1], b_r.at[k, 1], xl),
            ])
        else:
            y.append(remote(
                part_of(k, 2, 1 - ylo, False), part_of(k, 2, 1 - ylo), y_s.at[k], y_r.at[k], partner
            ))
            own = part_of(k, 2, ylo)
            a.append([remote(own, own, a_s.at[k, 0], a_r.at[k, 0], twin)])
            b.append([])

    z1 = [
        remote(xn.at[z], xn.at[z], z_s.at[0], z_r.at[0], zr),
        remote(xn.at[z], xn.at[z], z_s.at[1], z_r.at[1], zl),
    ]
    z2 = [
        remote(xn.at[zl_i, pl.ds(0, 64)], xn.at[zl_i, pl.ds(0, 64)], z_s.at[2], z_r.at[2], zr),
        remote(xn.at[zr_i, pl.ds(64, 64)], xn.at[zr_i, pl.ds(64, 64)], z_s.at[3], z_r.at[3], zl),
    ]
    own_up = remote(up_w, up.at[sib_rows], o_s.at[0], o_r.at[0], sib)
    own_dn = [
        remote(down_w.at[:, cols(j)], dns[j].at[sib_rows], o_s.at[1 + j], o_r.at[1 + j], sib) for j in range(NC)
    ]
    biases = [
        remote(up_b, ub.at[1, 0], bias_s.at[0], bias_r.at[0], sib),
        remote(up_b, ub.at[2, 0], bias_s.at[1], bias_r.at[1], partner),
        remote(up_b, ub.at[3, 0], bias_s.at[2], bias_r.at[2], partner_sib),
    ]

    def start(*copies):
        for cp in copies:
            cp.start()

    def recv(*copies):
        for cp in copies:
            cp.wait_recv()

    def hidden(n):
        units = pl.ds(n * NARROW, NARROW)

        @pl.loop(0, 2)
        def _(m):
            rows = pl.ds(pl.multiple_of(m * 256, 256), 256)
            acc = lax.dot_general(
                xn[pl.ds(2 * m, 2)].reshape(256, D), up[units, :], (((1,), (1,)), ((), ())),
                preferred_element_type=F32,
            )
            hid[rows, units] = gelu(acc + bias_row[:, units]).astype(BF)

    def partial(j, late):
        units = pl.ds(FIRST, D - FIRST) if late else pl.ds(0, FIRST)
        width = UNITS[CHUNKS[j]][3]

        @pl.loop(0, 2)
        def _(m):
            rows = pl.ds(pl.multiple_of(m * 256, 256), 256)
            acc = jnp.dot(hid[rows, units], dns[j][units], preferred_element_type=F32).reshape(2, ROWS, width)
            if late:
                acc = acc + parts[j][pl.ds(2 * m, 2)]
            parts[j][pl.ds(2 * m, 2)] = acc

    low, high = pl.ds(0, 64), pl.ds(64, 64)

    p1 = [
        [
            remote(opps[j].at[low], gots[j].at[0, 0], p_s.at[j, 0, 0], p_r.at[j, 0, 0], zr),
            remote(opps[j].at[high], gots[j].at[1, 0], p_s.at[j, 1, 0], p_r.at[j, 1, 0], zl),
        ]
        for j in range(NC)
    ]
    ind = [
        [
            remote(nbrs[j].at[0, 0], gots[j].at[0, 1], p_s.at[j, 0, 1], p_r.at[j, 0, 1], zr),
            remote(nbrs[j].at[1, 0], gots[j].at[1, 1], p_s.at[j, 1, 1], p_r.at[j, 1, 1], zl),
        ]
        for j in range(NC)
    ]
    p2 = [
        [
            remote(nbrs[j].at[0, 1], gots[j].at[0, 2], q_s.at[j, 0], q_r.at[j, 0], zr),
            remote(nbrs[j].at[1, 1], gots[j].at[1, 2], q_s.at[j, 1], q_r.at[j, 1], zl),
        ]
        for j in range(NC)
    ]

    def reduce_first(j):
        recv(c[CHUNKS[j]])
        partial(j, True)
        opps[j][...] = parts[j][zo_i].astype(BF)
        start(*p1[j])
        nbrs[j][0, 0] = parts[j][zr_i, high].astype(BF)
        nbrs[j][1, 0] = parts[j][zl_i, low].astype(BF)
        start(*ind[j])

    def reduce_second(j):
        recv(*p1[j])
        nbrs[j][0, 1] = (parts[j][zr_i, low] + gots[j][0, 0].astype(F32)).astype(BF)
        nbrs[j][1, 1] = (parts[j][zl_i, high] + gots[j][1, 0].astype(F32)).astype(BF)
        start(*p2[j])

    def finish(j):
        recv(*ind[j], *p2[j])
        for rows, left, right in ((low, 2, 1), (high, 1, 2)):
            total = parts[j][z, rows] + gots[j][0, left].astype(F32) + gots[j][1, right].astype(F32)
            total = total + down_row[:, cols(j)]
            out[rows, cols(j)] = (
                tok[rows, cols(j)].astype(F32) + gate[pl.ds(yhi, 1), cols(j)] * total
            ).astype(BF)

    start(y[PUSHED[0]])
    pair = ada[yhi]
    for rows in (low, high):
        v = norm_rows(tok[rows, :].astype(F32)) * (1.0 + pair[1:2, :]) + pair[0:1, :]
        xn[z, rows, :] = v.astype(BF)
    start(*z1, *biases, own_up)
    for cp in loc_dn:
        cp.start()
    y[PUSHED[0]].wait_send()
    start(y[PUSHED[1]], y[PUSHED[2]])
    for op, k in STEPS:
        if op == "y":
            recv(y[k])
            start(*a[k])
            at = PUSHED.index(k)
            if 0 < at < NU - 2:
                start(y[PUSHED[at + 2]])
            if k == PUSHED[-1]:
                start(ahead[0], *ahead[3])
        elif op == "panel" and k == 0:
            recv(ahead[0])
            start(*ahead[1])
        elif op == "panel":
            recv(*ahead[1])
            start(*ahead[2])
        elif op == "a":
            recv(*a[k])
            start(*(b[k] if UNITS[k][0] == "ring" else [c[k]]))
        elif op == "b":
            recv(*b[k])
            start(c[k])
        elif op == "z" and k == 1:
            recv(*z1)
            start(*z2, *own_dn)
            prepare()
        elif op == "z":
            loc_bias.wait()
            loc_down.wait()
            recv(*biases)
            bias_row[...] = jnp.concatenate([ub[i] for i in range(4)], axis=1)
            loc_up.wait()
            recv(own_up, *z2)
        elif op == "early":
            loc_dn[k].wait()
            recv(own_dn[k])
            partial(k, False)
        elif op == "tile":
            hidden(k)
        elif op == "late":
            recv(*[c[i] for i in range(NU) if UNITS[i][1] == "up"])
        elif op == "first":
            reduce_first(k)
        elif op == "second":
            reduce_second(k)
        else:
            finish(k)

    y[PUSHED[0]] = None
    for cp in [v for v in y if v is not None] + c + z1 + z2 + [own_up] + own_dn + biases:
        cp.wait_send()
    for group in a + b + p1 + ind + p2:
        for cp in group:
            cp.wait_send()


def head_part(
    ahead, blk, ada, head_w, head_b, noise, phi, phi_b, f_hat, out,
    h, mine, theirs, g, book_x, stage, turned, got,
    t_s, t_r, y_s, y_r, l_s, z_s, z_r, w_s, w_r, c_s, c_r, m_s, m_r,
):
    ylo, x, yhi, z, core = position()
    dp, mp = lax.axis_index("dp"), lax.axis_index("mp")
    sib = device(ylo, x, yhi, z, 1 - core)
    twin = device(1 - ylo, x, yhi, z, core)
    partner = device(1 - ylo, x, 1 - yhi, z, core)
    zr_i, zl_i, zo_i = (z + 1) % 4, (z + 3) % 4, (z + 2) % 4
    zr, zl = device(ylo, x, yhi, zr_i, core), device(ylo, x, yhi, zl_i, core)
    lo = pl.multiple_of(ylo * 64, 64)
    other = pl.multiple_of((1 - ylo) * 64, 64)
    t = [
        remote(
            h.at[pl.ds(pl.multiple_of(other + k * CR, CR), CR)], theirs.at[pl.ds(k * CR, CR)],
            t_s.at[k], t_r.at[k], twin,
        )
        for k in range(NCH)
    ]
    pair = ada[yhi]

    for first in (other, lo):
        rows = pl.ds(first, 64)
        v = norm_rows(blk[rows, :].astype(F32)) * (1.0 + pair[1:2, :]) + pair[0:1, :]
        h[rows, :] = v.astype(BF)
        if first is other:
            for cp in t:
                cp.start()
    same = ylo == yhi
    own_weight = jnp.where(ylo == 0, 1.0 + GUIDE, -GUIDE)
    twin_weight = jnp.where(ylo == 0, -GUIDE, 1.0 + GUIDE)

    def slot(k, zi):
        return g.at[zi, core, pl.ds(k * CR, CR)]

    def slot_half(k, zi, half):
        return g.at[zi, core, pl.ds(k * CR, CR), pl.ds(half * (D // 2), D // 2)]

    def mixed(k):
        return mine.at[pl.ds(k * CR, CR)]

    swap = [remote(mixed(k), slot(k, z), y_s.at[k], y_r.at[k], partner) for k in range(NCH)]
    stay = [pltpu.make_async_copy(mixed(k), slot(k, z), l_s.at[k]) for k in range(NCH)]
    z1 = [
        [remote(slot(k, z), slot(k, z), z_s.at[k, d], z_r.at[k, d], to) for d, to in ((0, zr), (1, zl))]
        for k in range(NCH)
    ]
    z2 = [
        [
            remote(slot_half(k, zl_i, 0), slot_half(k, zl_i, 0), w_s.at[k, 0], w_r.at[k, 0], zr),
            remote(slot_half(k, zr_i, 1), slot_half(k, zr_i, 1), w_s.at[k, 1], w_r.at[k, 1], zl),
        ]
        for k in range(NCH)
    ]
    cross = [
        [remote(slot(k, zi), slot(k, zi), c_s.at[k, i], c_r.at[k, i], sib) for i, zi in enumerate((z, zr_i, zl_i, zo_i))]
        for k in range(NCH)
    ]

    def mix(k):
        t[k].wait_recv()
        rows = pl.ds(k * CR, CR)
        own = h[pl.ds(pl.multiple_of(lo + k * CR, CR), CR), :].astype(F32)
        mine[rows, :] = (own_weight * own + twin_weight * theirs[rows, :].astype(F32)).astype(BF)

        @pl.when(same)
        def _():
            stay[k].start()

        @pl.when(jnp.logical_not(same))
        def _():
            swap[k].start()

    def gathered(k):
        @pl.when(same)
        def _():
            stay[k].wait()

        @pl.when(jnp.logical_not(same))
        def _():
            swap[k].wait_recv()

        for cp in z1[k] + cross[k][:1]:
            cp.start()

    def second(k):
        for cp in z1[k]:
            cp.wait_recv()
        for cp in z2[k] + cross[k][1:3]:
            cp.start()

    def third(k):
        for cp in z2[k]:
            cp.wait_recv()
        cross[k][3].start()

    for k in range(NCH + 3):
        if k < NCH:
            mix(k)
        if 0 <= k - 1 < NCH:
            gathered(k - 1)
        if 0 <= k - 2 < NCH:
            second(k - 2)
        if 0 <= k - 3 < NCH - 1:
            third(k - 3)
    for cp in ahead[2] + ahead[3]:
        cp.wait_recv()
    for k in range(NCH):
        for cp in cross[k][:3]:
            cp.wait_recv()

    column = lax.broadcasted_iota(jnp.int32, (4, 64, 128), 2)
    nothing = jnp.where(column == SIDE + 1, -1e30, 0.0)

    def sample(i):
        lhs = g[pl.ds(2 * i, 2)].reshape(256, D)
        scores = []
        for p in range(2):
            logits = jnp.dot(lhs, head_w[p], preferred_element_type=F32) + head_b[p]
            scores.append(logits + noise[p, pl.ds(4 * i, 4)].reshape(256, VB))
        peak = jnp.maximum(
            jnp.max(scores[0], axis=1, keepdims=True), jnp.max(scores[1], axis=1, keepdims=True)
        )
        code = jnp.zeros((256, 128), F32)
        for p in range(2):
            weights = jnp.exp(scores[p] - peak).astype(BF)
            code = code + jnp.dot(weights, book_x[p], preferred_element_type=F32)
        code = jnp.where(lax.broadcasted_iota(jnp.int32, code.shape, 1) == SIDE + 1, peak, code).reshape(4, 64, 128)
        spread = jnp.concatenate(
            [jnp.where(yhi == 0, code, nothing), jnp.where(yhi == 1, code, nothing)], axis=1
        ).reshape(512, 128)
        flipped = jnp.transpose(spread)
        turned[:, pl.ds(pl.multiple_of(128 + i * 512, 128), 512)] = flipped[0:MSG, :]

    sample(z // 2)
    third(NCH - 1)
    for k in range(NCH):
        cross[k][3].wait_recv()
    sample(1 - z // 2)

    zeros = jnp.zeros((MSG, 128), F32)
    turned[:, 0:128] = zeros
    turned[:, 1152:1280] = zeros
    cells = turned[...]
    for parity, shift in ((0, 96), (1, 32)):
        rolled = pltpu.roll(cells, 1280 - shift, 1)
        for i in range(8):
            to = 2 * i + parity
            start = (128 + 64 * to - 32 - shift)
            stage[to] = rolled[:, start:start + 128]

    posts = []
    for o in range(1, 16):
        to = (mp + o) % 16
        cp = remote(stage.at[to], got.at[o], m_s.at[o], m_r.at[o], (dp, to))
        cp.start()
        posts.append(cp)
    got[0] = stage[mp]
    for cp in posts:
        cp.wait_recv()
    peaks = got[:, SIDE + 1:SIDE + 2, :]
    factor = jnp.exp(peaks - jnp.max(peaks, axis=0, keepdims=True))
    sums = jnp.sum(got[:, 0:MSG, :] * factor, axis=0)
    lane = lax.broadcasted_iota(jnp.int32, (1, 128), 1)
    outside = jnp.logical_or(jnp.logical_and(mp == 0, lane < 32), jnp.logical_and(mp == 15, lane >= 96))
    soft = jnp.where(outside, 0.0, sums[0:32] / jnp.where(outside, 1.0, sums[32:33]))
    taps = []
    for i in range(3):
        for j in range(3):
            offset = 32 * (i - 1) + (j - 1)
            tap = soft if offset == 0 else pltpu.roll(soft, (-offset) % 128, 1)
            if j == 0:
                tap = jnp.where(lane % 32 == 0, 0.0, tap)
            if j == 2:
                tap = jnp.where(lane % 32 == 31, 0.0, tap)
            taps.append(tap)
    square = lax.broadcasted_iota(jnp.int32, (32, 32), 0) == lax.broadcasted_iota(jnp.int32, (32, 32), 1)
    conv = jnp.sum(jnp.where(square, phi_b[...], 0.0), axis=1, keepdims=True) + jnp.dot(
        phi[...], jnp.concatenate(taps, axis=0), preferred_element_type=F32, precision=lax.Precision.HIGHEST
    )
    total = 0.5 * soft + 0.5 * conv
    out[0] = f_hat[0] + pltpu.roll(total, 96, 1)[:, 0:64]

    for cp in t + posts:
        cp.wait_send()
    for k in range(NCH):

        @pl.when(jnp.logical_not(same))
        def _():
            swap[k].wait_send()

        for cp in z1[k] + z2[k] + cross[k]:
            cp.wait_send()


NCH = 4
CR = 64 // NCH


def kernel(
    tok, ada, gate, up_w, up_b, down_w, down_b, ada_head, head_w, head_b, noise, book, phi, phi_b, f_hat, out, f_out,
    ffn_scratch, head_scratch, head_w_here, head_b_here, noise_here, load_s, far_s, far_r, panel_s, panel_r, phi_flat,
):
    ylo, x, yhi, z, core = position()
    dp, mp = lax.axis_index("dp"), lax.axis_index("mp")
    arrived = greet(
        [
            device(1 - ylo, x, yhi, z, core), device(1 - ylo, x, 1 - yhi, z, core),
            device(1 - ylo, x, 1 - yhi, z, 1 - core),
            device(ylo, (x + 1) % 4, yhi, z, core), device(ylo, (x + 3) % 4, yhi, z, core),
        ]
        + [(dp, (mp + o) % 16) for o in range(1, 16)]
    )
    far = (dp, (mp + 8) % 16)
    mine_rows = pl.ds(pl.multiple_of(yhi * 64, 64), 64)
    far_rows = pl.ds(pl.multiple_of((1 - yhi) * 64, 64), 64)
    loads = [
        pltpu.make_async_copy(head_w, head_w_here.at[0], load_s.at[0]),
        pltpu.make_async_copy(noise.at[:, mine_rows], noise_here.at[0], load_s.at[1]),
        pltpu.make_async_copy(head_b, head_b_here.at[0], load_s.at[2]),
    ]
    for cp in loads:
        cp.start()
    book_x = head_scratch[4]

    def prepare():
        phi_flat[...] = jnp.concatenate([phi[i, j] for i in range(3) for j in range(3)], axis=1)
        wide = jnp.concatenate([book[...].astype(F32), jnp.zeros((96, VB), F32)], axis=0)
        wide = jnp.where(lax.broadcasted_iota(jnp.int32, (128, VB), 0) == SIDE, 1.0, wide)
        book_x[0] = jnp.transpose(wide).astype(BF)

    def quarter(ref, index, first=0, count=HID):
        return ref.at[pl.ds(pl.multiple_of(index * HID + first, 16), count)]

    there = head_w_here.at[1]
    x_l, x_r = (x + 3) % 4, (x + 1) % 4
    ways = ((0, device(ylo, x_r, yhi, z, core), x_l), (1, device(ylo, x_l, yhi, z, core), x_r))
    ahead = [
        remote(quarter(head_w, x), quarter(there, x), far_s.at[0], far_r.at[0], far),
        [remote(quarter(there, x), quarter(there, x), panel_s.at[0, d], panel_r.at[0, d], to) for d, to, _ in ways],
        [
            remote(
                quarter(there, back, d * TH, TH), quarter(there, back, d * TH, TH),
                panel_s.at[1, d], panel_r.at[1, d], to,
            )
            for d, to, back in ways
        ],
        [
            remote(noise.at[:, far_rows], noise_here.at[1], far_s.at[1], far_r.at[1], far),
            remote(book_x.at[0], book_x.at[1], far_s.at[2], far_r.at[2], far),
            remote(head_b, head_b_here.at[1], far_s.at[3], far_r.at[3], far),
        ],
    ]
    ffn_part(arrived, prepare, ahead, tok, ada, gate, up_w, up_b, down_w, down_b, out, *ffn_scratch)
    for cp in loads:
        cp.wait()
    head_part(
        ahead, out, ada_head, head_w_here, head_b_here, noise_here, phi_flat, phi_b, f_hat, f_out, *head_scratch
    )
    for cp in ahead[:1] + ahead[1] + ahead[2] + ahead[3]:
        cp.wait_send()


def deliver_kernel(rows, cells, rows_out, cells_out):
    rows_out[...] = rows[...]
    cells_out[...] = cells[...]


def deliver(rows, cells):
    vmem = pl.BlockSpec(memory_space=pltpu.VMEM)
    return pl.pallas_call(
        deliver_kernel,
        out_shape=tuple(jax.ShapeDtypeStruct(v.shape, v.dtype) for v in (rows, cells)),
        in_specs=[vmem] * 2,
        out_specs=(vmem, vmem),
        name="deliver",
    )(rows, cells)


def body(
    tokens, ada_ffn, ffn_gate, up_weight, up_bias, down_weight, down_bias, ada_head,
    head_weight, head_bias, gumbel_noise, codebook, phi_weight, phi_bias, f_hat,
):
    dma = pltpu.SemaphoreType.DMA
    widths = [UNITS[k][3] for k in CHUNKS]
    vmem, anywhere = pl.BlockSpec(memory_space=pltpu.VMEM), pl.BlockSpec(memory_space=pl.ANY)
    ffn_scratch = [
        pltpu.VMEM((4, ROWS, D), BF),
        pltpu.VMEM((4 * HID, D), BF),
        [pltpu.VMEM((4 * HID, w), BF) for w in widths],
        pltpu.VMEM((4, 1, HID), F32),
        pltpu.VMEM((1, 4 * HID), F32),
        pltpu.VMEM((1, D), F32),
        pltpu.VMEM((512, 4 * HID), BF),
        [pltpu.VMEM((4, ROWS, w), F32) for w in widths],
        [pltpu.VMEM((ROWS, w), BF) for w in widths],
        [pltpu.VMEM((2, 2, 64, w), BF) for w in widths],
        [pltpu.VMEM((2, 3, 64, w), BF) for w in widths],
        dma((4 + NC,)),
        dma((NU,)), dma((NU,)),
        dma((NU, 2)), dma((NU, 2)),
        dma((NU, 2)), dma((NU, 2)),
        dma((NU,)), dma((NU,)),
        dma((1 + NC,)), dma((1 + NC,)),
        dma((4,)), dma((4,)),
        dma((3,)), dma((3,)),
        dma((NC, 2, 2)), dma((NC, 2, 2)),
        dma((NC, 2)), dma((NC, 2)),
    ]
    head_scratch = [
        pltpu.VMEM((ROWS, D), BF),
        pltpu.VMEM((64, D), BF),
        pltpu.VMEM((64, D), BF),
        pltpu.VMEM((4, 2, 64, D), BF),
        pltpu.VMEM((2, VB, 128), BF),
        pltpu.VMEM((16, MSG, 128), F32),
        pltpu.VMEM((MSG, 1280), F32),
        pltpu.VMEM((16, MSG, 128), F32),
        dma((NCH,)), dma((NCH,)),
        dma((NCH,)), dma((NCH,)),
        dma((NCH,)),
        dma((NCH, 2)), dma((NCH, 2)),
        dma((NCH, 2)), dma((NCH, 2)),
        dma((NCH, 4)), dma((NCH, 4)),
        dma((16,)), dma((16,)),
    ]
    rows, cells = pl.pallas_call(
        kernel,
        out_shape=(jax.ShapeDtypeStruct((ROWS, D), BF), jax.ShapeDtypeStruct((1, 32, 64), F32)),
        in_specs=[vmem, vmem, vmem, anywhere, anywhere, anywhere, anywhere, vmem, anywhere, vmem, anywhere] + [vmem] * 4,
        out_specs=(vmem, vmem),
        scratch_shapes=[
            ffn_scratch,
            head_scratch,
            pltpu.VMEM((2, D, VB), BF),
            pltpu.VMEM((2, 1, VB), F32),
            pltpu.VMEM((2, 8, 64, VB), F32),
            dma((3,)),
            dma((4,)), dma((4,)),
            dma((2, 2)), dma((2, 2)),
            pltpu.VMEM((32, 288), F32),
        ],
        name="var_step",
        compiler_params=pltpu.CompilerParams(
            collective_id=1, has_side_effects=True, vmem_limit_bytes=60 * 1024 * 1024
        ),
    )(
        tokens, ada_ffn, ffn_gate, up_weight.T, up_bias, down_weight, down_bias,
        ada_head, head_weight, head_bias.reshape(1, -1), gumbel_noise.reshape(8, 128, VB), codebook.T,
        jnp.transpose(phi_weight, (2, 3, 0, 1)), phi_bias.reshape(1, -1), f_hat,
    )
    return deliver(rows, cells)


def solution(mesh):
    in_specs = (
        P(("dp", "mp"), None),
        P("dp", None, None),
        P("dp", None),
        P(None, "mp"),
        P("mp"),
        P("mp", None),
        P(),
        P("dp", None, None),
        P(None, "mp"),
        P("mp"),
        P("dp", None, "mp"),
        P("mp", None),
        P(),
        P(),
        P("dp", None, "mp"),
    )
    out_specs = (P(("dp", "mp"), None), P("dp", None, "mp"))
    return jax.shard_map(body, mesh=mesh, in_specs=in_specs, out_specs=out_specs, check_vma=False)
```

```python
import functools

import jax
import jax.numpy as jnp
from jax import lax
from jax.experimental import pallas as pl
from jax.experimental.pallas import tpu as pltpu
from jax.sharding import PartitionSpec as P

MESH = pl.DeviceIdType.MESH
BF = jnp.bfloat16
F32 = jnp.float32

D = 2304
ROWS = 128
HID = 576
FOREIGN = 2 * HID
DQ = HID // 4
TH = HID // 2
UNITS = (
    ("ring", "up", 0, 128),
    ("ring", "up", 128, 192),
    ("ring", "up", 320, 256),
    ("twin", "down", 0, 512),
    ("ring", "down", 512, 768),
    ("ring", "down", 1280, 512),
    ("twin", "down", 1792, 512),
)
PUSHED = (0, 1, 2, 3, 4, 5, 6)
NU = len(UNITS)
CHUNKS = tuple(k for k in range(NU) if UNITS[k][1] == "down")
NC = len(CHUNKS)
STEPS = (
    ("y", 0), ("a", 0), ("y", 1), ("b", 0), ("z", 1),
    ("y", 2), ("a", 1), ("z", 2), ("tile", 0), ("y", 3),
    ("tile", 1), ("tile", 2), ("a", 2), ("tile", 3), ("early", 0),
    ("early", 1), ("b", 1), ("early", 2), ("y", 4), ("early", 3),
    ("b", 2), ("a", 3), ("y", 5), ("late", 0), ("tile", 4),
    ("tile", 5), ("tile", 6), ("tile", 7), ("tile", 8), ("a", 4),
    ("first", 0), ("y", 6), ("a", 5), ("second", 0), ("b", 4),
    ("first", 1), ("b", 5), ("finish", 0), ("first", 2), ("a", 6),
    ("second", 1), ("first", 3), ("second", 2), ("panel", 0), ("finish", 1),
    ("second", 3), ("finish", 2), ("finish", 3), ("panel", 1),
)
NARROW = 256
FIRST = 1024
SIDE = 32
VB = 256
MSG = 40
GUIDE = 1.5


def position():
    dp, mp = lax.axis_index("dp"), lax.axis_index("mp")
    return dp // 4, dp % 4, mp // 8, (mp // 2) % 4, mp % 2


def device(ylo, x, yhi, z, core):
    return (ylo * 4 + x, yhi * 8 + z * 2 + core)


def remote(src, dst, send, recv, target):
    return pltpu.make_async_remote_copy(
        src_ref=src, dst_ref=dst, send_sem=send, recv_sem=recv, device_id=target, device_id_type=MESH
    )


def norm_rows(values):
    centred = values - jnp.mean(values, axis=-1, keepdims=True)
    spread = jnp.mean(centred * centred, axis=-1, keepdims=True)
    return centred * lax.rsqrt(spread + 1e-06)


def gelu(v):
    return 0.5 * v * (1.0 + jnp.tanh(0.7978845608028654 * (v + 0.044715 * v * v * v)))


def greet(targets):
    barrier = pltpu.get_barrier_semaphore()
    for target in targets:
        pl.semaphore_signal(barrier, inc=1, device_id=target, device_id_type=MESH)
    return lambda: pl.semaphore_wait(barrier, len(targets))


def ffn_part(
    arrived, ahead, tok, ada, gate, up_w, up_b, down_w, down_b, out,
    xn, up, dns, ub, bias_row, down_row, hid, parts, opps, nbrs, gots,
    loc_s, y_s, y_r, a_s, a_r, b_s, b_r, c_s, c_r, o_s, o_r, z_s, z_r, bias_s, bias_r,
    p_s, p_r, q_s, q_r,
):
    ylo, x, yhi, z, core = position()
    sib = device(ylo, x, yhi, z, 1 - core)
    partner = device(1 - ylo, x, 1 - yhi, z, core)
    partner_sib = device(1 - ylo, x, 1 - yhi, z, 1 - core)
    twin = device(1 - ylo, x, yhi, z, core)
    x_l, x_r = (x + 3) % 4, (x + 1) % 4
    xr, xl = device(ylo, x_r, yhi, z, core), device(ylo, x_l, yhi, z, core)
    zr_i, zl_i, zo_i = (z + 1) % 4, (z + 3) % 4, (z + 2) % 4
    zr, zl = device(ylo, x, yhi, zr_i, core), device(ylo, x, yhi, zl_i, core)

    own_rows, sib_rows = pl.ds(0, HID), pl.ds(HID, HID)

    def cols(j):
        return pl.ds(UNITS[CHUNKS[j]][2], UNITS[CHUNKS[j]][3])

    loc_up = pltpu.make_async_copy(up_w, up.at[own_rows], loc_s.at[0])
    loc_up.start()
    loc_dn = [
        pltpu.make_async_copy(down_w.at[:, cols(j)], dns[j].at[own_rows], loc_s.at[3 + j]) for j in range(NC)
    ]
    loc_bias = pltpu.make_async_copy(up_b, ub.at[0, 0], loc_s.at[2])
    loc_bias.start()
    loc_down = pltpu.make_async_copy(down_b, down_row.at[0], loc_s.at[3 + NC])
    loc_down.start()

    @pl.loop(0, ROWS // 16)
    def _(i):
        rows = pl.ds(pl.multiple_of(i * 16, 16), 16)
        pair = ada[yhi]
        v = norm_rows(tok[rows, :].astype(F32)) * (1.0 + pair[1:2, :]) + pair[0:1, :]
        xn[z, rows, :] = v.astype(BF)

    arrived()

    def part_of(k, count, index, foreign=True):
        way, panel, first, size = UNITS[k]
        base = FOREIGN if foreign else 0
        if panel == "up":
            rows = pl.ds(pl.multiple_of(base + first + index * (size // count), 16), size // count)
            return (up if foreign else up_w).at[rows]
        rows = pl.ds(pl.multiple_of(base + index * (HID // count), 16), HID // count)
        return dns[CHUNKS.index(k)].at[rows] if foreign else down_w.at[rows, pl.ds(first, size)]

    def half_of(k, index, half):
        way, panel, first, size = UNITS[k]
        if panel == "up":
            rows = pl.ds(pl.multiple_of(FOREIGN + first + index * (size // 4), 16), size // 4)
            return up.at[rows, pl.ds(half * (D // 2), D // 2)]
        rows = pl.ds(pl.multiple_of(FOREIGN + index * DQ, 16), DQ)
        return dns[CHUNKS.index(k)].at[rows, pl.ds(half * (size // 2), size // 2)]

    def whole(k, base):
        way, panel, first, size = UNITS[k]
        if panel == "up":
            return up.at[pl.ds(base + first, size)]
        return dns[CHUNKS.index(k)].at[pl.ds(base, HID)]

    y, a, b, c = [], [], [], []
    for k in range(NU):
        c.append(remote(whole(k, FOREIGN), whole(k, FOREIGN + HID), c_s.at[k], c_r.at[k], sib))
        if UNITS[k][0] == "ring":
            own = part_of(k, 4, x)
            y.append(remote(part_of(k, 4, x, False), own, y_s.at[k], y_r.at[k], partner))
            a.append([
                remote(own, own, a_s.at[k, 0], a_r.at[k, 0], xr), remote(own, own, a_s.at[k, 1], a_r.at[k, 1], xl)
            ])
            from_l, from_r = half_of(k, x_l, 0), half_of(k, x_r, 1)
            b.append([
                remote(from_l, from_l, b_s.at[k, 0], b_r.at[k, 0], xr),
                remote(from_r, from_r, b_s.at[k, 1], b_r.at[k, 1], xl),
            ])
        else:
            y.append(remote(
                part_of(k, 2, 1 - ylo, False), part_of(k, 2, 1 - ylo), y_s.at[k], y_r.at[k], partner
            ))
            own = part_of(k, 2, ylo)
            a.append([remote(own, own, a_s.at[k, 0], a_r.at[k, 0], twin)])
            b.append([])

    z1 = [
        remote(xn.at[z], xn.at[z], z_s.at[0], z_r.at[0], zr),
        remote(xn.at[z], xn.at[z], z_s.at[1], z_r.at[1], zl),
    ]
    z2 = [
        remote(xn.at[zl_i, pl.ds(0, 64)], xn.at[zl_i, pl.ds(0, 64)], z_s.at[2], z_r.at[2], zr),
        remote(xn.at[zr_i, pl.ds(64, 64)], xn.at[zr_i, pl.ds(64, 64)], z_s.at[3], z_r.at[3], zl),
    ]
    own_up = remote(up_w, up.at[sib_rows], o_s.at[0], o_r.at[0], sib)
    own_dn = [
        remote(down_w.at[:, cols(j)], dns[j].at[sib_rows], o_s.at[1 + j], o_r.at[1 + j], sib) for j in range(NC)
    ]
    biases = [
        remote(up_b, ub.at[1, 0], bias_s.at[0], bias_r.at[0], sib),
        remote(up_b, ub.at[2, 0], bias_s.at[1], bias_r.at[1], partner),
        remote(up_b, ub.at[3, 0], bias_s.at[2], bias_r.at[2], partner_sib),
    ]

    def start(*copies):
        for cp in copies:
            cp.start()

    def recv(*copies):
        for cp in copies:
            cp.wait_recv()

    def hidden(n):
        units = pl.ds(n * NARROW, NARROW)

        @pl.loop(0, 2)
        def _(m):
            rows = pl.ds(pl.multiple_of(m * 256, 256), 256)
            acc = lax.dot_general(
                xn[pl.ds(2 * m, 2)].reshape(256, D), up[units, :], (((1,), (1,)), ((), ())),
                preferred_element_type=F32,
            )
            hid[rows, units] = gelu(acc + bias_row[:, units]).astype(BF)

    def partial(j, late):
        units = pl.ds(FIRST, D - FIRST) if late else pl.ds(0, FIRST)
        width = UNITS[CHUNKS[j]][3]

        @pl.loop(0, 2)
        def _(m):
            rows = pl.ds(pl.multiple_of(m * 256, 256), 256)
            acc = jnp.dot(hid[rows, units], dns[j][units], preferred_element_type=F32).reshape(2, ROWS, width)
            if late:
                acc = acc + parts[j][pl.ds(2 * m, 2)]
            parts[j][pl.ds(2 * m, 2)] = acc

    low, high = pl.ds(0, 64), pl.ds(64, 64)

    p1 = [
        [
            remote(opps[j].at[low], gots[j].at[0, 0], p_s.at[j, 0, 0], p_r.at[j, 0, 0], zr),
            remote(opps[j].at[high], gots[j].at[1, 0], p_s.at[j, 1, 0], p_r.at[j, 1, 0], zl),
        ]
        for j in range(NC)
    ]
    ind = [
        [
            remote(nbrs[j].at[0, 0], gots[j].at[0, 1], p_s.at[j, 0, 1], p_r.at[j, 0, 1], zr),
            remote(nbrs[j].at[1, 0], gots[j].at[1, 1], p_s.at[j, 1, 1], p_r.at[j, 1, 1], zl),
        ]
        for j in range(NC)
    ]
    p2 = [
        [
            remote(nbrs[j].at[0, 1], gots[j].at[0, 2], q_s.at[j, 0], q_r.at[j, 0], zr),
            remote(nbrs[j].at[1, 1], gots[j].at[1, 2], q_s.at[j, 1], q_r.at[j, 1], zl),
        ]
        for j in range(NC)
    ]

    def reduce_first(j):
        recv(c[CHUNKS[j]])
        partial(j, True)
        opps[j][...] = parts[j][zo_i].astype(BF)
        start(*p1[j])
        nbrs[j][0, 0] = parts[j][zr_i, high].astype(BF)
        nbrs[j][1, 0] = parts[j][zl_i, low].astype(BF)
        start(*ind[j])

    def reduce_second(j):
        recv(*p1[j])
        nbrs[j][0, 1] = (parts[j][zr_i, low] + gots[j][0, 0].astype(F32)).astype(BF)
        nbrs[j][1, 1] = (parts[j][zl_i, high] + gots[j][1, 0].astype(F32)).astype(BF)
        start(*p2[j])

    def finish(j):
        recv(*ind[j], *p2[j])
        for rows, left, right in ((low, 2, 1), (high, 1, 2)):
            total = parts[j][z, rows] + gots[j][0, left].astype(F32) + gots[j][1, right].astype(F32)
            total = total + down_row[:, cols(j)]
            out[rows, cols(j)] = (
                tok[rows, cols(j)].astype(F32) + gate[pl.ds(yhi, 1), cols(j)] * total
            ).astype(BF)

    start(y[PUSHED[0]], *z1, *biases, own_up)
    for cp in loc_dn:
        cp.start()
    y[PUSHED[0]].wait_send()
    start(y[PUSHED[1]], y[PUSHED[2]], y[PUSHED[3]])
    for op, k in STEPS:
        if op == "y":
            recv(y[k])
            start(*a[k])
            at = PUSHED.index(k)
            if 0 < at < NU - 3:
                start(y[PUSHED[at + 3]])
            if k == PUSHED[-1]:
                start(ahead[0], *ahead[3])
        elif op == "panel" and k == 0:
            recv(ahead[0])
            start(*ahead[1])
        elif op == "panel":
            recv(*ahead[1])
            start(*ahead[2])
        elif op == "a":
            recv(*a[k])
            start(*(b[k] if UNITS[k][0] == "ring" else [c[k]]))
        elif op == "b":
            recv(*b[k])
            start(c[k])
        elif op == "z" and k == 1:
            recv(*z1)
            start(*z2, *own_dn)
        elif op == "z":
            loc_bias.wait()
            loc_down.wait()
            recv(*biases)
            bias_row[...] = jnp.concatenate([ub[i] for i in range(4)], axis=1)
            loc_up.wait()
            recv(own_up, *z2)
        elif op == "early":
            loc_dn[k].wait()
            recv(own_dn[k])
            partial(k, False)
        elif op == "tile":
            hidden(k)
        elif op == "late":
            recv(*[c[i] for i in range(NU) if UNITS[i][1] == "up"])
        elif op == "first":
            reduce_first(k)
        elif op == "second":
            reduce_second(k)
        else:
            finish(k)

    y[PUSHED[0]] = None
    for cp in [v for v in y if v is not None] + c + z1 + z2 + [own_up] + own_dn + biases:
        cp.wait_send()
    for group in a + b + p1 + ind + p2:
        for cp in group:
            cp.wait_send()


def head_part(
    ahead, blk, ada, head_w, head_b, noise, phi, phi_b, f_hat, out,
    h, mine, theirs, g, book_x, stage, turned, got,
    t_s, t_r, y_s, y_r, l_s, z_s, z_r, w_s, w_r, c_s, c_r, m_s, m_r,
):
    ylo, x, yhi, z, core = position()
    dp, mp = lax.axis_index("dp"), lax.axis_index("mp")
    sib = device(ylo, x, yhi, z, 1 - core)
    twin = device(1 - ylo, x, yhi, z, core)
    partner = device(1 - ylo, x, 1 - yhi, z, core)
    zr_i, zl_i, zo_i = (z + 1) % 4, (z + 3) % 4, (z + 2) % 4
    zr, zl = device(ylo, x, yhi, zr_i, core), device(ylo, x, yhi, zl_i, core)
    lo = pl.multiple_of(ylo * 64, 64)
    other = pl.multiple_of((1 - ylo) * 64, 64)
    t = [
        remote(
            h.at[pl.ds(pl.multiple_of(other + k * CR, CR), CR)], theirs.at[pl.ds(k * CR, CR)],
            t_s.at[k], t_r.at[k], twin,
        )
        for k in range(NCH)
    ]
    pair = ada[yhi]

    for first in (other, lo):
        rows = pl.ds(first, 64)
        v = norm_rows(blk[rows, :].astype(F32)) * (1.0 + pair[1:2, :]) + pair[0:1, :]
        h[rows, :] = v.astype(BF)
        if first is other:
            for cp in t:
                cp.start()
    same = ylo == yhi
    own_weight = jnp.where(ylo == 0, 1.0 + GUIDE, -GUIDE)
    twin_weight = jnp.where(ylo == 0, -GUIDE, 1.0 + GUIDE)

    def slot(k, zi):
        return g.at[zi, core, pl.ds(k * CR, CR)]

    def slot_half(k, zi, half):
        return g.at[zi, core, pl.ds(k * CR, CR), pl.ds(half * (D // 2), D // 2)]

    def mixed(k):
        return mine.at[pl.ds(k * CR, CR)]

    swap = [remote(mixed(k), slot(k, z), y_s.at[k], y_r.at[k], partner) for k in range(NCH)]
    stay = [pltpu.make_async_copy(mixed(k), slot(k, z), l_s.at[k]) for k in range(NCH)]
    z1 = [
        [remote(slot(k, z), slot(k, z), z_s.at[k, d], z_r.at[k, d], to) for d, to in ((0, zr), (1, zl))]
        for k in range(NCH)
    ]
    z2 = [
        [
            remote(slot_half(k, zl_i, 0), slot_half(k, zl_i, 0), w_s.at[k, 0], w_r.at[k, 0], zr),
            remote(slot_half(k, zr_i, 1), slot_half(k, zr_i, 1), w_s.at[k, 1], w_r.at[k, 1], zl),
        ]
        for k in range(NCH)
    ]
    cross = [
        [remote(slot(k, zi), slot(k, zi), c_s.at[k, i], c_r.at[k, i], sib) for i, zi in enumerate((z, zr_i, zl_i, zo_i))]
        for k in range(NCH)
    ]

    def mix(k):
        t[k].wait_recv()
        rows = pl.ds(k * CR, CR)
        own = h[pl.ds(pl.multiple_of(lo + k * CR, CR), CR), :].astype(F32)
        mine[rows, :] = (own_weight * own + twin_weight * theirs[rows, :].astype(F32)).astype(BF)

        @pl.when(same)
        def _():
            stay[k].start()

        @pl.when(jnp.logical_not(same))
        def _():
            swap[k].start()

    def gathered(k):
        @pl.when(same)
        def _():
            stay[k].wait()

        @pl.when(jnp.logical_not(same))
        def _():
            swap[k].wait_recv()

        for cp in z1[k] + cross[k][:1]:
            cp.start()

    def second(k):
        for cp in z1[k]:
            cp.wait_recv()
        for cp in z2[k] + cross[k][1:3]:
            cp.start()

    def third(k):
        for cp in z2[k]:
            cp.wait_recv()
        cross[k][3].start()

    for k in range(NCH + 3):
        if k < NCH:
            mix(k)
        if 0 <= k - 1 < NCH:
            gathered(k - 1)
        if 0 <= k - 2 < NCH:
            second(k - 2)
        if 0 <= k - 3 < NCH - 1:
            third(k - 3)
    for cp in ahead[2] + ahead[3]:
        cp.wait_recv()
    for k in range(NCH):
        for cp in cross[k][:3]:
            cp.wait_recv()

    column = lax.broadcasted_iota(jnp.int32, (4, 64, 128), 2)
    nothing = jnp.where(column == SIDE + 1, -1e30, 0.0)

    def sample(i):
        lhs = g[pl.ds(2 * i, 2)].reshape(256, D)
        scores = []
        for p in range(2):
            logits = jnp.dot(lhs, head_w[p], preferred_element_type=F32) + head_b[p]
            scores.append(logits + noise[p, pl.ds(4 * i, 4)].reshape(256, VB))
        peak = jnp.maximum(
            jnp.max(scores[0], axis=1, keepdims=True), jnp.max(scores[1], axis=1, keepdims=True)
        )
        code = jnp.zeros((256, 128), F32)
        for p in range(2):
            weights = jnp.exp(scores[p] - peak).astype(BF)
            code = code + jnp.dot(weights, book_x[p], preferred_element_type=F32)
        code = jnp.where(lax.broadcasted_iota(jnp.int32, code.shape, 1) == SIDE + 1, peak, code).reshape(4, 64, 128)
        spread = jnp.concatenate(
            [jnp.where(yhi == 0, code, nothing), jnp.where(yhi == 1, code, nothing)], axis=1
        ).reshape(512, 128)
        flipped = jnp.transpose(spread)
        turned[:, pl.ds(pl.multiple_of(128 + i * 512, 128), 512)] = flipped[0:MSG, :]

    sample(z // 2)
    third(NCH - 1)
    for k in range(NCH):
        cross[k][3].wait_recv()
    sample(1 - z // 2)

    zeros = jnp.zeros((MSG, 128), F32)
    turned[:, 0:128] = zeros
    turned[:, 1152:1280] = zeros
    cells = turned[...]
    for parity, shift in ((0, 96), (1, 32)):
        rolled = pltpu.roll(cells, 1280 - shift, 1)
        for i in range(8):
            to = 2 * i + parity
            start = (128 + 64 * to - 32 - shift)
            stage[to] = rolled[:, start:start + 128]

    posts = []
    for o in range(1, 16):
        to = (mp + o) % 16
        cp = remote(stage.at[to], got.at[o], m_s.at[o], m_r.at[o], (dp, to))
        cp.start()
        posts.append(cp)
    got[0] = stage[mp]
    for cp in posts:
        cp.wait_recv()
    peaks = got[:, SIDE + 1:SIDE + 2, :]
    factor = jnp.exp(peaks - jnp.max(peaks, axis=0, keepdims=True))
    sums = jnp.sum(got[:, 0:MSG, :] * factor, axis=0)
    lane = lax.broadcasted_iota(jnp.int32, (1, 128), 1)
    outside = jnp.logical_or(jnp.logical_and(mp == 0, lane < 32), jnp.logical_and(mp == 15, lane >= 96))
    soft = jnp.where(outside, 0.0, sums[0:32] / jnp.where(outside, 1.0, sums[32:33]))
    taps = []
    for i in range(3):
        for j in range(3):
            offset = 32 * (i - 1) + (j - 1)
            tap = soft if offset == 0 else pltpu.roll(soft, (-offset) % 128, 1)
            if j == 0:
                tap = jnp.where(lane % 32 == 0, 0.0, tap)
            if j == 2:
                tap = jnp.where(lane % 32 == 31, 0.0, tap)
            taps.append(tap)
    square = lax.broadcasted_iota(jnp.int32, (32, 32), 0) == lax.broadcasted_iota(jnp.int32, (32, 32), 1)
    conv = jnp.sum(jnp.where(square, phi_b[...], 0.0), axis=1, keepdims=True) + jnp.dot(
        phi[...], jnp.concatenate(taps, axis=0), preferred_element_type=F32, precision=lax.Precision.HIGHEST
    )
    total = 0.5 * soft + 0.5 * conv
    out[0] = f_hat[0] + pltpu.roll(total, 96, 1)[:, 0:64]

    for cp in t + posts:
        cp.wait_send()
    for k in range(NCH):

        @pl.when(jnp.logical_not(same))
        def _():
            swap[k].wait_send()

        for cp in z1[k] + z2[k] + cross[k]:
            cp.wait_send()


NCH = 4
CR = 64 // NCH


def kernel(
    tok, ada, gate, up_w, up_b, down_w, down_b, ada_head, head_w, head_b, noise, book, phi, phi_b, f_hat, out, f_out,
    ffn_scratch, head_scratch, head_w_here, head_b_here, noise_here, load_s, far_s, far_r, panel_s, panel_r, phi_flat,
):
    ylo, x, yhi, z, core = position()
    dp, mp = lax.axis_index("dp"), lax.axis_index("mp")
    arrived = greet(
        [
            device(1 - ylo, x, yhi, z, core), device(1 - ylo, x, 1 - yhi, z, core),
            device(1 - ylo, x, 1 - yhi, z, 1 - core),
            device(ylo, (x + 1) % 4, yhi, z, core), device(ylo, (x + 3) % 4, yhi, z, core),
        ]
        + [(dp, (mp + o) % 16) for o in range(1, 16)]
    )
    far = (dp, (mp + 8) % 16)
    mine_rows = pl.ds(pl.multiple_of(yhi * 64, 64), 64)
    far_rows = pl.ds(pl.multiple_of((1 - yhi) * 64, 64), 64)
    loads = [
        pltpu.make_async_copy(head_w, head_w_here.at[0], load_s.at[0]),
        pltpu.make_async_copy(noise.at[:, mine_rows], noise_here.at[0], load_s.at[1]),
        pltpu.make_async_copy(head_b, head_b_here.at[0], load_s.at[2]),
    ]
    for cp in loads:
        cp.start()
    phi_flat[...] = jnp.concatenate([phi[i, j] for i in range(3) for j in range(3)], axis=1)
    book_x = head_scratch[4]
    wide = jnp.concatenate([book[...].astype(F32), jnp.zeros((96, VB), F32)], axis=0)
    wide = jnp.where(lax.broadcasted_iota(jnp.int32, (128, VB), 0) == SIDE, 1.0, wide)
    book_x[0] = jnp.transpose(wide).astype(BF)
    def quarter(ref, index, first=0, count=HID):
        return ref.at[pl.ds(pl.multiple_of(index * HID + first, 16), count)]

    there = head_w_here.at[1]
    x_l, x_r = (x + 3) % 4, (x + 1) % 4
    ways = ((0, device(ylo, x_r, yhi, z, core), x_l), (1, device(ylo, x_l, yhi, z, core), x_r))
    ahead = [
        remote(quarter(head_w, x), quarter(there, x), far_s.at[0], far_r.at[0], far),
        [remote(quarter(there, x), quarter(there, x), panel_s.at[0, d], panel_r.at[0, d], to) for d, to, _ in ways],
        [
            remote(
                quarter(there, back, d * TH, TH), quarter(there, back, d * TH, TH),
                panel_s.at[1, d], panel_r.at[1, d], to,
            )
            for d, to, back in ways
        ],
        [
            remote(noise.at[:, far_rows], noise_here.at[1], far_s.at[1], far_r.at[1], far),
            remote(book_x.at[0], book_x.at[1], far_s.at[2], far_r.at[2], far),
            remote(head_b, head_b_here.at[1], far_s.at[3], far_r.at[3], far),
        ],
    ]
    ffn_part(arrived, ahead, tok, ada, gate, up_w, up_b, down_w, down_b, out, *ffn_scratch)
    for cp in loads:
        cp.wait()
    head_part(
        ahead, out, ada_head, head_w_here, head_b_here, noise_here, phi_flat, phi_b, f_hat, f_out, *head_scratch
    )
    for cp in ahead[:1] + ahead[1] + ahead[2] + ahead[3]:
        cp.wait_send()


def deliver_kernel(rows, cells, rows_out, cells_out):
    rows_out[...] = rows[...]
    cells_out[...] = cells[...]


def deliver(rows, cells):
    vmem = pl.BlockSpec(memory_space=pltpu.VMEM)
    return pl.pallas_call(
        deliver_kernel,
        out_shape=tuple(jax.ShapeDtypeStruct(v.shape, v.dtype) for v in (rows, cells)),
        in_specs=[vmem] * 2,
        out_specs=(vmem, vmem),
        name="deliver",
    )(rows, cells)


def body(
    tokens, ada_ffn, ffn_gate, up_weight, up_bias, down_weight, down_bias, ada_head,
    head_weight, head_bias, gumbel_noise, codebook, phi_weight, phi_bias, f_hat,
):
    dma = pltpu.SemaphoreType.DMA
    widths = [UNITS[k][3] for k in CHUNKS]
    vmem, anywhere = pl.BlockSpec(memory_space=pltpu.VMEM), pl.BlockSpec(memory_space=pl.ANY)
    ffn_scratch = [
        pltpu.VMEM((4, ROWS, D), BF),
        pltpu.VMEM((4 * HID, D), BF),
        [pltpu.VMEM((4 * HID, w), BF) for w in widths],
        pltpu.VMEM((4, 1, HID), F32),
        pltpu.VMEM((1, 4 * HID), F32),
        pltpu.VMEM((1, D), F32),
        pltpu.VMEM((512, 4 * HID), BF),
        [pltpu.VMEM((4, ROWS, w), F32) for w in widths],
        [pltpu.VMEM((ROWS, w), BF) for w in widths],
        [pltpu.VMEM((2, 2, 64, w), BF) for w in widths],
        [pltpu.VMEM((2, 3, 64, w), BF) for w in widths],
        dma((4 + NC,)),
        dma((NU,)), dma((NU,)),
        dma((NU, 2)), dma((NU, 2)),
        dma((NU, 2)), dma((NU, 2)),
        dma((NU,)), dma((NU,)),
        dma((1 + NC,)), dma((1 + NC,)),
        dma((4,)), dma((4,)),
        dma((3,)), dma((3,)),
        dma((NC, 2, 2)), dma((NC, 2, 2)),
        dma((NC, 2)), dma((NC, 2)),
    ]
    head_scratch = [
        pltpu.VMEM((ROWS, D), BF),
        pltpu.VMEM((64, D), BF),
        pltpu.VMEM((64, D), BF),
        pltpu.VMEM((4, 2, 64, D), BF),
        pltpu.VMEM((2, VB, 128), BF),
        pltpu.VMEM((16, MSG, 128), F32),
        pltpu.VMEM((MSG, 1280), F32),
        pltpu.VMEM((16, MSG, 128), F32),
        dma((NCH,)), dma((NCH,)),
        dma((NCH,)), dma((NCH,)),
        dma((NCH,)),
        dma((NCH, 2)), dma((NCH, 2)),
        dma((NCH, 2)), dma((NCH, 2)),
        dma((NCH, 4)), dma((NCH, 4)),
        dma((16,)), dma((16,)),
    ]
    rows, cells = pl.pallas_call(
        kernel,
        out_shape=(jax.ShapeDtypeStruct((ROWS, D), BF), jax.ShapeDtypeStruct((1, 32, 64), F32)),
        in_specs=[vmem, vmem, vmem, anywhere, anywhere, anywhere, anywhere, vmem, anywhere, vmem, anywhere] + [vmem] * 4,
        out_specs=(vmem, vmem),
        scratch_shapes=[
            ffn_scratch,
            head_scratch,
            pltpu.VMEM((2, D, VB), BF),
            pltpu.VMEM((2, 1, VB), F32),
            pltpu.VMEM((2, 8, 64, VB), F32),
            dma((3,)),
            dma((4,)), dma((4,)),
            dma((2, 2)), dma((2, 2)),
            pltpu.VMEM((32, 288), F32),
        ],
        name="var_step",
        compiler_params=pltpu.CompilerParams(
            collective_id=1, has_side_effects=True, vmem_limit_bytes=60 * 1024 * 1024
        ),
    )(
        tokens, ada_ffn, ffn_gate, up_weight.T, up_bias, down_weight, down_bias,
        ada_head, head_weight, head_bias.reshape(1, -1), gumbel_noise.reshape(8, 128, VB), codebook.T,
        jnp.transpose(phi_weight, (2, 3, 0, 1)), phi_bias.reshape(1, -1), f_hat,
    )
    return deliver(rows, cells)


def solution(mesh):
    in_specs = (
        P(("dp", "mp"), None),
        P("dp", None, None),
        P("dp", None),
        P(None, "mp"),
        P("mp"),
        P("mp", None),
        P(),
        P("dp", None, None),
        P(None, "mp"),
        P("mp"),
        P("dp", None, "mp"),
        P("mp", None),
        P(),
        P(),
        P("dp", None, "mp"),
    )
    out_specs = (P(("dp", "mp"), None), P("dp", None, "mp"))
    return jax.shard_map(body, mesh=mesh, in_specs=in_specs, out_specs=out_specs, check_vma=False)
```
